32 devices in a mesh: groups: 2 (over x), rows: 16 (over z, y, core).
Axes of the slice: x: 2, y: 2, z: 4, core: 2. Of those that a mesh axis runs over, the one named last changes fastest.
Arguments:
- samples: bfloat16 [32768, 256], P(('groups', 'rows')), parts along dimension 0
- omega_diag: float32 [256, 128, 128], P(('groups', 'rows')), parts along dimension 0, as said below
- omega_off: float32 [960, 128, 128], P(('groups', 'rows')), parts along dimension 0, as said below
- pattern: int32 [960, 2], P(('groups', 'rows')), parts along dimension 0, may hold values from 0 to 127, as said below
- block_count: int32 [256], P(('groups', 'rows')), parts along dimension 0, may hold values from 0 to 15, as said below
- diag_term: float32 [32768], P(('groups', 'rows')), parts along dimension 0, may hold values from -1 to -0.5
Outputs:
- omega_diag_next: float32 [256, 128, 128], P(('groups', 'rows')), parts along dimension 0
- omega_off_next: float32 [960, 128, 128], P(('groups', 'rows')), parts along dimension 0
- objective: float32 [2], P('groups'), parts along dimension 0
The draws below stay inside these ranges and needn't reach their ends.
There are 2 independent parts, one for each index of `groups`. The reference program is written for one: setup_inputs(seed, part) draws one part's arguments, and reference() takes and returns one part's arrays. A program takes and returns all parts, laid end to end along the dimension named above; each array names one. Nothing has to cross between parts.
Inputs may be any that keep to these rules, and one draw needn't show every extreme that they name: `pattern`: row e names a stored off-diagonal block by its block row i, which lies on the device holding e, and its block column j; for live entries j lies on another device. A device's live entries come first, ordered by block row; the live entries of all devices are symmetric: (j, i) is live wherever (i, j) is, and no pair is named twice. Between the block rows of two devices there are either none or exactly 2 live blocks. Dead entries name the device's first block row twice. The live entries of a device are its first entries, as many as the sum of block_count over its 8 block rows; some device has all 30 entries live. `omega_diag`: each diagonal block is symmetric. Omega is symmetric: for live entries e = (i, j) and f = (j, i), omega_off[f] is the transpose of omega_off[e].
All inputs are finite; a program needn't handle non-finite values.
Results may differ from the reference program's by a relative error of at most 0.0003.
Values may be sent and summed in bfloat16 or wider, within the bound.
No kernel may reach another device: no remote copies, remote signals or barrier semaphores. Data moves between devices by JAX's collectives and lax.ppermute only.
A program may use at most 128 MiB of HBM per device.

```python
import jax
import jax.numpy as jnp
from jax import lax

BLOCK = 128
BR_DEV = 8
SAMPLES = 256
NEAR = 3
LINKS = 15
ENTRIES = 30
BLOCK_ROWS = 128
VARIABLES = 16384
N_ROWS = 16


def pattern_tables(key):
    streams = jax.random.split(jax.random.fold_in(key, 11), 5)
    half_axis = N_ROWS // 2
    pool = jax.random.permutation(streams[0], N_ROWS - 2 - NEAR)[:LINKS - NEAR - 1].astype(jnp.int32) + NEAR + 1
    distant = jnp.where(pool >= half_axis, pool + 1, pool)
    offsets = jnp.concatenate([jnp.arange(1, NEAR + 1, dtype=jnp.int32), jnp.full((1,), half_axis, jnp.int32), distant])
    row_flip = jax.random.randint(streams[1], (LINKS,), 1, BR_DEV, dtype=jnp.int32)
    anchor = jax.random.randint(streams[2], (), 0, BR_DEV, dtype=jnp.int32)
    busiest = jax.random.randint(streams[3], (), 0, N_ROWS, dtype=jnp.int32)
    chance = jax.random.randint(streams[4], (N_ROWS, LINKS), 0, 4, dtype=jnp.int32)
    devices = jnp.broadcast_to(jnp.arange(N_ROWS, dtype=jnp.int32)[:, None], (N_ROWS, LINKS))
    lane_ids = jnp.broadcast_to(jnp.arange(LINKS, dtype=jnp.int32)[None, :], (N_ROWS, LINKS))
    partner = jnp.bitwise_xor(devices, offsets[None, :])
    smaller = jnp.minimum(devices, partner)
    active = (lane_ids <= NEAR) | (devices == busiest) | (partner == busiest) | (chance[smaller, lane_ids] < 3)
    flipped = jnp.broadcast_to(jnp.bitwise_xor(anchor, row_flip)[None, :], (N_ROWS, LINKS))
    rows_first = devices * BR_DEV + anchor
    cols_first = partner * BR_DEV + flipped
    rows_second = devices * BR_DEV + flipped
    cols_second = partner * BR_DEV + anchor
    own_first = devices * ENTRIES + 2 * lane_ids
    mate_first = partner * ENTRIES + 2 * lane_ids + 1
    own_second = devices * ENTRIES + 2 * lane_ids + 1
    mate_second = partner * ENTRIES + 2 * lane_ids
    lower = devices < partner
    source_first = jnp.where(lower, own_first, mate_first)
    source_second = jnp.where(lower, own_second, mate_second)
    row_ids = jnp.stack([rows_first, rows_second], axis=2).reshape(N_ROWS, ENTRIES)
    col_ids = jnp.stack([cols_first, cols_second], axis=2).reshape(N_ROWS, ENTRIES)
    valid = jnp.stack([active, active], axis=2).reshape(N_ROWS, ENTRIES)
    sources = jnp.stack([source_first, source_second], axis=2).reshape(N_ROWS, ENTRIES)
    turned = jnp.stack([~lower, ~lower], axis=2).reshape(N_ROWS, ENTRIES)
    base_rows = devices[:, :1] * BR_DEV
    slot_ids = jnp.arange(ENTRIES, dtype=jnp.int32)[None, :]
    scores = jnp.where(valid, (row_ids - base_rows) * ENTRIES + slot_ids, BR_DEV * ENTRIES + slot_ids)
    ordering = jnp.argsort(scores, axis=1)
    row_ids = jnp.take_along_axis(row_ids, ordering, axis=1)
    col_ids = jnp.take_along_axis(col_ids, ordering, axis=1)
    valid = jnp.take_along_axis(valid, ordering, axis=1)
    sources = jnp.take_along_axis(sources, ordering, axis=1)
    turned = jnp.take_along_axis(turned, ordering, axis=1)
    row_ids = jnp.where(valid, row_ids, base_rows)
    col_ids = jnp.where(valid, col_ids, base_rows)
    pattern = jnp.stack([row_ids, col_ids], axis=2).reshape(N_ROWS * ENTRIES, 2)
    row_counts = jnp.zeros((BR_DEV * N_ROWS,), jnp.int32).at[row_ids.reshape(-1)].add(valid.reshape(-1).astype(jnp.int32))
    return (pattern, row_counts, sources.reshape(-1), turned.reshape(-1))


def draw_pattern(key, part):
    return pattern_tables(key)[0]


def draw_block_count(key, part):
    return pattern_tables(key)[1]


def draw_omega_off(key, part):
    tables = pattern_tables(key)
    sources = tables[2]
    turned = tables[3]
    extent = (N_ROWS * ENTRIES, BLOCK, BLOCK)
    raw = jnp.clip(jax.random.normal(jax.random.fold_in(key, 23), extent, jnp.float32) * 0.05, -0.3, 0.3)
    chosen = raw[sources]
    return jnp.where(turned[:, None, None], jnp.swapaxes(chosen, 1, 2), chosen)


def draw_samples(key, part):
    rows_pos = jnp.arange(VARIABLES, dtype=jnp.float32)[:, None] / VARIABLES
    spread = jnp.sqrt(1.0 + 2.0 * rows_pos)
    values = jax.random.normal(key, (VARIABLES, SAMPLES), jnp.float32)
    return (values * spread).astype(jnp.bfloat16)


def draw_omega_diag(key, part):
    first, second = jax.random.split(key)
    extent = (BLOCK_ROWS, BLOCK, BLOCK)
    identity = jnp.eye(BLOCK, dtype=jnp.float32)[None]
    spread = jax.random.uniform(first, extent, jnp.float32, 1.0, 2.0)
    noise = jax.random.normal(second, extent, jnp.float32)
    coupling = jnp.clip((noise + jnp.swapaxes(noise, 1, 2)) * 0.0354, -0.3, 0.3)
    return identity * spread + (1.0 - identity) * coupling


def block_scale(key, dims, shards, smallest, largest):
    def one(axis_at, parts):
        heights = jax.random.uniform(jax.random.fold_in(jax.random.fold_in(key, 6), axis_at), (parts,), jnp.float32, smallest / len(shards), largest / len(shards))
        return jnp.repeat(jnp.exp(heights), dims[axis_at] // parts).reshape((-1,) + (1,) * (len(dims) - axis_at - 1))

    gain = one(*shards[0])
    for cut in shards[1:]:
        gain = gain * one(*cut)
    return gain


def setup_inputs(seed: int = 0, part: int = 0) -> dict:
    arg_keys = jax.random.split(jax.random.key(seed), 7)
    part_splits = jax.random.split(jax.random.fold_in(arg_keys[6], part), 7)
    return {
        "samples": draw_samples(jax.random.fold_in(jax.random.fold_in(arg_keys[6], part), 71), part),
        "omega_diag": draw_omega_diag(jax.random.fold_in(jax.random.fold_in(arg_keys[6], part), 71), part),
        "omega_off": draw_omega_off(jax.random.fold_in(jax.random.fold_in(arg_keys[6], part), 71), part),
        "pattern": draw_pattern(jax.random.fold_in(jax.random.fold_in(arg_keys[6], part), 71), part),
        "block_count": draw_block_count(jax.random.fold_in(jax.random.fold_in(arg_keys[6], part), 71), part),
        "diag_term": jnp.clip(-1.0 + 0.5 * jax.random.uniform(part_splits[5], (VARIABLES,), jnp.float32) ** block_scale(part_splits[5], (VARIABLES,), ((0, 16),), -0.2, 0.2), -1.0, -0.5),
    }


STEP_SIZE = 0.5
PENALTY = 0.01


def soften(values, level):
    return values - jnp.clip(values, -level, level)


def reference(samples, omega_diag, omega_off, pattern, block_count, diag_term):
    highest = lax.Precision.HIGHEST
    block_total = BR_DEV * N_ROWS
    entry_total = ENTRIES * N_ROWS
    xblocks = samples.astype(jnp.float32).reshape(block_total, BLOCK, SAMPLES)
    positions = jnp.arange(entry_total, dtype=jnp.int32)
    per_device = jnp.sum(block_count.reshape(N_ROWS, BR_DEV), axis=1)
    living = (positions % ENTRIES) < per_device[positions // ENTRIES]
    row_ids = pattern[:, 0]
    col_ids = pattern[:, 1]
    masked = jnp.where(living[:, None, None], omega_off, 0.0)
    projected = jnp.einsum("kab,kbn->kan", omega_diag, xblocks, precision=highest)
    device_ids = jnp.arange(N_ROWS, dtype=jnp.int32)

    def add_device(carry, device):
        start = device * ENTRIES
        blocks = lax.dynamic_slice_in_dim(masked, start, ENTRIES, 0)
        targets = lax.dynamic_slice_in_dim(row_ids, start, ENTRIES, 0)
        sources = lax.dynamic_slice_in_dim(col_ids, start, ENTRIES, 0)
        contributions = jnp.einsum("eab,ebn->ean", blocks, xblocks[sources], precision=highest)
        return carry + jax.ops.segment_sum(contributions, targets, num_segments=block_total), None

    projected = lax.scan(add_device, projected, device_ids)[0]

    def products(device):
        start = device * ENTRIES
        targets = lax.dynamic_slice_in_dim(row_ids, start, ENTRIES, 0)
        sources = lax.dynamic_slice_in_dim(col_ids, start, ENTRIES, 0)
        return jnp.einsum("ean,ebn->eab", projected[targets], xblocks[sources], precision=highest)

    off_products = lax.map(products, device_ids).reshape(entry_total, BLOCK, BLOCK)
    entry_keys = jnp.where(living, row_ids * block_total + col_ids, block_total * block_total + positions)
    ordering = jnp.argsort(entry_keys)
    located = jnp.searchsorted(entry_keys[ordering], col_ids * block_total + row_ids)
    partner = ordering[jnp.clip(located, 0, entry_total - 1)]
    mirrored = jnp.swapaxes(off_products[partner], 1, 2)
    gradient = (off_products + mirrored) / (2.0 * SAMPLES)
    off_next = jnp.where(living[:, None, None], soften(omega_off - STEP_SIZE * gradient, STEP_SIZE * PENALTY), 0.0)
    diag_products = jnp.einsum("kan,kbn->kab", projected, xblocks, precision=highest)
    identity = jnp.eye(BLOCK, dtype=jnp.float32)[None]
    diag_gradient = (diag_products + jnp.swapaxes(diag_products, 1, 2)) / (2.0 * SAMPLES) + identity * diag_term.reshape(block_total, BLOCK)[:, :, None]
    moved = omega_diag - STEP_SIZE * diag_gradient
    diag_next = jnp.where(identity > 0.5, moved, soften(moved, STEP_SIZE * PENALTY))
    objective = (jnp.sum(projected * projected) / (2.0 * SAMPLES) - jnp.sum(jnp.log(jnp.diagonal(omega_diag, axis1=1, axis2=2)))) / (block_total * BLOCK)
    return diag_next, off_next, objective.reshape(1)
```

```python
import functools

import jax
import jax.numpy as jnp
from jax import lax
from jax.experimental import pallas as pl
from jax.experimental.pallas import tpu as pltpu
from jax.sharding import PartitionSpec as P

SLOTS = 2
STAT_ROWS = 8
STEP_SIZE = 0.5
PENALTY = 0.01
LOG_STEPS = 128.0
HEADROOM = 1e-4
FRACTION = 32000.0
VMEM_LIMIT = 60 * 1024 * 1024


def soften(values, level):
    return values - jnp.clip(values, -level, level)


def split_halves(values):
    high = values.astype(jnp.bfloat16)
    low = (values - high.astype(jnp.float32)).astype(jnp.bfloat16)
    return high, low


def unroll_of(entries):
    return max(k for k in range(1, 7) if entries % k == 0)


def live_count(count, rows_dev):
    total = count[0]
    for k in range(1, rows_dev):
        total = total + count[k]
    return total


def pack_kernel(pattern, count, x, send, slots, first, sems, *, rows_dev, devices, entries, block_total):
    live = live_count(count, rows_dev)
    position = pattern[0, 0] // rows_dev
    base = position * rows_dev

    def clear(o, carry):
        first[o] = -1
        return carry

    lax.fori_loop(0, devices, clear, 0)

    def key(e):
        i = pattern[e, 0]
        j = pattern[e, 1]
        return jnp.minimum(i, j) * block_total + jnp.maximum(i, j)

    def copy(e, slot):
        return pltpu.make_async_copy(x.at[pattern[e, 0] - base], send.at[slot], sems.at[e])

    spare = pltpu.make_async_copy(x.at[0], send.at[position * SLOTS], sems.at[entries])
    spare.start()

    def place(e, carry):
        owner = pattern[e, 1] // rows_dev
        earlier = first[owner]

        @pl.when(earlier < 0)
        def _():
            first[owner] = e

        @pl.when(earlier >= 0)
        def _():
            later = jnp.where(key(e) > key(earlier), 1, 0)
            slots[e] = owner * SLOTS + later
            slots[earlier] = owner * SLOTS + 1 - later
            copy(e, owner * SLOTS + later).start()
            copy(earlier, owner * SLOTS + 1 - later).start()

        return carry

    lax.fori_loop(0, live, place, 0)

    def rest(e, carry):
        slots[e] = position * SLOTS
        return carry

    lax.fori_loop(live, entries, rest, 0)
    spare.wait()

    def drain(e, carry):
        copy(e, slots[e]).wait()
        return carry

    lax.fori_loop(0, live, drain, 0)


def own_kernel(x, omega, projected, logs, *, rows_dev, edge):
    on_diagonal = lax.broadcasted_iota(jnp.int32, (edge, edge), 0) == lax.broadcasted_iota(
        jnp.int32, (edge, edge), 1
    )
    total = jnp.zeros((1, edge), jnp.float32)
    for k in range(rows_dev):
        block = omega[k]
        high, low = split_halves(block)
        rows = x[k]
        projected[k] = jnp.dot(
            jnp.concatenate([high, low], axis=1),
            jnp.concatenate([rows, rows], axis=0),
            preferred_element_type=jnp.float32,
        )
        total = total + jnp.log(jnp.sum(jnp.where(on_diagonal, block, 0.0), axis=0, keepdims=True))
    logs[...] = jnp.broadcast_to(total, logs.shape)


def main_kernel(
    pattern,
    count,
    slots,
    own,
    logs,
    arrived,
    omega,
    moved,
    payload,
    projected,
    xs,
    om,
    mv,
    halves,
    stats,
    sem_x,
    sem_o,
    sem_m,
    *,
    rows_dev,
    devices,
    entries,
    edge,
    samples_dev,
):
    live = live_count(count, rows_dev)
    base = (pattern[0, 0] // rows_dev) * rows_dev
    unroll = unroll_of(entries)

    def fetch(e):
        return pltpu.make_async_copy(arrived.at[slots[e]], xs.at[e], sem_x.at[e])

    def fetch_omega(e):
        return pltpu.make_async_copy(omega.at[e], om.at[e], sem_o.at[e])

    def store(e):
        return pltpu.make_async_copy(mv.at[e], moved.at[e], sem_m.at[e])

    def begin(e, carry):
        fetch(e).start()
        fetch_omega(e).start()
        return carry

    lax.fori_loop(0, entries, begin, 0)
    projected[...] = own[...]
    stats[...] = jnp.zeros(stats.shape, jnp.float32)

    def gather(step, carry):
        parts = []
        for k in range(unroll):
            e = step * unroll + k
            fetch(e).wait()
            fetch_omega(e).wait()
            high, low = split_halves(jnp.where(e < live, om[e], 0.0))
            rows = xs[e]
            parts.append(
                jnp.dot(
                    jnp.concatenate([high, low], axis=1),
                    jnp.concatenate([rows, rows], axis=0),
                    preferred_element_type=jnp.float32,
                )
            )
        for k in range(unroll):
            row = pattern[step * unroll + k, 0] - base
            projected[row] = projected[row] + parts[k]
        return carry

    lax.fori_loop(0, entries // unroll, gather, 0)

    squares = jnp.zeros((edge, samples_dev), jnp.float32)
    for k in range(rows_dev):
        values = projected[k]
        squares = squares + values * values
        high, low = split_halves(values)
        halves[k, :edge] = high
        halves[k, edge:] = low

    def products(step, carry):
        for k in range(unroll):
            e = step * unroll + k
            row = pattern[e, 0] - base
            both = lax.dot_general(
                halves[row], xs[e], (((1,), (1,)), ((), ())), preferred_element_type=jnp.float32
            )
            product = both[:edge] + both[edge:]
            mv[e] = om[e] - product * (STEP_SIZE / (2.0 * samples_dev))
            store(e).start()
            largest = jnp.maximum(jnp.max(jnp.abs(product), axis=0, keepdims=True), 1e-30)
            code = jnp.ceil(jnp.log2(largest) * LOG_STEPS + 0.01)
            scaled = product * jnp.exp2(15.0 - HEADROOM - code * (1.0 / LOG_STEPS))
            slot = slots[e]
            owner = slot // SLOTS
            rank = slot - owner * SLOTS
            payload[owner, pl.ds(pl.multiple_of(rank * edge, edge), edge), :] = (
                jnp.round(scaled).astype(jnp.int32).astype(jnp.int16)
            )
            stats[owner, pl.ds(rank, 1), :] = code
        return carry

    lax.fori_loop(0, entries // unroll, products, 0)

    term = jnp.sum(squares) * (1.0 / (2.0 * samples_dev)) - jnp.sum(logs[0:1, :])
    term = jnp.full((1, edge), term, jnp.float32)
    power = jnp.ceil(jnp.log2(jnp.maximum(jnp.abs(term), 1e-30)) + 0.01)
    scaled = term * jnp.exp2(14.0 - power)
    whole = jnp.round(scaled)
    digits = jnp.concatenate(
        [
            jnp.zeros((SLOTS, edge), jnp.float32),
            power,
            whole,
            jnp.round((scaled - whole) * FRACTION),
            jnp.zeros((STAT_ROWS - SLOTS - 3, edge), jnp.float32),
        ],
        axis=0,
    )
    payload[:, SLOTS * edge :, :] = (stats[...] + digits[None]).astype(jnp.int32).astype(jnp.int16)

    def finish(e, carry):
        store(e).wait()
        return carry

    lax.fori_loop(0, entries, finish, 0)


def diagonal_kernel(x, omega, term, projected, result, *, rows_dev, edge, samples_dev):
    on_diagonal = lax.broadcasted_iota(jnp.int32, (edge, edge), 0) == lax.broadcasted_iota(
        jnp.int32, (edge, edge), 1
    )
    for k in range(rows_dev):
        high, low = split_halves(projected[k])
        both = lax.dot_general(
            jnp.concatenate([high, low], axis=0),
            x[k],
            (((1,), (1,)), ((), ())),
            preferred_element_type=jnp.float32,
        )
        product = both[:edge] + both[edge:]
        gradient = (product + product.T) * (1.0 / (2.0 * samples_dev))
        gradient = gradient + jnp.where(on_diagonal, term[k : k + 1, :], 0.0)
        value = omega[k] - STEP_SIZE * gradient
        result[k] = jnp.where(on_diagonal, value, soften(value, STEP_SIZE * PENALTY))


def last_kernel(
    count,
    slots,
    moved,
    returned,
    result,
    objective,
    mv,
    rt,
    rs,
    sem_m,
    sem_r,
    sem_o,
    *,
    rows_dev,
    devices,
    entries,
    edge,
    samples_dev,
):
    live = live_count(count, rows_dev)
    unroll = unroll_of(entries)

    def fetch(e):
        return pltpu.make_async_copy(moved.at[e], mv.at[e], sem_m.at[e])

    def store(e):
        return pltpu.make_async_copy(rs.at[e], result.at[e], sem_o.at[e])

    whole = pltpu.make_async_copy(returned, rt, sem_r.at[0])
    whole.start()

    def begin(e, carry):
        fetch(e).start()
        return carry

    lax.fori_loop(0, entries, begin, 0)
    whole.wait()

    def update(step, carry):
        for k in range(unroll):
            e = step * unroll + k
            fetch(e).wait()
            slot = slots[e]
            owner = slot // SLOTS
            rank = slot - owner * SLOTS
            codes = rt[owner, SLOTS * edge :, :].astype(jnp.int32).astype(jnp.float32)
            code = jnp.where(rank == 0, codes[0:1], codes[1:2])
            digits = rt[owner, pl.ds(pl.multiple_of(rank * edge, edge), edge), :]
            mirrored = digits.astype(jnp.int32).astype(jnp.float32) * jnp.exp2(
                code * (1.0 / LOG_STEPS) - (15.0 - HEADROOM)
            )
            value = mv[e] - mirrored.T * (STEP_SIZE / (2.0 * samples_dev))
            rs[e] = jnp.where(e < live, soften(value, STEP_SIZE * PENALTY), 0.0)
            store(e).start()
        return carry

    lax.fori_loop(0, entries // unroll, update, 0)
    codes = rt[:, SLOTS * edge :, :].astype(jnp.int32).astype(jnp.float32)
    power = codes[:, SLOTS : SLOTS + 1]
    digits = codes[:, SLOTS + 1 : SLOTS + 2] + codes[:, SLOTS + 2 : SLOTS + 3] * (1.0 / FRACTION)
    total = jnp.sum(digits * jnp.exp2(power - 14.0), axis=0)
    objective[...] = jnp.broadcast_to(
        total * (1.0 / (devices * rows_dev * edge)), objective.shape
    )

    def finish(e, carry):
        store(e).wait()
        return carry

    lax.fori_loop(0, entries, finish, 0)


def shards(samples, omega_diag, omega_off, pattern, block_count, diag_term):
    devices = lax.axis_size("rows")
    rows_dev, edge = omega_diag.shape[:2]
    samples_dev = samples.shape[1]
    entries = omega_off.shape[0]
    capacity = devices * SLOTS
    f32 = jnp.float32
    x = samples.reshape(rows_dev, edge, samples_dev)
    term = diag_term.reshape(rows_dev, edge)
    smem = pl.BlockSpec(memory_space=pltpu.SMEM)
    vmem = pl.BlockSpec(memory_space=pltpu.VMEM)
    hbm = pl.BlockSpec(memory_space=pl.ANY)
    dma = pltpu.SemaphoreType.DMA
    params = pltpu.CompilerParams(vmem_limit_bytes=VMEM_LIMIT)

    send, slots = pl.pallas_call(
        functools.partial(
            pack_kernel,
            rows_dev=rows_dev,
            devices=devices,
            entries=entries,
            block_total=rows_dev * devices,
        ),
        out_shape=(
            jax.ShapeDtypeStruct((capacity, edge, samples_dev), samples.dtype),
            jax.ShapeDtypeStruct((entries,), jnp.int32),
        ),
        in_specs=[smem, smem, vmem],
        out_specs=(hbm, smem),
        scratch_shapes=[pltpu.SMEM((devices,), jnp.int32), dma((entries + 1,))],
        compiler_params=params,
        name="pack",
    )(pattern, block_count, x)

    arrived = lax.all_to_all(
        send.reshape(devices, SLOTS, edge, samples_dev),
        "rows",
        split_axis=0,
        concat_axis=0,
        tiled=True,
    ).reshape(capacity, edge, samples_dev)

    own, logs = pl.pallas_call(
        functools.partial(own_kernel, rows_dev=rows_dev, edge=edge),
        out_shape=(
            jax.ShapeDtypeStruct((rows_dev, edge, samples_dev), f32),
            jax.ShapeDtypeStruct((8, edge), f32),
        ),
        in_specs=[vmem, vmem],
        out_specs=(vmem, vmem),
        compiler_params=params,
        cost_estimate=pl.CostEstimate(
            flops=4 * rows_dev * edge * edge * samples_dev, transcendentals=0, bytes_accessed=1 << 21
        ),
        name="own",
    )(x, omega_diag)

    moved, payload, projected = pl.pallas_call(
        functools.partial(
            main_kernel,
            rows_dev=rows_dev,
            devices=devices,
            entries=entries,
            edge=edge,
            samples_dev=samples_dev,
        ),
        out_shape=(
            jax.ShapeDtypeStruct((entries, edge, edge), f32),
            jax.ShapeDtypeStruct((devices, SLOTS * edge + STAT_ROWS, edge), jnp.int16),
            jax.ShapeDtypeStruct((rows_dev, edge, samples_dev), f32),
        ),
        in_specs=[smem, smem, smem, vmem, vmem, hbm, hbm],
        out_specs=(hbm, vmem, vmem),
        scratch_shapes=[
            pltpu.VMEM((entries, edge, samples_dev), samples.dtype),
            pltpu.VMEM((entries, edge, edge), f32),
            pltpu.VMEM((entries, edge, edge), f32),
            pltpu.VMEM((rows_dev, 2 * edge, samples_dev), jnp.bfloat16),
            pltpu.VMEM((devices, STAT_ROWS, edge), f32),
            dma((entries,)),
            dma((entries,)),
            dma((entries,)),
        ],
        compiler_params=params,
        name="main",
    )(pattern, block_count, slots, own, logs, arrived, omega_off)

    returned = lax.all_to_all(payload, "rows", split_axis=0, concat_axis=0, tiled=True)

    diag_next = pl.pallas_call(
        functools.partial(diagonal_kernel, rows_dev=rows_dev, edge=edge, samples_dev=samples_dev),
        out_shape=jax.ShapeDtypeStruct((rows_dev, edge, edge), f32),
        in_specs=[vmem, vmem, vmem, vmem],
        out_specs=vmem,
        compiler_params=params,
        cost_estimate=pl.CostEstimate(
            flops=4 * rows_dev * edge * edge * samples_dev, transcendentals=0, bytes_accessed=1 << 21
        ),
        name="diagonal",
    )(x, omega_diag, term, projected)

    off_next, objective = pl.pallas_call(
        functools.partial(
            last_kernel,
            rows_dev=rows_dev,
            devices=devices,
            entries=entries,
            edge=edge,
            samples_dev=samples_dev,
        ),
        out_shape=(
            jax.ShapeDtypeStruct((entries, edge, edge), f32),
            jax.ShapeDtypeStruct((8, edge), f32),
        ),
        in_specs=[smem, smem, hbm, hbm],
        out_specs=(hbm, vmem),
        scratch_shapes=[
            pltpu.VMEM((entries, edge, edge), f32),
            pltpu.VMEM((devices, SLOTS * edge + STAT_ROWS, edge), jnp.int16),
            pltpu.VMEM((entries, edge, edge), f32),
            dma((entries,)),
            dma((1,)),
            dma((entries,)),
        ],
        compiler_params=params,
        name="last",
    )(block_count, slots, moved, returned)
    return diag_next, off_next, objective[0, :1]


def solution(mesh):
    return jax.shard_map(
        shards,
        mesh=mesh,
        in_specs=(
            P(("groups", "rows"), None),
            P(("groups", "rows"), None, None),
            P(("groups", "rows"), None, None),
            P(("groups", "rows"), None),
            P(("groups", "rows")),
            P(("groups", "rows")),
        ),
        out_specs=(
            P(("groups", "rows"), None, None),
            P(("groups", "rows"), None, None),
            P("groups"),
        ),
        check_vma=False,
    )
```

```python
import functools

import jax
import jax.numpy as jnp
from jax import lax
from jax.experimental import pallas as pl
from jax.experimental.pallas import tpu as pltpu
from jax.sharding import PartitionSpec as P

SLOTS = 2
STAT_ROWS = 8
STEP_SIZE = 0.5
PENALTY = 0.01
LOG_STEPS = 128.0
HEADROOM = 1e-4
FRACTION = 32000.0
VMEM_LIMIT = 40 * 1024 * 1024
VMEM_ALONE = 60 * 1024 * 1024


def soften(values, level):
    return values - jnp.clip(values, -level, level)


def split_halves(values):
    high = values.astype(jnp.bfloat16)
    low = (values - high.astype(jnp.float32)).astype(jnp.bfloat16)
    return high, low


def divide(value, by):
    if by & (by - 1):
        return value // by
    return lax.shift_right_logical(value, by.bit_length() - 1)


def parts_of(entries, head):
    first = max(1, entries // 5)
    first = first if head else entries - first
    return ((0, first), (first, entries - first))


def live_count(count, rows_dev):
    total = count[0]
    for k in range(1, rows_dev):
        total = total + count[k]
    return total


def pack_kernel(pattern, count, x, send, slots, sums, sems, *, rows_dev, devices, entries, block_total):
    live = live_count(count, rows_dev)
    position = divide(pattern[0, 0], rows_dev)
    base = position * rows_dev

    def key(e):
        i = pattern[0, e]
        j = pattern[1, e]
        return jnp.minimum(i, j) * block_total + jnp.maximum(i, j)

    def copy(e):
        return pltpu.make_async_copy(x.at[pattern[0, e] - base], send.at[slots[e]], sems.at[e])

    spare = pltpu.make_async_copy(x.at[0], send.at[position * SLOTS], sems.at[entries])
    spare.start()
    for o in range(devices):
        sums[o] = 0
    for e in range(entries):
        owner = divide(pattern[1, e], rows_dev)
        sums[owner] = sums[owner] + key(e)
    for e in range(entries):
        owner = divide(pattern[1, e], rows_dev)
        later = jnp.where((2 * key(e) > sums[owner]) & (e < live), 1, 0)
        slots[e] = owner * SLOTS + later

    def begin(e, carry):
        copy(e).start()
        return carry

    def finish(e, carry):
        copy(e).wait()
        return carry

    lax.fori_loop(0, live, begin, 0)
    spare.wait()
    lax.fori_loop(0, live, finish, 0)


def own_kernel(count, x, omega, off, projected, logs, wide, *, rows_dev, entries, edge):
    live = live_count(count, rows_dev)
    on_diagonal = lax.broadcasted_iota(jnp.int32, (edge, edge), 0) == lax.broadcasted_iota(
        jnp.int32, (edge, edge), 1
    )
    total = jnp.zeros((1, edge), jnp.float32)
    for k in range(rows_dev):
        block = omega[k]
        high, low = split_halves(block)
        rows = x[k]
        projected[k] = jnp.dot(
            jnp.concatenate([high, low], axis=1),
            jnp.concatenate([rows, rows], axis=0),
            preferred_element_type=jnp.float32,
        )
        total = total + jnp.log(jnp.sum(jnp.where(on_diagonal, block, 0.0), axis=0, keepdims=True))
    logs[...] = jnp.broadcast_to(total, logs.shape)

    def widen(e, carry):
        high, low = split_halves(jnp.where(e < live, off[e], 0.0))
        wide[e, :, :edge] = high
        wide[e, :, edge:] = low
        return carry

    lax.fori_loop(0, entries, widen, 0)


def main_kernel(
    pattern,
    count,
    slots,
    logs,
    arrived,
    own,
    wide,
    payload,
    projected,
    held_wide,
    held_own,
    held_rows,
    halves,
    coded,
    stats,
    tail,
    sem_wide,
    sem_own,
    sem_rows,
    sem_code,
    *,
    rows_dev,
    devices,
    entries,
    edge,
    samples_dev,
):
    live = live_count(count, rows_dev)
    base = divide(pattern[0, 0], rows_dev) * rows_dev
    fetches = []
    for at, (start, size) in enumerate(parts_of(entries, True)):
        part = pl.ds(start, size)
        fetches.append(pltpu.make_async_copy(wide.at[part], held_wide.at[part], sem_wide.at[at]))
        fetches[-1].start()
    fetch_own = pltpu.make_async_copy(own, held_own, sem_own.at[0])
    fetch_own.start()
    held_rows[...] = jnp.zeros(held_rows.shape, jnp.float32)
    stats[...] = jnp.zeros(stats.shape, jnp.float32)

    for at, (start, size) in enumerate(parts_of(entries, True)):
        fetches[at].wait()
        for e in range(start, start + size):
            rows = arrived[slots[e]]
            part = jnp.dot(
                held_wide[e],
                jnp.concatenate([rows, rows], axis=0),
                preferred_element_type=jnp.float32,
            )
            row = pattern[0, e] - base
            held_rows[row] = held_rows[row] + part

    fetch_own.wait()
    squares = jnp.zeros((8, samples_dev), jnp.float32)
    for k in range(rows_dev):
        values = held_rows[k] + held_own[k]
        held_own[k] = values
        squares = squares + jnp.sum((values * values).reshape(edge // 8, 8, samples_dev), axis=0)
        high, low = split_halves(values)
        halves[k, :edge] = high
        halves[k, edge:] = low
    store_rows = pltpu.make_async_copy(held_own, projected, sem_rows.at[0])
    store_rows.start()

    def store(e):
        slot = slots[e]
        owner = divide(slot, SLOTS)
        rank = slot - owner * SLOTS
        return pltpu.make_async_copy(
            coded.at[e],
            payload.at[owner, pl.ds(pl.multiple_of(rank * edge, edge), edge), :],
            sem_code.at[e],
        )

    for start, size in parts_of(entries, False):
        for e in range(start, start + size):
            row = pattern[0, e] - base
            slot = slots[e]
            both = lax.dot_general(
                arrived[slot],
                halves[row],
                (((1,), (1,)), ((), ())),
                preferred_element_type=jnp.float32,
            )
            product = both[:, :edge] + both[:, edge:]
            largest = jnp.maximum(jnp.max(jnp.abs(product), axis=0, keepdims=True), 1e-30)
            code = jnp.ceil(jnp.log2(largest) * LOG_STEPS + 0.01)
            scaled = product * jnp.exp2(15.0 - HEADROOM - code * (1.0 / LOG_STEPS))
            owner = divide(slot, SLOTS)
            rank = slot - owner * SLOTS
            coded[e] = jnp.round(scaled).astype(jnp.int32).astype(jnp.int16)
            stats[owner, pl.ds(rank, 1), :] = code

        def begin(e, carry):
            store(e).start()
            return carry

        lax.fori_loop(start, jnp.clip(live, start, start + size), begin, 0)

    term = jnp.sum(squares) * (1.0 / (2.0 * samples_dev)) - jnp.sum(logs[0:1, :])
    term = jnp.full((1, edge), term, jnp.float32)
    power = jnp.ceil(jnp.log2(jnp.maximum(jnp.abs(term), 1e-30)) + 0.01)
    scaled = term * jnp.exp2(14.0 - power)
    whole = jnp.round(scaled)
    digits = jnp.concatenate(
        [
            jnp.zeros((SLOTS, edge), jnp.float32),
            power,
            whole,
            jnp.round((scaled - whole) * FRACTION),
            jnp.zeros((STAT_ROWS - SLOTS - 3, edge), jnp.float32),
        ],
        axis=0,
    )
    tail[...] = (stats[...] + digits[None]).astype(jnp.int32).astype(jnp.int16)
    store_tail = pltpu.make_async_copy(
        tail, payload.at[:, pl.ds(SLOTS * edge, STAT_ROWS), :], sem_code.at[entries]
    )
    store_tail.start()

    def finish(e, carry):
        store(e).wait()
        return carry

    lax.fori_loop(0, live, finish, 0)
    store_rows.wait()
    store_tail.wait()


def side_kernel(
    pattern,
    count,
    slots,
    x,
    omega,
    term,
    projected,
    off,
    arrived,
    result,
    moved,
    halves,
    *,
    rows_dev,
    entries,
    edge,
    samples_dev,
):
    live = live_count(count, rows_dev)
    base = divide(pattern[0, 0], rows_dev) * rows_dev
    on_diagonal = lax.broadcasted_iota(jnp.int32, (edge, edge), 0) == lax.broadcasted_iota(
        jnp.int32, (edge, edge), 1
    )

    def against(row, other):
        both = lax.dot_general(
            halves[row], other, (((1,), (1,)), ((), ())), preferred_element_type=jnp.float32
        )
        return both[:edge] + both[edge:]

    for k in range(rows_dev):
        high, low = split_halves(projected[k])
        halves[k, :edge] = high
        halves[k, edge:] = low
        product = against(k, x[k])
        gradient = (product + product.T) * (1.0 / (2.0 * samples_dev))
        gradient = gradient + jnp.where(on_diagonal, term[k : k + 1, :], 0.0)
        value = omega[k] - STEP_SIZE * gradient
        result[k] = jnp.where(on_diagonal, value, soften(value, STEP_SIZE * PENALTY))

    def move(e, carry):
        product = against(pattern[0, e] - base, arrived[slots[e]])
        value = off[e] - product * (STEP_SIZE / (2.0 * samples_dev))
        moved[e] = jnp.where(e < live, value, 0.0)
        return carry

    lax.fori_loop(0, entries, move, 0)


def last_kernel(
    count,
    slots,
    moved,
    returned,
    result,
    objective,
    held,
    rs,
    sem_in,
    sem_out,
    *,
    rows_dev,
    devices,
    entries,
    edge,
    samples_dev,
):
    live = live_count(count, rows_dev)

    def fetch(at, part):
        return pltpu.make_async_copy(moved.at[part], held.at[part], sem_in.at[at])

    def store(at, part):
        return pltpu.make_async_copy(rs.at[part], result.at[part], sem_out.at[at])

    width = max(k for k in range(1, 11) if entries % k == 0)
    parts = [(at, pl.ds(at * width, width)) for at in range(entries // width)]
    for at, part in parts:
        fetch(at, part).start()
    codes = returned[:, SLOTS * edge :, :].astype(jnp.int32).astype(jnp.float32)
    power = codes[:, SLOTS : SLOTS + 1]
    digits = codes[:, SLOTS + 1 : SLOTS + 2] + codes[:, SLOTS + 2 : SLOTS + 3] * (1.0 / FRACTION)
    total = jnp.sum(digits * jnp.exp2(power - 14.0), axis=0)
    objective[0] = jnp.max(total) * (1.0 / (devices * rows_dev * edge))
    for at, part in parts:
        fetch(at, part).wait()
        for e in range(at * width, (at + 1) * width):
            slot = slots[e]
            owner = divide(slot, SLOTS)
            rank = slot - owner * SLOTS
            codes = returned[owner, SLOTS * edge :, :].astype(jnp.int32).astype(jnp.float32)
            code = jnp.where(rank == 0, codes[0:1], codes[1:2])
            weight = jnp.exp2(code * (1.0 / LOG_STEPS) - (15.0 - HEADROOM)) * (
                STEP_SIZE / (2.0 * samples_dev)
            )
            weight = jnp.where(e < live, weight, 0.0)
            digits = returned[owner, pl.ds(pl.multiple_of(rank * edge, edge), edge), :]
            value = held[e] - digits.astype(jnp.int32).astype(jnp.float32) * weight
            rs[e] = soften(value, STEP_SIZE * PENALTY)
        store(at, part).start()
    for at, part in parts:
        store(at, part).wait()


def shards(samples, omega_diag, omega_off, pattern, block_count, diag_term):
    devices = lax.axis_size("rows")
    rows_dev, edge = omega_diag.shape[:2]
    samples_dev = samples.shape[1]
    entries = omega_off.shape[0]
    capacity = devices * SLOTS
    f32 = jnp.float32
    x = samples.reshape(rows_dev, edge, samples_dev)
    term = diag_term.reshape(rows_dev, edge)
    pattern = pattern.T
    smem = pl.BlockSpec(memory_space=pltpu.SMEM)
    vmem = pl.BlockSpec(memory_space=pltpu.VMEM)
    hbm = pl.BlockSpec(memory_space=pltpu.HBM)
    params = pltpu.CompilerParams(vmem_limit_bytes=VMEM_LIMIT)
    alone = pltpu.CompilerParams(vmem_limit_bytes=VMEM_ALONE)
    sizes = dict(rows_dev=rows_dev, entries=entries, edge=edge)
    every = dict(sizes, devices=devices, samples_dev=samples_dev)
    held = functools.partial(pltpu.with_memory_space_constraint, memory_space=pltpu.VMEM)
    kept = functools.partial(pltpu.with_memory_space_constraint, memory_space=pltpu.HBM)

    dma = pltpu.SemaphoreType.DMA

    send, slots = pl.pallas_call(
        functools.partial(
            pack_kernel,
            rows_dev=rows_dev,
            devices=devices,
            entries=entries,
            block_total=rows_dev * devices,
        ),
        out_shape=(
            jax.ShapeDtypeStruct((capacity, edge, samples_dev), samples.dtype),
            jax.ShapeDtypeStruct((entries,), jnp.int32),
        ),
        in_specs=[smem, smem, hbm],
        out_specs=(hbm, smem),
        scratch_shapes=[pltpu.SMEM((devices,), jnp.int32), dma((entries + 1,))],
        compiler_params=alone,
        name="pack",
    )(pattern, block_count, x)

    arrived = lax.all_to_all(
        send.reshape(devices, SLOTS, edge, samples_dev),
        "rows",
        split_axis=0,
        concat_axis=0,
        tiled=True,
    ).reshape(capacity, edge, samples_dev)

    own, logs, wide = pl.pallas_call(
        functools.partial(own_kernel, **sizes),
        out_shape=(
            pltpu.HBM((rows_dev, edge, samples_dev), f32),
            jax.ShapeDtypeStruct((8, edge), f32),
            pltpu.HBM((entries, edge, 2 * edge), jnp.bfloat16),
        ),
        in_specs=[smem, vmem, vmem, vmem],
        out_specs=(vmem, vmem, vmem),
        compiler_params=params,
        cost_estimate=pl.CostEstimate(
            flops=4 * rows_dev * edge * edge * samples_dev, transcendentals=0, bytes_accessed=1 << 23
        ),
        name="own",
    )(block_count, x, omega_diag, omega_off)

    payload, projected = pl.pallas_call(
        functools.partial(main_kernel, **every),
        out_shape=(
            pltpu.HBM((devices, SLOTS * edge + STAT_ROWS, edge), jnp.int16),
            pltpu.HBM((rows_dev, edge, samples_dev), f32),
        ),
        in_specs=[smem, smem, smem, vmem, vmem, hbm, hbm],
        out_specs=(hbm, hbm),
        scratch_shapes=[
            pltpu.VMEM((entries, edge, 2 * edge), jnp.bfloat16),
            pltpu.VMEM((rows_dev, edge, samples_dev), f32),
            pltpu.VMEM((rows_dev, edge, samples_dev), f32),
            pltpu.VMEM((rows_dev, 2 * edge, samples_dev), jnp.bfloat16),
            pltpu.VMEM((entries, edge, edge), jnp.int16),
            pltpu.VMEM((devices, STAT_ROWS, edge), f32),
            pltpu.VMEM((devices, STAT_ROWS, edge), jnp.int16),
            dma((2,)),
            dma((1,)),
            dma((1,)),
            dma((entries + 1,)),
        ],
        compiler_params=params,
        name="main",
    )(pattern, block_count, slots, logs, held(arrived), kept(own), kept(wide))

    returned = lax.all_to_all(kept(payload), "rows", split_axis=0, concat_axis=0, tiled=True)

    diag_next, moved = pl.pallas_call(
        functools.partial(side_kernel, samples_dev=samples_dev, **sizes),
        out_shape=(
            jax.ShapeDtypeStruct((rows_dev, edge, edge), f32),
            pltpu.HBM((entries, edge, edge), f32),
        ),
        in_specs=[smem] * 3 + [vmem] * 6,
        out_specs=(vmem, vmem),
        scratch_shapes=[pltpu.VMEM((rows_dev, 2 * edge, samples_dev), jnp.bfloat16)],
        compiler_params=params,
        cost_estimate=pl.CostEstimate(
            flops=4 * rows_dev * edge * edge * samples_dev, transcendentals=0, bytes_accessed=1 << 23
        ),
        name="side",
    )(pattern, block_count, slots, x, omega_diag, term, projected, omega_off, arrived)

    off_next, objective = pl.pallas_call(
        functools.partial(last_kernel, **every),
        out_shape=(
            jax.ShapeDtypeStruct((entries, edge, edge), f32),
            jax.ShapeDtypeStruct((1,), f32),
        ),
        in_specs=[smem, smem, hbm, vmem],
        out_specs=(hbm, smem),
        scratch_shapes=[
            pltpu.VMEM((entries, edge, edge), f32),
            pltpu.VMEM((entries, edge, edge), f32),
            dma((entries,)),
            dma((entries,)),
        ],
        compiler_params=params,
        name="last",
    )(block_count, slots, kept(moved), held(returned))
    return diag_next, off_next, objective


def solution(mesh):
    return jax.shard_map(
        shards,
        mesh=mesh,
        in_specs=(
            P(("groups", "rows"), None),
            P(("groups", "rows"), None, None),
            P(("groups", "rows"), None, None),
            P(("groups", "rows"), None),
            P(("groups", "rows")),
            P(("groups", "rows")),
        ),
        out_specs=(
            P(("groups", "rows"), None, None),
            P(("groups", "rows"), None, None),
            P("groups"),
        ),
        check_vma=False,
    )
```

```python
import functools

import jax
import jax.numpy as jnp
from jax import lax
from jax.experimental import pallas as pl
from jax.experimental.pallas import tpu as pltpu
from jax.sharding import PartitionSpec as P

SLOTS = 2
STAT_ROWS = 8
STEP_SIZE = 0.5
PENALTY = 0.01
LOG_STEPS = 128.0
HEADROOM = 1e-4
FRACTION = 32000.0
VMEM_LIMIT = 40 * 1024 * 1024
VMEM_ALONE = 60 * 1024 * 1024


def soften(values, level):
    return values - jnp.clip(values, -level, level)


def split_halves(values):
    high = values.astype(jnp.bfloat16)
    low = (values - high.astype(jnp.float32)).astype(jnp.bfloat16)
    return high, low


def divide(value, by):
    if by & (by - 1):
        return value // by
    return lax.shift_right_logical(value, by.bit_length() - 1)


def parts_of(entries, head):
    first = max(1, entries // 5)
    first = first if head else entries - first
    return ((0, first), (first, entries - first))


def live_count(count, rows_dev):
    total = count[0]
    for k in range(1, rows_dev):
        total = total + count[k]
    return total


def pack_kernel(
    pattern, count, x, send, slots, sums, held, sem_x, sems, *, rows_dev, devices, entries, block_total
):
    live = live_count(count, rows_dev)
    position = divide(pattern[0, 0], rows_dev)
    base = position * rows_dev

    def key(e):
        i = pattern[0, e]
        j = pattern[1, e]
        return jnp.minimum(i, j) * block_total + jnp.maximum(i, j)

    def copy(e):
        return pltpu.make_async_copy(held.at[pattern[0, e] - base], send.at[slots[e]], sems.at[e])

    fetch = pltpu.make_async_copy(x, held, sem_x.at[0])
    fetch.start()
    spare = pltpu.make_async_copy(held.at[0], send.at[position * SLOTS], sems.at[entries])
    for o in range(devices):
        sums[o] = 0
    for e in range(entries):
        owner = divide(pattern[1, e], rows_dev)
        sums[owner] = sums[owner] + key(e)
    for e in range(entries):
        owner = divide(pattern[1, e], rows_dev)
        later = jnp.where((2 * key(e) > sums[owner]) & (e < live), 1, 0)
        slots[e] = owner * SLOTS + later

    def begin(e, carry):
        copy(e).start()
        return carry

    def finish(e, carry):
        copy(e).wait()
        return carry

    fetch.wait()
    spare.start()
    lax.fori_loop(0, live, begin, 0)
    spare.wait()
    lax.fori_loop(0, live, finish, 0)


def own_kernel(count, x, omega, off, projected, logs, wide, *, rows_dev, entries, edge):
    live = live_count(count, rows_dev)
    on_diagonal = lax.broadcasted_iota(jnp.int32, (edge, edge), 0) == lax.broadcasted_iota(
        jnp.int32, (edge, edge), 1
    )
    total = jnp.zeros((1, edge), jnp.float32)
    for k in range(rows_dev):
        block = omega[k]
        high, low = split_halves(block)
        rows = x[k]
        projected[k] = jnp.dot(
            jnp.concatenate([high, low], axis=1),
            jnp.concatenate([rows, rows], axis=0),
            preferred_element_type=jnp.float32,
        )
        total = total + jnp.log(jnp.sum(jnp.where(on_diagonal, block, 0.0), axis=0, keepdims=True))
    logs[...] = jnp.broadcast_to(total, logs.shape)

    def widen(e, carry):
        high, low = split_halves(jnp.where(e < live, off[e], 0.0))
        wide[e, :, :edge] = high
        wide[e, :, edge:] = low
        return carry

    lax.fori_loop(0, entries, widen, 0)


def main_kernel(
    pattern,
    count,
    slots,
    logs,
    arrived,
    own,
    wide,
    payload,
    projected,
    held_wide,
    held_own,
    held_rows,
    halves,
    coded,
    stats,
    tail,
    sem_wide,
    sem_own,
    sem_rows,
    sem_code,
    *,
    rows_dev,
    devices,
    entries,
    edge,
    samples_dev,
):
    live = live_count(count, rows_dev)
    base = divide(pattern[0, 0], rows_dev) * rows_dev
    fetches = []
    for at, (start, size) in enumerate(parts_of(entries, True)):
        part = pl.ds(start, size)
        fetches.append(pltpu.make_async_copy(wide.at[part], held_wide.at[part], sem_wide.at[at]))
        fetches[-1].start()
    fetch_own = pltpu.make_async_copy(own, held_own, sem_own.at[0])
    fetch_own.start()
    held_rows[...] = jnp.zeros(held_rows.shape, jnp.float32)
    stats[...] = jnp.zeros(stats.shape, jnp.float32)

    for at, (start, size) in enumerate(parts_of(entries, True)):
        fetches[at].wait()
        for e in range(start, start + size):
            rows = arrived[slots[e]]
            part = jnp.dot(
                held_wide[e],
                jnp.concatenate([rows, rows], axis=0),
                preferred_element_type=jnp.float32,
            )
            row = pattern[0, e] - base
            held_rows[row] = held_rows[row] + part

    fetch_own.wait()
    squares = jnp.zeros((8, samples_dev), jnp.float32)
    for k in range(rows_dev):
        values = held_rows[k] + held_own[k]
        held_own[k] = values
        squares = squares + jnp.sum((values * values).reshape(edge // 8, 8, samples_dev), axis=0)
        high, low = split_halves(values)
        halves[k, :edge] = high
        halves[k, edge:] = low
    store_rows = pltpu.make_async_copy(held_own, projected, sem_rows.at[0])
    store_rows.start()

    def store(e):
        slot = slots[e]
        owner = divide(slot, SLOTS)
        rank = slot - owner * SLOTS
        return pltpu.make_async_copy(
            coded.at[e],
            payload.at[owner, pl.ds(pl.multiple_of(rank * edge, edge), edge), :],
            sem_code.at[e],
        )

    for start, size in parts_of(entries, False):
        for e in range(start, start + size):
            row = pattern[0, e] - base
            slot = slots[e]
            both = lax.dot_general(
                arrived[slot],
                halves[row],
                (((1,), (1,)), ((), ())),
                preferred_element_type=jnp.float32,
            )
            product = both[:, :edge] + both[:, edge:]
            largest = jnp.maximum(jnp.max(jnp.abs(product), axis=0, keepdims=True), 1e-30)
            code = jnp.ceil(jnp.log2(largest) * LOG_STEPS + 0.01)
            scaled = product * jnp.exp2(15.0 - HEADROOM - code * (1.0 / LOG_STEPS))
            owner = divide(slot, SLOTS)
            rank = slot - owner * SLOTS
            coded[e] = jnp.round(scaled).astype(jnp.int32).astype(jnp.int16)
            stats[owner, pl.ds(rank, 1), :] = code

        def begin(e, carry):
            store(e).start()
            return carry

        lax.fori_loop(start, jnp.clip(live, start, start + size), begin, 0)

    term = jnp.sum(squares) * (1.0 / (2.0 * samples_dev)) - jnp.sum(logs[0:1, :])
    term = jnp.full((1, edge), term, jnp.float32)
    power = jnp.ceil(jnp.log2(jnp.maximum(jnp.abs(term), 1e-30)) + 0.01)
    scaled = term * jnp.exp2(14.0 - power)
    whole = jnp.round(scaled)
    digits = jnp.concatenate(
        [
            jnp.zeros((SLOTS, edge), jnp.float32),
            power,
            whole,
            jnp.round((scaled - whole) * FRACTION),
            jnp.zeros((STAT_ROWS - SLOTS - 3, edge), jnp.float32),
        ],
        axis=0,
    )
    tail[...] = (stats[...] + digits[None]).astype(jnp.int32).astype(jnp.int16)
    store_tail = pltpu.make_async_copy(
        tail, payload.at[:, pl.ds(SLOTS * edge, STAT_ROWS), :], sem_code.at[entries]
    )
    store_tail.start()

    def finish(e, carry):
        store(e).wait()
        return carry

    lax.fori_loop(0, live, finish, 0)
    store_rows.wait()
    store_tail.wait()


def side_kernel(
    pattern,
    count,
    slots,
    x,
    omega,
    term,
    projected,
    off,
    arrived,
    result,
    moved,
    halves,
    *,
    rows_dev,
    entries,
    edge,
    samples_dev,
):
    live = live_count(count, rows_dev)
    base = divide(pattern[0, 0], rows_dev) * rows_dev
    on_diagonal = lax.broadcasted_iota(jnp.int32, (edge, edge), 0) == lax.broadcasted_iota(
        jnp.int32, (edge, edge), 1
    )

    def against(row, other):
        both = lax.dot_general(
            halves[row], other, (((1,), (1,)), ((), ())), preferred_element_type=jnp.float32
        )
        return both[:edge] + both[edge:]

    for k in range(rows_dev):
        high, low = split_halves(projected[k])
        halves[k, :edge] = high
        halves[k, edge:] = low
        product = against(k, x[k])
        gradient = (product + product.T) * (1.0 / (2.0 * samples_dev))
        gradient = gradient + jnp.where(on_diagonal, term[k : k + 1, :], 0.0)
        value = omega[k] - STEP_SIZE * gradient
        result[k] = jnp.where(on_diagonal, value, soften(value, STEP_SIZE * PENALTY))

    def move(e, carry):
        product = against(pattern[0, e] - base, arrived[slots[e]])
        value = off[e] - product * (STEP_SIZE / (2.0 * samples_dev))
        moved[e] = jnp.where(e < live, value, 0.0)
        return carry

    lax.fori_loop(0, entries, move, 0)


def last_kernel(
    count,
    slots,
    moved,
    returned,
    result,
    objective,
    held,
    rt,
    rs,
    sem_in,
    sem_rt,
    sem_out,
    *,
    rows_dev,
    devices,
    entries,
    edge,
    samples_dev,
):
    live = live_count(count, rows_dev)

    def fetch(at, part):
        return pltpu.make_async_copy(moved.at[part], held.at[part], sem_in.at[at])

    def store(at, part):
        return pltpu.make_async_copy(rs.at[part], result.at[part], sem_out.at[at])

    width = max(k for k in range(1, 11) if entries % k == 0)
    parts = [(at, pl.ds(at * width, width)) for at in range(entries // width)]
    whole = pltpu.make_async_copy(returned, rt, sem_rt.at[0])
    whole.start()
    for at, part in parts:
        fetch(at, part).start()
    whole.wait()
    codes = rt[:, SLOTS * edge :, :].astype(jnp.int32).astype(jnp.float32)
    power = codes[:, SLOTS : SLOTS + 1]
    digits = codes[:, SLOTS + 1 : SLOTS + 2] + codes[:, SLOTS + 2 : SLOTS + 3] * (1.0 / FRACTION)
    total = jnp.sum(digits * jnp.exp2(power - 14.0), axis=0)
    objective[0] = jnp.max(total) * (1.0 / (devices * rows_dev * edge))
    for at, part in parts:
        fetch(at, part).wait()
        for e in range(at * width, (at + 1) * width):
            slot = slots[e]
            owner = divide(slot, SLOTS)
            rank = slot - owner * SLOTS
            codes = rt[owner, SLOTS * edge :, :].astype(jnp.int32).astype(jnp.float32)
            code = jnp.where(rank == 0, codes[0:1], codes[1:2])
            weight = jnp.exp2(code * (1.0 / LOG_STEPS) - (15.0 - HEADROOM)) * (
                STEP_SIZE / (2.0 * samples_dev)
            )
            weight = jnp.where(e < live, weight, 0.0)
            digits = rt[owner, pl.ds(pl.multiple_of(rank * edge, edge), edge), :]
            value = held[e] - digits.astype(jnp.int32).astype(jnp.float32) * weight
            rs[e] = soften(value, STEP_SIZE * PENALTY)
        store(at, part).start()
    for at, part in parts:
        store(at, part).wait()


def shards(samples, omega_diag, omega_off, pattern, block_count, diag_term):
    devices = lax.axis_size("rows")
    rows_dev, edge = omega_diag.shape[:2]
    samples_dev = samples.shape[1]
    entries = omega_off.shape[0]
    capacity = devices * SLOTS
    f32 = jnp.float32
    x = samples.reshape(rows_dev, edge, samples_dev)
    term = diag_term.reshape(rows_dev, edge)
    pattern = pattern.T
    smem = pl.BlockSpec(memory_space=pltpu.SMEM)
    vmem = pl.BlockSpec(memory_space=pltpu.VMEM)
    hbm = pl.BlockSpec(memory_space=pltpu.HBM)
    params = pltpu.CompilerParams(vmem_limit_bytes=VMEM_LIMIT)
    alone = pltpu.CompilerParams(vmem_limit_bytes=VMEM_ALONE)
    sizes = dict(rows_dev=rows_dev, entries=entries, edge=edge)
    every = dict(sizes, devices=devices, samples_dev=samples_dev)
    held = functools.partial(pltpu.with_memory_space_constraint, memory_space=pltpu.VMEM)
    kept = functools.partial(pltpu.with_memory_space_constraint, memory_space=pltpu.HBM)

    dma = pltpu.SemaphoreType.DMA

    send, slots = pl.pallas_call(
        functools.partial(
            pack_kernel,
            rows_dev=rows_dev,
            devices=devices,
            entries=entries,
            block_total=rows_dev * devices,
        ),
        out_shape=(
            jax.ShapeDtypeStruct((capacity, edge, samples_dev), samples.dtype),
            jax.ShapeDtypeStruct((entries,), jnp.int32),
        ),
        in_specs=[smem, smem, hbm],
        out_specs=(hbm, smem),
        scratch_shapes=[
            pltpu.SMEM((devices,), jnp.int32),
            pltpu.VMEM((rows_dev, edge, samples_dev), samples.dtype),
            dma((1,)),
            dma((entries + 1,)),
        ],
        compiler_params=alone,
        name="pack",
    )(pattern, block_count, x)

    arrived = lax.all_to_all(
        send.reshape(devices, SLOTS, edge, samples_dev),
        "rows",
        split_axis=0,
        concat_axis=0,
        tiled=True,
    ).reshape(capacity, edge, samples_dev)

    own, logs, wide = pl.pallas_call(
        functools.partial(own_kernel, **sizes),
        out_shape=(
            pltpu.HBM((rows_dev, edge, samples_dev), f32),
            jax.ShapeDtypeStruct((8, edge), f32),
            pltpu.HBM((entries, edge, 2 * edge), jnp.bfloat16),
        ),
        in_specs=[smem, vmem, vmem, vmem],
        out_specs=(vmem, vmem, vmem),
        compiler_params=params,
        cost_estimate=pl.CostEstimate(
            flops=4 * rows_dev * edge * edge * samples_dev, transcendentals=0, bytes_accessed=1 << 23
        ),
        name="own",
    )(block_count, x, omega_diag, omega_off)

    payload, projected = pl.pallas_call(
        functools.partial(main_kernel, **every),
        out_shape=(
            pltpu.HBM((devices, SLOTS * edge + STAT_ROWS, edge), jnp.int16),
            pltpu.HBM((rows_dev, edge, samples_dev), f32),
        ),
        in_specs=[smem, smem, smem, vmem, vmem, hbm, hbm],
        out_specs=(hbm, hbm),
        scratch_shapes=[
            pltpu.VMEM((entries, edge, 2 * edge), jnp.bfloat16),
            pltpu.VMEM((rows_dev, edge, samples_dev), f32),
            pltpu.VMEM((rows_dev, edge, samples_dev), f32),
            pltpu.VMEM((rows_dev, 2 * edge, samples_dev), jnp.bfloat16),
            pltpu.VMEM((entries, edge, edge), jnp.int16),
            pltpu.VMEM((devices, STAT_ROWS, edge), f32),
            pltpu.VMEM((devices, STAT_ROWS, edge), jnp.int16),
            dma((2,)),
            dma((1,)),
            dma((1,)),
            dma((entries + 1,)),
        ],
        compiler_params=params,
        name="main",
    )(pattern, block_count, slots, logs, held(arrived), kept(own), kept(wide))

    returned = lax.all_to_all(kept(payload), "rows", split_axis=0, concat_axis=0, tiled=True)

    diag_next, moved = pl.pallas_call(
        functools.partial(side_kernel, samples_dev=samples_dev, **sizes),
        out_shape=(
            jax.ShapeDtypeStruct((rows_dev, edge, edge), f32),
            pltpu.HBM((entries, edge, edge), f32),
        ),
        in_specs=[smem] * 3 + [vmem] * 6,
        out_specs=(vmem, vmem),
        scratch_shapes=[pltpu.VMEM((rows_dev, 2 * edge, samples_dev), jnp.bfloat16)],
        compiler_params=params,
        cost_estimate=pl.CostEstimate(
            flops=4 * rows_dev * edge * edge * samples_dev, transcendentals=0, bytes_accessed=1 << 23
        ),
        name="side",
    )(pattern, block_count, slots, x, omega_diag, term, projected, omega_off, arrived)

    off_next, objective = pl.pallas_call(
        functools.partial(last_kernel, **every),
        out_shape=(
            jax.ShapeDtypeStruct((entries, edge, edge), f32),
            jax.ShapeDtypeStruct((1,), f32),
        ),
        in_specs=[smem, smem, hbm, hbm],
        out_specs=(hbm, smem),
        scratch_shapes=[
            pltpu.VMEM((entries, edge, edge), f32),
            pltpu.VMEM((devices, SLOTS * edge + STAT_ROWS, edge), jnp.int16),
            pltpu.VMEM((entries, edge, edge), f32),
            dma((entries,)),
            dma((1,)),
            dma((entries,)),
        ],
        compiler_params=alone,
        name="last",
    )(block_count, slots, kept(moved), kept(returned))
    return diag_next, off_next, objective


def solution(mesh):
    return jax.shard_map(
        shards,
        mesh=mesh,
        in_specs=(
            P(("groups", "rows"), None),
            P(("groups", "rows"), None, None),
            P(("groups", "rows"), None, None),
            P(("groups", "rows"), None),
            P(("groups", "rows")),
            P(("groups", "rows")),
        ),
        out_specs=(
            P(("groups", "rows"), None, None),
            P(("groups", "rows"), None, None),
            P("groups"),
        ),
        check_vma=False,
    )
```

```python
import functools

import jax
import jax.numpy as jnp
from jax import lax
from jax.experimental import pallas as pl
from jax.experimental.pallas import tpu as pltpu
from jax.sharding import PartitionSpec as P


SLOTS = 2
STAT_ROWS = 8
STEP_SIZE = 0.5
PENALTY = 0.01
LOG_STEPS = 128.0
HEADROOM = 1e-4
FRACTION = 32000.0
VMEM_LIMIT = 40 * 1024 * 1024
VMEM_ALONE = 60 * 1024 * 1024


def soften(values, level):
    return values - jnp.clip(values, -level, level)


def split_halves(values):
    high = values.astype(jnp.bfloat16)
    low = (values - high.astype(jnp.float32)).astype(jnp.bfloat16)
    return high, low


def divide(value, by):
    if by & (by - 1):
        return value // by
    return lax.shift_right_logical(value, by.bit_length() - 1)


def limits(entries, devices):
    half = devices // 2
    return min(entries, SLOTS * half), min(entries, SLOTS * (half - 1))


def live_count(count, rows_dev):
    total = count[0]
    for k in range(1, rows_dev):
        total = total + count[k]
    return total


def pack_kernel(
    pattern,
    count,
    x,
    send,
    slots,
    lists,
    wanted,
    sums,
    keys,
    held,
    sem_x,
    sems,
    *,
    rows_dev,
    devices,
    entries,
    block_total,
):
    live = live_count(count, rows_dev)
    half = devices // 2
    far_limit, near_limit = limits(entries, devices)
    position = divide(pattern[0, 0], rows_dev)
    base = position * rows_dev
    side = divide(position, half)
    spot = (position - side * half) * SLOTS

    fetch = pltpu.make_async_copy(x, held, sem_x.at[0])
    fetch.start()
    spare = pltpu.make_async_copy(held.at[0], send.at[spot], sems.at[near_limit])
    for o in range(devices):
        sums[o] = 0
    for q in range(SLOTS * half):
        wanted[q] = 0
    for k in range(far_limit + near_limit):
        lists[0, k] = entries
        lists[1, k] = rows_dev
        lists[2, k] = spot if k >= far_limit else 0
        lists[3, k] = position * SLOTS
    for e in range(entries):
        i = pattern[0, e]
        j = pattern[1, e]
        owner = divide(j, rows_dev)
        key = jnp.minimum(i * block_total + j, j * block_total + i)
        keys[e] = key
        sums[owner] = sums[owner] + key
    fars = jnp.int32(0)
    nears = jnp.int32(far_limit)
    for e in range(entries):
        row = pattern[0, e] - base
        owner = divide(pattern[1, e], rows_dev)
        alive = e < live
        later = jnp.where((2 * keys[e] > sums[owner]) & alive, 1, 0)
        slot = owner * SLOTS + later
        slots[e] = slot
        away = divide(owner, half)
        place = slot - away * (SLOTS * half)
        near = away == side
        wanted[jnp.where(alive & ~near, place, SLOTS * half)] = row
        at = jnp.where(alive, jnp.where(near, nears, fars), far_limit + near_limit)
        lists[0, at] = e
        lists[1, at] = row
        lists[2, at] = place
        lists[3, at] = slot
        fars = fars + jnp.where(alive & ~near, 1, 0)
        nears = nears + jnp.where(alive & near, 1, 0)

    def copy(k):
        return pltpu.make_async_copy(
            held.at[lists[1, k]], send.at[lists[2, k]], sems.at[k - far_limit]
        )

    def begin(k, carry):
        copy(k).start()
        return carry

    def finish(k, carry):
        copy(k).wait()
        return carry

    fetch.wait()
    spare.start()
    lax.fori_loop(far_limit, nears, begin, 0)
    lists[0, far_limit + near_limit + 1] = fars
    lists[0, far_limit + near_limit + 2] = nears
    spare.wait()
    lax.fori_loop(far_limit, nears, finish, 0)


def relay_kernel(wanted, x, send, sems, *, devices):
    copies = [
        pltpu.make_async_copy(x.at[wanted[q]], send.at[q], sems.at[q])
        for q in range(SLOTS * (devices // 2))
    ]
    for copy in copies:
        copy.start()
    for copy in copies:
        copy.wait()


def own_kernel(lists, x, omega, off, near, projected, logs, wide, *, rows_dev, devices, entries, edge):
    far_limit, near_limit = limits(entries, devices)
    on_diagonal = lax.broadcasted_iota(jnp.int32, (edge, edge), 0) == lax.broadcasted_iota(
        jnp.int32, (edge, edge), 1
    )

    def apply(block, rows):
        high, low = split_halves(block)
        return jnp.dot(
            jnp.concatenate([high, low], axis=1),
            jnp.concatenate([rows, rows], axis=0),
            preferred_element_type=jnp.float32,
        )

    total = jnp.zeros((1, edge), jnp.float32)
    for k in range(rows_dev):
        projected[k] = apply(omega[k], x[k])
        total = total + jnp.log(
            jnp.sum(jnp.where(on_diagonal, omega[k], 0.0), axis=0, keepdims=True)
        )
    projected[rows_dev] = jnp.zeros(projected.shape[1:], jnp.float32)
    logs[...] = jnp.broadcast_to(total, logs.shape)

    def add(k, carry):
        row = lists[1, k]
        block = off[jnp.minimum(lists[0, k], entries - 1)]
        projected[row] = projected[row] + apply(block, near[lists[2, k]])
        return carry

    lax.fori_loop(far_limit, far_limit + near_limit, add, 0)

    def widen(k, carry):
        high, low = split_halves(off[jnp.minimum(lists[0, k], entries - 1)])
        wide[k, :, :edge] = high
        wide[k, :, edge:] = low
        return carry

    lax.fori_loop(0, far_limit, widen, 0)


def main_kernel(
    lists,
    logs,
    far,
    near,
    own,
    wide,
    payload,
    projected,
    held_near,
    held_wide,
    held_own,
    held_rows,
    halves,
    coded,
    stats,
    tail,
    sem_near,
    sem_wide,
    sem_own,
    sem_rows,
    sem_code,
    *,
    rows_dev,
    devices,
    entries,
    edge,
    samples_dev,
):
    far_limit, near_limit = limits(entries, devices)
    limit = far_limit + near_limit
    split = far_limit // 4
    parts = (pl.ds(0, split), pl.ds(split, far_limit - split))
    fetches = [
        pltpu.make_async_copy(wide.at[part], held_wide.at[part], sem_wide.at[at])
        for at, part in enumerate(parts)
    ]
    fetch_own = pltpu.make_async_copy(own.at[pl.ds(0, rows_dev)], held_own, sem_own.at[0])
    fetch_near = pltpu.make_async_copy(near, held_near, sem_near.at[0])
    for fetch in (*fetches, fetch_own, fetch_near):
        fetch.start()
    held_rows[...] = jnp.zeros(held_rows.shape, jnp.float32)
    stats[...] = jnp.zeros(stats.shape, jnp.float32)
    halves[rows_dev] = jnp.zeros(halves.shape[1:], halves.dtype)

    total = jnp.zeros((edge, samples_dev), jnp.float32)
    for k in range(far_limit):
        if k == 0:
            fetches[0].wait()
        if k == split:
            fetches[1].wait()
        rows = far[lists[2, k]]
        part = jnp.dot(
            held_wide[k],
            jnp.concatenate([rows, rows], axis=0),
            preferred_element_type=jnp.float32,
        )
        row = lists[1, k]
        total = part if k == 0 else jnp.where(row == lists[1, k - 1], total, 0.0) + part
        held_rows[row] = total

    fetch_own.wait()
    squares = jnp.zeros((8, samples_dev), jnp.float32)
    for k in range(rows_dev):
        values = held_rows[k] + held_own[k]
        held_own[k] = values
        squares = squares + jnp.sum((values * values).reshape(edge // 8, 8, samples_dev), axis=0)
        high, low = split_halves(values)
        halves[k, :edge] = high
        halves[k, edge:] = low
    store_rows = pltpu.make_async_copy(held_own, projected, sem_rows.at[0])
    store_rows.start()
    fetch_near.wait()

    def store(k):
        slot = lists[3, k]
        owner = divide(slot, SLOTS)
        rank = slot - owner * SLOTS
        return pltpu.make_async_copy(
            coded.at[k],
            payload.at[owner, pl.ds(pl.multiple_of(rank * edge, edge), edge), :],
            sem_code.at[k],
        )

    def begin(k, carry):
        store(k).start()
        return carry

    def finish(k, carry):
        store(k).wait()
        return carry

    def encode(k, rows):
        slot = lists[3, k]
        both = lax.dot_general(
            rows,
            halves[lists[1, k]],
            (((1,), (1,)), ((), ())),
            preferred_element_type=jnp.float32,
        )
        product = both[:, :edge] + both[:, edge:]
        largest = jnp.maximum(jnp.max(jnp.abs(product), axis=0, keepdims=True), 1e-30)
        code = jnp.ceil(jnp.log2(largest) * LOG_STEPS + 0.01)
        scaled = product * jnp.exp2(15.0 - HEADROOM - code * (1.0 / LOG_STEPS))
        owner = divide(slot, SLOTS)
        coded[k] = jnp.round(scaled).astype(jnp.int32).astype(jnp.int16)
        stats[owner, pl.ds(slot - owner * SLOTS, 1), :] = code

    fars = lists[0, limit + 1]
    nears = lists[0, limit + 2]
    for k in range(far_limit):
        encode(k, far[lists[2, k]])
    lax.fori_loop(0, fars, begin, 0)
    for k in range(far_limit, limit):
        encode(k, held_near[lists[2, k]])
    lax.fori_loop(far_limit, nears, begin, 0)

    term = jnp.sum(squares) * (1.0 / (2.0 * samples_dev)) - jnp.sum(logs[0:1, :])
    term = jnp.full((1, edge), term, jnp.float32)
    power = jnp.ceil(jnp.log2(jnp.maximum(jnp.abs(term), 1e-30)) + 0.01)
    scaled = term * jnp.exp2(14.0 - power)
    whole = jnp.round(scaled)
    digits = jnp.concatenate(
        [
            jnp.zeros((SLOTS, edge), jnp.float32),
            power,
            whole,
            jnp.round((scaled - whole) * FRACTION),
            jnp.zeros((STAT_ROWS - SLOTS - 3, edge), jnp.float32),
        ],
        axis=0,
    )
    tail[...] = (stats[...] + digits[None]).astype(jnp.int32).astype(jnp.int16)
    store_tail = pltpu.make_async_copy(
        tail, payload.at[:, pl.ds(SLOTS * edge, STAT_ROWS), :], sem_code.at[limit]
    )
    store_tail.start()
    lax.fori_loop(0, fars, finish, 0)
    lax.fori_loop(far_limit, nears, finish, 0)
    store_rows.wait()
    store_tail.wait()


def side_kernel(
    lists,
    x,
    omega,
    term,
    projected,
    off,
    far,
    near,
    result,
    moved,
    halves,
    *,
    rows_dev,
    devices,
    entries,
    edge,
    samples_dev,
):
    far_limit, near_limit = limits(entries, devices)
    on_diagonal = lax.broadcasted_iota(jnp.int32, (edge, edge), 0) == lax.broadcasted_iota(
        jnp.int32, (edge, edge), 1
    )

    def against(row, other):
        both = lax.dot_general(
            halves[row], other, (((1,), (1,)), ((), ())), preferred_element_type=jnp.float32
        )
        return both[:edge] + both[edge:]

    moved[...] = jnp.zeros(moved.shape, jnp.float32)
    halves[rows_dev] = jnp.zeros(halves.shape[1:], halves.dtype)
    for k in range(rows_dev):
        high, low = split_halves(projected[k])
        halves[k, :edge] = high
        halves[k, edge:] = low
        product = against(k, x[k])
        gradient = (product + product.T) * (1.0 / (2.0 * samples_dev))
        gradient = gradient + jnp.where(on_diagonal, term[k : k + 1, :], 0.0)
        value = omega[k] - STEP_SIZE * gradient
        result[k] = jnp.where(on_diagonal, value, soften(value, STEP_SIZE * PENALTY))

    def move(source, k, carry):
        e = lists[0, k]
        product = against(lists[1, k], source[lists[2, k]])
        moved[e] = off[jnp.minimum(e, entries - 1)] - product * (STEP_SIZE / (2.0 * samples_dev))
        return carry

    lax.fori_loop(0, far_limit, functools.partial(move, far), 0)
    lax.fori_loop(far_limit, far_limit + near_limit, functools.partial(move, near), 0)


def last_kernel(
    count,
    slots,
    moved,
    returned,
    result,
    objective,
    held,
    rt,
    rs,
    sem_in,
    sem_rt,
    sem_out,
    *,
    rows_dev,
    devices,
    entries,
    edge,
    samples_dev,
):
    live = live_count(count, rows_dev)

    def fetch(at, part):
        return pltpu.make_async_copy(moved.at[part], held.at[part], sem_in.at[at])

    def store(at, part):
        return pltpu.make_async_copy(rs.at[part], result.at[part], sem_out.at[at])

    width = max(k for k in range(1, 11) if entries % k == 0)
    parts = [(at, pl.ds(at * width, width)) for at in range(entries // width)]
    whole = pltpu.make_async_copy(returned, rt, sem_rt.at[0])
    whole.start()
    for at, part in parts:
        fetch(at, part).start()
    whole.wait()
    codes = rt[:, SLOTS * edge :, :].astype(jnp.int32).astype(jnp.float32)
    power = codes[:, SLOTS : SLOTS + 1]
    digits = codes[:, SLOTS + 1 : SLOTS + 2] + codes[:, SLOTS + 2 : SLOTS + 3] * (1.0 / FRACTION)
    total = jnp.sum(digits * jnp.exp2(power - 14.0), axis=0)
    objective[0] = jnp.max(total) * (1.0 / (devices * rows_dev * edge))
    for at, part in parts:
        fetch(at, part).wait()
        for e in range(at * width, (at + 1) * width):
            slot = slots[e]
            owner = divide(slot, SLOTS)
            rank = slot - owner * SLOTS
            codes = rt[owner, SLOTS * edge :, :].astype(jnp.int32).astype(jnp.float32)
            code = jnp.where(rank == 0, codes[0:1], codes[1:2])
            weight = jnp.exp2(code * (1.0 / LOG_STEPS) - (15.0 - HEADROOM)) * (
                STEP_SIZE / (2.0 * samples_dev)
            )
            weight = jnp.where(e < live, weight, 0.0)
            digits = rt[owner, pl.ds(pl.multiple_of(rank * edge, edge), edge), :]
            value = held[e] - digits.astype(jnp.int32).astype(jnp.float32) * weight
            rs[e] = soften(value, STEP_SIZE * PENALTY)
        store(at, part).start()
    for at, part in parts:
        store(at, part).wait()


def shards(samples, omega_diag, omega_off, pattern, block_count, diag_term):
    devices = lax.axis_size("rows")
    rows_dev, edge = omega_diag.shape[:2]
    samples_dev = samples.shape[1]
    entries = omega_off.shape[0]
    f32 = jnp.float32
    x = samples.reshape(rows_dev, edge, samples_dev)
    term = diag_term.reshape(rows_dev, edge)
    pattern = pattern.T
    smem = pl.BlockSpec(memory_space=pltpu.SMEM)
    vmem = pl.BlockSpec(memory_space=pltpu.VMEM)
    hbm = pl.BlockSpec(memory_space=pltpu.HBM)
    params = pltpu.CompilerParams(vmem_limit_bytes=VMEM_LIMIT)
    alone = pltpu.CompilerParams(vmem_limit_bytes=VMEM_ALONE)
    sizes = dict(rows_dev=rows_dev, entries=entries, edge=edge)
    every = dict(sizes, devices=devices, samples_dev=samples_dev)
    held = functools.partial(pltpu.with_memory_space_constraint, memory_space=pltpu.VMEM)
    kept = functools.partial(pltpu.with_memory_space_constraint, memory_space=pltpu.HBM)

    dma = pltpu.SemaphoreType.DMA

    half = devices // 2
    far_limit, near_limit = limits(entries, devices)
    limit = far_limit + near_limit
    across = [(o, (o + half) % devices) for o in range(devices)]
    halves = [list(range(half)), list(range(half, devices))]

    other = lax.ppermute(kept(x), "rows", across)

    send, slots, lists, wanted = pl.pallas_call(
        functools.partial(
            pack_kernel,
            rows_dev=rows_dev,
            devices=devices,
            entries=entries,
            block_total=rows_dev * devices,
        ),
        out_shape=(
            pltpu.HBM((SLOTS * half, edge, samples_dev), samples.dtype),
            jax.ShapeDtypeStruct((entries,), jnp.int32),
            jax.ShapeDtypeStruct((4, limit + 3), jnp.int32),
            jax.ShapeDtypeStruct((SLOTS * half + 1,), jnp.int32),
        ),
        in_specs=[smem, smem, hbm],
        out_specs=(hbm, smem, smem, smem),
        scratch_shapes=[
            pltpu.SMEM((devices,), jnp.int32),
            pltpu.SMEM((entries,), jnp.int32),
            pltpu.VMEM((rows_dev, edge, samples_dev), samples.dtype),
            dma((1,)),
            dma((near_limit + 1,)),
        ],
        compiler_params=params,
        name="pack",
    )(pattern, block_count, kept(x))

    def within(blocks):
        return lax.all_to_all(
            blocks.reshape(half, SLOTS, edge, samples_dev),
            "rows",
            split_axis=0,
            concat_axis=0,
            axis_index_groups=halves,
            tiled=True,
        ).reshape(SLOTS * half, edge, samples_dev)

    wanted = lax.ppermute(wanted, "rows", across)
    near = within(send)

    passed = pl.pallas_call(
        functools.partial(relay_kernel, devices=devices),
        out_shape=pltpu.HBM((SLOTS * half, edge, samples_dev), samples.dtype),
        in_specs=[smem, vmem],
        out_specs=hbm,
        scratch_shapes=[dma((SLOTS * half,))],
        compiler_params=params,
        name="relay",
    )(wanted, held(other))
    far = within(passed)

    own, logs, wide = pl.pallas_call(
        functools.partial(own_kernel, devices=devices, **sizes),
        out_shape=(
            pltpu.HBM((rows_dev + 1, edge, samples_dev), f32),
            jax.ShapeDtypeStruct((8, edge), f32),
            pltpu.HBM((far_limit, edge, 2 * edge), jnp.bfloat16),
        ),
        in_specs=[smem] + [vmem] * 4,
        out_specs=(vmem, vmem, vmem),
        compiler_params=params,
        cost_estimate=pl.CostEstimate(
            flops=12 * rows_dev * edge * edge * samples_dev, transcendentals=0, bytes_accessed=1 << 23
        ),
        name="own",
    )(lists, x, omega_diag, omega_off, near)

    payload, projected = pl.pallas_call(
        functools.partial(main_kernel, **every),
        out_shape=(
            pltpu.HBM((devices, SLOTS * edge + STAT_ROWS, edge), jnp.int16),
            pltpu.HBM((rows_dev, edge, samples_dev), f32),
        ),
        in_specs=[smem, vmem, vmem, hbm, hbm, hbm],
        out_specs=(hbm, hbm),
        scratch_shapes=[
            pltpu.VMEM((SLOTS * half, edge, samples_dev), samples.dtype),
            pltpu.VMEM((far_limit, edge, 2 * edge), jnp.bfloat16),
            pltpu.VMEM((rows_dev, edge, samples_dev), f32),
            pltpu.VMEM((rows_dev + 1, edge, samples_dev), f32),
            pltpu.VMEM((rows_dev + 1, 2 * edge, samples_dev), jnp.bfloat16),
            pltpu.VMEM((limit, edge, edge), jnp.int16),
            pltpu.VMEM((devices, STAT_ROWS, edge), f32),
            pltpu.VMEM((devices, STAT_ROWS, edge), jnp.int16),
            dma((1,)),
            dma((2,)),
            dma((1,)),
            dma((1,)),
            dma((limit + 1,)),
        ],
        compiler_params=params,
        name="main",
    )(lists, logs, held(far), kept(near), kept(own), kept(wide))

    returned = lax.all_to_all(kept(payload), "rows", split_axis=0, concat_axis=0, tiled=True)

    diag_next, moved = pl.pallas_call(
        functools.partial(side_kernel, **every),
        out_shape=(
            jax.ShapeDtypeStruct((rows_dev, edge, edge), f32),
            pltpu.HBM((entries + 1, edge, edge), f32),
        ),
        in_specs=[smem] + [vmem] * 7,
        out_specs=(vmem, vmem),
        scratch_shapes=[pltpu.VMEM((rows_dev + 1, 2 * edge, samples_dev), jnp.bfloat16)],
        compiler_params=params,
        cost_estimate=pl.CostEstimate(
            flops=12 * rows_dev * edge * edge * samples_dev, transcendentals=0, bytes_accessed=1 << 23
        ),
        name="side",
    )(lists, x, omega_diag, term, projected, omega_off, far, near)

    off_next, objective = pl.pallas_call(
        functools.partial(last_kernel, **every),
        out_shape=(
            jax.ShapeDtypeStruct((entries, edge, edge), f32),
            jax.ShapeDtypeStruct((1,), f32),
        ),
        in_specs=[smem, smem, hbm, hbm],
        out_specs=(hbm, smem),
        scratch_shapes=[
            pltpu.VMEM((entries, edge, edge), f32),
            pltpu.VMEM((devices, SLOTS * edge + STAT_ROWS, edge), jnp.int16),
            pltpu.VMEM((entries, edge, edge), f32),
            dma((entries,)),
            dma((1,)),
            dma((entries,)),
        ],
        compiler_params=alone,
        name="last",
    )(block_count, slots, kept(moved), kept(returned))
    return diag_next, off_next, objective


def solution(mesh):
    return jax.shard_map(
        shards,
        mesh=mesh,
        in_specs=(
            P(("groups", "rows"), None),
            P(("groups", "rows"), None, None),
            P(("groups", "rows"), None, None),
            P(("groups", "rows"), None),
            P(("groups", "rows")),
            P(("groups", "rows")),
        ),
        out_specs=(
            P(("groups", "rows"), None, None),
            P(("groups", "rows"), None, None),
            P("groups"),
        ),
        check_vma=False,
    )
```

```python
import functools

import jax
import jax.numpy as jnp
from jax import lax
from jax.experimental import pallas as pl
from jax.experimental.pallas import tpu as pltpu
from jax.sharding import PartitionSpec as P


SLOTS = 2
STAT_ROWS = 8
STEP_SIZE = 0.5
PENALTY = 0.01
LOG_STEPS = 128.0
HEADROOM = 1e-4
FRACTION = 32000.0
VMEM_LIMIT = 40 * 1024 * 1024
VMEM_ALONE = 60 * 1024 * 1024


def soften(values, level):
    return values - jnp.clip(values, -level, level)


def split_halves(values):
    high = values.astype(jnp.bfloat16)
    low = (values - high.astype(jnp.float32)).astype(jnp.bfloat16)
    return high, low


def divide(value, by):
    if by & (by - 1):
        return value // by
    return lax.shift_right_logical(value, by.bit_length() - 1)


def limits(entries, devices):
    half = devices // 2
    return min(entries, SLOTS * half), min(entries, SLOTS * (half - 1))


def live_count(count, rows_dev):
    total = count[0]
    for k in range(1, rows_dev):
        total = total + count[k]
    return total


def pack_kernel(
    pattern,
    count,
    x,
    send,
    slots,
    lists,
    wanted,
    sums,
    keys,
    held,
    sem_x,
    sems,
    *,
    rows_dev,
    devices,
    entries,
    block_total,
):
    live = live_count(count, rows_dev)
    half = devices // 2
    far_limit, near_limit = limits(entries, devices)
    position = divide(pattern[0, 0], rows_dev)
    base = position * rows_dev
    side = divide(position, half)
    spot = (position - side * half) * SLOTS

    fetch = pltpu.make_async_copy(x, held, sem_x.at[0])
    fetch.start()
    spare = pltpu.make_async_copy(held.at[0], send.at[spot], sems.at[near_limit])
    for o in range(devices):
        sums[o] = 0
    for q in range(SLOTS * half):
        wanted[q] = 0
    for k in range(far_limit + near_limit):
        lists[0, k] = entries
        lists[1, k] = rows_dev
        lists[2, k] = spot if k >= far_limit else 0
        lists[3, k] = position * SLOTS
    for e in range(entries):
        i = pattern[0, e]
        j = pattern[1, e]
        owner = divide(j, rows_dev)
        key = jnp.minimum(i * block_total + j, j * block_total + i)
        keys[e] = key
        sums[owner] = sums[owner] + key
    fars = jnp.int32(0)
    nears = jnp.int32(far_limit)
    for e in range(entries):
        row = pattern[0, e] - base
        owner = divide(pattern[1, e], rows_dev)
        alive = e < live
        later = jnp.where((2 * keys[e] > sums[owner]) & alive, 1, 0)
        slot = owner * SLOTS + later
        slots[e] = slot
        away = divide(owner, half)
        place = slot - away * (SLOTS * half)
        near = away == side
        wanted[jnp.where(alive & ~near, place, SLOTS * half)] = row
        at = jnp.where(alive, jnp.where(near, nears, fars), far_limit + near_limit)
        lists[0, at] = e
        lists[1, at] = row
        lists[2, at] = place
        lists[3, at] = slot
        fars = fars + jnp.where(alive & ~near, 1, 0)
        nears = nears + jnp.where(alive & near, 1, 0)

    def copy(k):
        return pltpu.make_async_copy(
            held.at[lists[1, k]], send.at[lists[2, k]], sems.at[k - far_limit]
        )

    def begin(k, carry):
        copy(k).start()
        return carry

    def finish(k, carry):
        copy(k).wait()
        return carry

    fetch.wait()
    spare.start()
    lax.fori_loop(far_limit, nears, begin, 0)
    lists[0, far_limit + near_limit + 1] = fars
    lists[0, far_limit + near_limit + 2] = nears
    spare.wait()
    lax.fori_loop(far_limit, nears, finish, 0)


def relay_kernel(wanted, early, late, send, x, sems, *, devices):
    x[: early.shape[0]] = early[...]
    x[early.shape[0] :] = late[...]
    copies = [
        pltpu.make_async_copy(x.at[wanted[q]], send.at[q], sems.at[q])
        for q in range(SLOTS * (devices // 2))
    ]
    for copy in copies:
        copy.start()
    for copy in copies:
        copy.wait()


def own_kernel(lists, x, omega, off, near, projected, logs, wide, *, rows_dev, devices, entries, edge):
    far_limit, near_limit = limits(entries, devices)
    on_diagonal = lax.broadcasted_iota(jnp.int32, (edge, edge), 0) == lax.broadcasted_iota(
        jnp.int32, (edge, edge), 1
    )

    def apply(block, rows):
        high, low = split_halves(block)
        return jnp.dot(
            jnp.concatenate([high, low], axis=1),
            jnp.concatenate([rows, rows], axis=0),
            preferred_element_type=jnp.float32,
        )

    total = jnp.zeros((1, edge), jnp.float32)
    for k in range(rows_dev):
        projected[k] = apply(omega[k], x[k])
        total = total + jnp.log(
            jnp.sum(jnp.where(on_diagonal, omega[k], 0.0), axis=0, keepdims=True)
        )
    projected[rows_dev] = jnp.zeros(projected.shape[1:], jnp.float32)
    logs[...] = jnp.broadcast_to(total, logs.shape)

    def add(k, carry):
        row = lists[1, k]
        block = off[jnp.minimum(lists[0, k], entries - 1)]
        projected[row] = projected[row] + apply(block, near[lists[2, k]])
        return carry

    lax.fori_loop(far_limit, far_limit + near_limit, add, 0)

    def widen(k, carry):
        high, low = split_halves(off[jnp.minimum(lists[0, k], entries - 1)])
        wide[k, :, :edge] = high
        wide[k, :, edge:] = low
        return carry

    lax.fori_loop(0, far_limit, widen, 0)


def main_kernel(
    lists,
    logs,
    far,
    near,
    own,
    wide,
    payload,
    projected,
    held_near,
    held_wide,
    held_own,
    held_rows,
    halves,
    coded,
    stats,
    tail,
    sem_near,
    sem_wide,
    sem_own,
    sem_rows,
    sem_code,
    *,
    rows_dev,
    devices,
    entries,
    edge,
    samples_dev,
):
    far_limit, near_limit = limits(entries, devices)
    limit = far_limit + near_limit
    split = far_limit // 4
    parts = (pl.ds(0, split), pl.ds(split, far_limit - split))
    fetches = [
        pltpu.make_async_copy(wide.at[part], held_wide.at[part], sem_wide.at[at])
        for at, part in enumerate(parts)
    ]
    fetch_own = pltpu.make_async_copy(own.at[pl.ds(0, rows_dev)], held_own, sem_own.at[0])
    fetch_near = pltpu.make_async_copy(near, held_near, sem_near.at[0])
    for fetch in (*fetches, fetch_own, fetch_near):
        fetch.start()
    held_rows[...] = jnp.zeros(held_rows.shape, jnp.float32)
    stats[...] = jnp.zeros(stats.shape, jnp.float32)
    halves[rows_dev] = jnp.zeros(halves.shape[1:], halves.dtype)

    total = jnp.zeros((edge, samples_dev), jnp.float32)
    for k in range(far_limit):
        if k == 0:
            fetches[0].wait()
        if k == split:
            fetches[1].wait()
        rows = far[lists[2, k]]
        part = jnp.dot(
            held_wide[k],
            jnp.concatenate([rows, rows], axis=0),
            preferred_element_type=jnp.float32,
        )
        row = lists[1, k]
        total = part if k == 0 else jnp.where(row == lists[1, k - 1], total, 0.0) + part
        held_rows[row] = total

    fetch_own.wait()
    squares = jnp.zeros((8, samples_dev), jnp.float32)
    for k in range(rows_dev):
        values = held_rows[k] + held_own[k]
        held_own[k] = values
        squares = squares + jnp.sum((values * values).reshape(edge // 8, 8, samples_dev), axis=0)
        high, low = split_halves(values)
        halves[k, :edge] = high
        halves[k, edge:] = low
    store_rows = pltpu.make_async_copy(held_own, projected, sem_rows.at[0])
    store_rows.start()
    fetch_near.wait()

    def store(k):
        slot = lists[3, k]
        owner = divide(slot, SLOTS)
        rank = slot - owner * SLOTS
        return pltpu.make_async_copy(
            coded.at[k],
            payload.at[owner, pl.ds(pl.multiple_of(rank * edge, edge), edge), :],
            sem_code.at[k],
        )

    def begin(k, carry):
        store(k).start()
        return carry

    def finish(k, carry):
        store(k).wait()
        return carry

    def encode(k, rows):
        slot = lists[3, k]
        both = lax.dot_general(
            rows,
            halves[lists[1, k]],
            (((1,), (1,)), ((), ())),
            preferred_element_type=jnp.float32,
        )
        product = both[:, :edge] + both[:, edge:]
        largest = jnp.maximum(jnp.max(jnp.abs(product), axis=0, keepdims=True), 1e-30)
        code = jnp.ceil(jnp.log2(largest) * LOG_STEPS + 0.01)
        scaled = product * jnp.exp2(15.0 - HEADROOM - code * (1.0 / LOG_STEPS))
        owner = divide(slot, SLOTS)
        coded[k] = jnp.round(scaled).astype(jnp.int32).astype(jnp.int16)
        stats[owner, pl.ds(slot - owner * SLOTS, 1), :] = code

    fars = lists[0, limit + 1]
    nears = lists[0, limit + 2]
    for k in range(far_limit):
        encode(k, far[lists[2, k]])
    lax.fori_loop(0, fars, begin, 0)
    for k in range(far_limit, limit):
        encode(k, held_near[lists[2, k]])
    lax.fori_loop(far_limit, nears, begin, 0)

    term = jnp.sum(squares) * (1.0 / (2.0 * samples_dev)) - jnp.sum(logs[0:1, :])
    term = jnp.full((1, edge), term, jnp.float32)
    power = jnp.ceil(jnp.log2(jnp.maximum(jnp.abs(term), 1e-30)) + 0.01)
    scaled = term * jnp.exp2(14.0 - power)
    whole = jnp.round(scaled)
    digits = jnp.concatenate(
        [
            jnp.zeros((SLOTS, edge), jnp.float32),
            power,
            whole,
            jnp.round((scaled - whole) * FRACTION),
            jnp.zeros((STAT_ROWS - SLOTS - 3, edge), jnp.float32),
        ],
        axis=0,
    )
    tail[...] = (stats[...] + digits[None]).astype(jnp.int32).astype(jnp.int16)
    store_tail = pltpu.make_async_copy(
        tail, payload.at[:, pl.ds(SLOTS * edge, STAT_ROWS), :], sem_code.at[limit]
    )
    store_tail.start()
    lax.fori_loop(0, fars, finish, 0)
    lax.fori_loop(far_limit, nears, finish, 0)
    store_rows.wait()
    store_tail.wait()


def side_kernel(
    lists,
    x,
    omega,
    term,
    projected,
    off,
    far,
    near,
    result,
    moved,
    halves,
    *,
    rows_dev,
    devices,
    entries,
    edge,
    samples_dev,
):
    far_limit, near_limit = limits(entries, devices)
    on_diagonal = lax.broadcasted_iota(jnp.int32, (edge, edge), 0) == lax.broadcasted_iota(
        jnp.int32, (edge, edge), 1
    )

    def against(row, other):
        both = lax.dot_general(
            halves[row], other, (((1,), (1,)), ((), ())), preferred_element_type=jnp.float32
        )
        return both[:edge] + both[edge:]

    moved[...] = jnp.zeros(moved.shape, jnp.float32)
    halves[rows_dev] = jnp.zeros(halves.shape[1:], halves.dtype)
    for k in range(rows_dev):
        high, low = split_halves(projected[k])
        halves[k, :edge] = high
        halves[k, edge:] = low
        product = against(k, x[k])
        gradient = (product + product.T) * (1.0 / (2.0 * samples_dev))
        gradient = gradient + jnp.where(on_diagonal, term[k : k + 1, :], 0.0)
        value = omega[k] - STEP_SIZE * gradient
        result[k] = jnp.where(on_diagonal, value, soften(value, STEP_SIZE * PENALTY))

    def move(source, k, carry):
        e = lists[0, k]
        product = against(lists[1, k], source[lists[2, k]])
        moved[e] = off[jnp.minimum(e, entries - 1)] - product * (STEP_SIZE / (2.0 * samples_dev))
        return carry

    lax.fori_loop(0, far_limit, functools.partial(move, far), 0)
    lax.fori_loop(far_limit, far_limit + near_limit, functools.partial(move, near), 0)


def last_kernel(
    count,
    slots,
    moved,
    returned,
    result,
    objective,
    held,
    rt,
    rs,
    sem_in,
    sem_rt,
    sem_out,
    *,
    rows_dev,
    devices,
    entries,
    edge,
    samples_dev,
):
    live = live_count(count, rows_dev)

    def fetch(at, part):
        return pltpu.make_async_copy(moved.at[part], held.at[part], sem_in.at[at])

    def store(at, part):
        return pltpu.make_async_copy(rs.at[part], result.at[part], sem_out.at[at])

    width = max(k for k in range(1, 11) if entries % k == 0)
    parts = [(at, pl.ds(at * width, width)) for at in range(entries // width)]
    whole = pltpu.make_async_copy(returned, rt, sem_rt.at[0])
    whole.start()
    for at, part in parts:
        fetch(at, part).start()
    whole.wait()
    codes = rt[:, SLOTS * edge :, :].astype(jnp.int32).astype(jnp.float32)
    power = codes[:, SLOTS : SLOTS + 1]
    digits = codes[:, SLOTS + 1 : SLOTS + 2] + codes[:, SLOTS + 2 : SLOTS + 3] * (1.0 / FRACTION)
    total = jnp.sum(digits * jnp.exp2(power - 14.0), axis=0)
    objective[0] = jnp.max(total) * (1.0 / (devices * rows_dev * edge))
    for at, part in parts:
        fetch(at, part).wait()
        for e in range(at * width, (at + 1) * width):
            slot = slots[e]
            owner = divide(slot, SLOTS)
            rank = slot - owner * SLOTS
            codes = rt[owner, SLOTS * edge :, :].astype(jnp.int32).astype(jnp.float32)
            code = jnp.where(rank == 0, codes[0:1], codes[1:2])
            weight = jnp.exp2(code * (1.0 / LOG_STEPS) - (15.0 - HEADROOM)) * (
                STEP_SIZE / (2.0 * samples_dev)
            )
            weight = jnp.where(e < live, weight, 0.0)
            digits = rt[owner, pl.ds(pl.multiple_of(rank * edge, edge), edge), :]
            value = held[e] - digits.astype(jnp.int32).astype(jnp.float32) * weight
            rs[e] = soften(value, STEP_SIZE * PENALTY)
        store(at, part).start()
    for at, part in parts:
        store(at, part).wait()


def shards(samples, omega_diag, omega_off, pattern, block_count, diag_term):
    devices = lax.axis_size("rows")
    rows_dev, edge = omega_diag.shape[:2]
    samples_dev = samples.shape[1]
    entries = omega_off.shape[0]
    f32 = jnp.float32
    x = samples.reshape(rows_dev, edge, samples_dev)
    term = diag_term.reshape(rows_dev, edge)
    pattern = pattern.T
    smem = pl.BlockSpec(memory_space=pltpu.SMEM)
    vmem = pl.BlockSpec(memory_space=pltpu.VMEM)
    hbm = pl.BlockSpec(memory_space=pltpu.HBM)
    params = pltpu.CompilerParams(vmem_limit_bytes=VMEM_LIMIT)
    alone = pltpu.CompilerParams(vmem_limit_bytes=VMEM_ALONE)
    sizes = dict(rows_dev=rows_dev, entries=entries, edge=edge)
    every = dict(sizes, devices=devices, samples_dev=samples_dev)
    held = functools.partial(pltpu.with_memory_space_constraint, memory_space=pltpu.VMEM)
    kept = functools.partial(pltpu.with_memory_space_constraint, memory_space=pltpu.HBM)

    dma = pltpu.SemaphoreType.DMA

    half = devices // 2
    far_limit, near_limit = limits(entries, devices)
    limit = far_limit + near_limit
    across = [(o, (o + half) % devices) for o in range(devices)]
    halves = [list(range(half)), list(range(half, devices))]

    early = max(1, rows_dev // 4)
    other_early = lax.ppermute(x[:early], "rows", across)

    send, slots, lists, wanted = pl.pallas_call(
        functools.partial(
            pack_kernel,
            rows_dev=rows_dev,
            devices=devices,
            entries=entries,
            block_total=rows_dev * devices,
        ),
        out_shape=(
            pltpu.HBM((SLOTS * half, edge, samples_dev), samples.dtype),
            jax.ShapeDtypeStruct((entries,), jnp.int32),
            jax.ShapeDtypeStruct((4, limit + 3), jnp.int32),
            jax.ShapeDtypeStruct((SLOTS * half + 1,), jnp.int32),
        ),
        in_specs=[smem, smem, hbm],
        out_specs=(hbm, smem, smem, smem),
        scratch_shapes=[
            pltpu.SMEM((devices,), jnp.int32),
            pltpu.SMEM((entries,), jnp.int32),
            pltpu.VMEM((rows_dev, edge, samples_dev), samples.dtype),
            dma((1,)),
            dma((near_limit + 1,)),
        ],
        compiler_params=params,
        name="pack",
    )(pattern, block_count, kept(x))

    def within(blocks):
        return lax.all_to_all(
            blocks.reshape(half, SLOTS, edge, samples_dev),
            "rows",
            split_axis=0,
            concat_axis=0,
            axis_index_groups=halves,
            tiled=True,
        ).reshape(SLOTS * half, edge, samples_dev)

    wanted = lax.ppermute(wanted, "rows", across)
    near = within(send)
    other_late = lax.ppermute(x[early:], "rows", across)

    passed = pl.pallas_call(
        functools.partial(relay_kernel, devices=devices),
        out_shape=pltpu.HBM((SLOTS * half, edge, samples_dev), samples.dtype),
        in_specs=[smem, vmem, vmem],
        out_specs=hbm,
        scratch_shapes=[
            pltpu.VMEM((rows_dev, edge, samples_dev), samples.dtype),
            dma((SLOTS * half,)),
        ],
        compiler_params=params,
        name="relay",
    )(wanted, held(other_early), held(other_late))
    far = within(passed)

    own, logs, wide = pl.pallas_call(
        functools.partial(own_kernel, devices=devices, **sizes),
        out_shape=(
            pltpu.HBM((rows_dev + 1, edge, samples_dev), f32),
            jax.ShapeDtypeStruct((8, edge), f32),
            pltpu.HBM((far_limit, edge, 2 * edge), jnp.bfloat16),
        ),
        in_specs=[smem] + [vmem] * 4,
        out_specs=(vmem, vmem, vmem),
        compiler_params=params,
        cost_estimate=pl.CostEstimate(
            flops=12 * rows_dev * edge * edge * samples_dev, transcendentals=0, bytes_accessed=1 << 23
        ),
        name="own",
    )(lists, x, omega_diag, omega_off, near)

    payload, projected = pl.pallas_call(
        functools.partial(main_kernel, **every),
        out_shape=(
            pltpu.HBM((devices, SLOTS * edge + STAT_ROWS, edge), jnp.int16),
            pltpu.HBM((rows_dev, edge, samples_dev), f32),
        ),
        in_specs=[smem, vmem, vmem, hbm, hbm, hbm],
        out_specs=(hbm, hbm),
        scratch_shapes=[
            pltpu.VMEM((SLOTS * half, edge, samples_dev), samples.dtype),
            pltpu.VMEM((far_limit, edge, 2 * edge), jnp.bfloat16),
            pltpu.VMEM((rows_dev, edge, samples_dev), f32),
            pltpu.VMEM((rows_dev + 1, edge, samples_dev), f32),
            pltpu.VMEM((rows_dev + 1, 2 * edge, samples_dev), jnp.bfloat16),
            pltpu.VMEM((limit, edge, edge), jnp.int16),
            pltpu.VMEM((devices, STAT_ROWS, edge), f32),
            pltpu.VMEM((devices, STAT_ROWS, edge), jnp.int16),
            dma((1,)),
            dma((2,)),
            dma((1,)),
            dma((1,)),
            dma((limit + 1,)),
        ],
        compiler_params=params,
        name="main",
    )(lists, logs, held(far), kept(near), kept(own), kept(wide))

    returned = lax.all_to_all(kept(payload), "rows", split_axis=0, concat_axis=0, tiled=True)

    diag_next, moved = pl.pallas_call(
        functools.partial(side_kernel, **every),
        out_shape=(
            jax.ShapeDtypeStruct((rows_dev, edge, edge), f32),
            pltpu.HBM((entries + 1, edge, edge), f32),
        ),
        in_specs=[smem] + [vmem] * 7,
        out_specs=(vmem, vmem),
        scratch_shapes=[pltpu.VMEM((rows_dev + 1, 2 * edge, samples_dev), jnp.bfloat16)],
        compiler_params=params,
        cost_estimate=pl.CostEstimate(
            flops=12 * rows_dev * edge * edge * samples_dev, transcendentals=0, bytes_accessed=1 << 23
        ),
        name="side",
    )(lists, x, omega_diag, term, projected, omega_off, far, near)

    off_next, objective = pl.pallas_call(
        functools.partial(last_kernel, **every),
        out_shape=(
            jax.ShapeDtypeStruct((entries, edge, edge), f32),
            jax.ShapeDtypeStruct((1,), f32),
        ),
        in_specs=[smem, smem, hbm, hbm],
        out_specs=(hbm, smem),
        scratch_shapes=[
            pltpu.VMEM((entries, edge, edge), f32),
            pltpu.VMEM((devices, SLOTS * edge + STAT_ROWS, edge), jnp.int16),
            pltpu.VMEM((entries, edge, edge), f32),
            dma((entries,)),
            dma((1,)),
            dma((entries,)),
        ],
        compiler_params=alone,
        name="last",
    )(block_count, slots, kept(moved), kept(returned))
    return diag_next, off_next, objective


def solution(mesh):
    return jax.shard_map(
        shards,
        mesh=mesh,
        in_specs=(
            P(("groups", "rows"), None),
            P(("groups", "rows"), None, None),
            P(("groups", "rows"), None, None),
            P(("groups", "rows"), None),
            P(("groups", "rows")),
            P(("groups", "rows")),
        ),
        out_specs=(
            P(("groups", "rows"), None, None),
            P(("groups", "rows"), None, None),
            P("groups"),
        ),
        check_vma=False,
    )
```

```python
import functools

import jax
import jax.numpy as jnp
from jax import lax
from jax.experimental import pallas as pl
from jax.experimental.pallas import tpu as pltpu
from jax.sharding import PartitionSpec as P


SLOTS = 2
STAT_ROWS = 8
STEP_SIZE = 0.5
PENALTY = 0.01
LOG_STEPS = 128.0
HEADROOM = 1e-4
FRACTION = 32000.0
VMEM_LIMIT = 40 * 1024 * 1024
VMEM_ALONE = 60 * 1024 * 1024


def soften(values, level):
    return values - jnp.clip(values, -level, level)


def split_halves(values):
    high = values.astype(jnp.bfloat16)
    low = (values - high.astype(jnp.float32)).astype(jnp.bfloat16)
    return high, low


def divide(value, by):
    if isinstance(value, int) or by & (by - 1):
        return value // by
    return lax.shift_right_logical(value, by.bit_length() - 1)


def mirror(o, devices, layer):
    return o + (devices - layer) - 2 * layer * divide(o, layer)


def limits(entries, devices):
    half = devices // 2
    return min(entries, SLOTS * half), min(entries, SLOTS * (half - 1))


def live_count(count, rows_dev):
    total = count[0]
    for k in range(1, rows_dev):
        total = total + count[k]
    return total


def pack_kernel(
    pattern,
    count,
    x,
    send,
    slots,
    lists,
    wanted,
    sums,
    keys,
    held,
    sem_x,
    sems,
    *,
    rows_dev,
    devices,
    layer,
    entries,
    block_total,
):
    live = live_count(count, rows_dev)
    half = devices // 2
    far_limit, near_limit = limits(entries, devices)
    position = divide(pattern[0, 0], rows_dev)
    base = position * rows_dev
    side = divide(position, half)
    spot = (position - side * half) * SLOTS

    fetch = pltpu.make_async_copy(x, held, sem_x.at[0])
    fetch.start()
    spare = pltpu.make_async_copy(held.at[0], send.at[spot], sems.at[near_limit])
    for o in range(devices):
        sums[o] = 0
    for q in range(SLOTS * half):
        wanted[q] = 0
    for k in range(far_limit + near_limit):
        lists[0, k] = entries
        lists[1, k] = rows_dev
        lists[2, k] = spot if k >= far_limit else 0
        lists[3, k] = position * SLOTS
    for e in range(entries):
        i = pattern[0, e]
        j = pattern[1, e]
        owner = divide(j, rows_dev)
        key = jnp.minimum(i * block_total + j, j * block_total + i)
        keys[e] = key
        sums[owner] = sums[owner] + key
    fars = jnp.int32(0)
    nears = jnp.int32(far_limit)
    for e in range(entries):
        row = pattern[0, e] - base
        owner = divide(pattern[1, e], rows_dev)
        alive = e < live
        later = jnp.where((2 * keys[e] > sums[owner]) & alive, 1, 0)
        slot = owner * SLOTS + later
        slots[e] = slot
        away = divide(owner, half)
        place = slot - away * (SLOTS * half)
        near = away == side
        wanted[jnp.where(alive & ~near, place, SLOTS * half)] = row
        at = jnp.where(alive, jnp.where(near, nears, fars), far_limit + near_limit)
        lists[0, at] = e
        lists[1, at] = row
        across = mirror(owner, devices, layer)
        across = across - divide(across, half) * half
        lists[2, at] = jnp.where(near, place, across * SLOTS + later)
        lists[3, at] = slot
        fars = fars + jnp.where(alive & ~near, 1, 0)
        nears = nears + jnp.where(alive & near, 1, 0)

    def copy(k):
        return pltpu.make_async_copy(
            held.at[lists[1, k]], send.at[lists[2, k]], sems.at[k - far_limit]
        )

    def begin(k, carry):
        copy(k).start()
        return carry

    def finish(k, carry):
        copy(k).wait()
        return carry

    fetch.wait()
    spare.start()
    lax.fori_loop(far_limit, nears, begin, 0)
    lists[0, far_limit + near_limit + 1] = fars
    lists[0, far_limit + near_limit + 2] = nears
    spare.wait()
    lax.fori_loop(far_limit, nears, finish, 0)


def relay_kernel(wanted, outer, inner, send, x, sems, *, devices):
    x[...] = outer[...] + inner[...]
    copies = [
        pltpu.make_async_copy(x.at[wanted[q]], send.at[q], sems.at[q])
        for q in range(SLOTS * (devices // 2))
    ]
    for copy in copies:
        copy.start()
    for copy in copies:
        copy.wait()


def own_kernel(lists, x, omega, off, near, projected, logs, wide, *, rows_dev, devices, entries, edge):
    far_limit, near_limit = limits(entries, devices)
    on_diagonal = lax.broadcasted_iota(jnp.int32, (edge, edge), 0) == lax.broadcasted_iota(
        jnp.int32, (edge, edge), 1
    )

    def apply(block, rows):
        high, low = split_halves(block)
        return jnp.dot(
            jnp.concatenate([high, low], axis=1),
            jnp.concatenate([rows, rows], axis=0),
            preferred_element_type=jnp.float32,
        )

    total = jnp.zeros((1, edge), jnp.float32)
    for k in range(rows_dev):
        projected[k] = apply(omega[k], x[k])
        total = total + jnp.log(
            jnp.sum(jnp.where(on_diagonal, omega[k], 0.0), axis=0, keepdims=True)
        )
    projected[rows_dev] = jnp.zeros(projected.shape[1:], jnp.float32)
    logs[...] = jnp.broadcast_to(total, logs.shape)

    def add(k, carry):
        row = lists[1, k]
        block = off[jnp.minimum(lists[0, k], entries - 1)]
        projected[row] = projected[row] + apply(block, near[lists[2, k]])
        return carry

    lax.fori_loop(far_limit, far_limit + near_limit, add, 0)

    def widen(k, carry):
        high, low = split_halves(off[jnp.minimum(lists[0, k], entries - 1)])
        wide[k, :, :edge] = high
        wide[k, :, edge:] = low
        return carry

    lax.fori_loop(0, far_limit, widen, 0)


def main_kernel(
    lists,
    logs,
    far,
    near,
    own,
    wide,
    payload,
    projected,
    held_near,
    held_wide,
    held_own,
    held_rows,
    halves,
    coded,
    stats,
    tail,
    sem_near,
    sem_wide,
    sem_own,
    sem_rows,
    sem_code,
    *,
    rows_dev,
    devices,
    entries,
    edge,
    samples_dev,
):
    far_limit, near_limit = limits(entries, devices)
    limit = far_limit + near_limit
    split = far_limit // 4
    parts = (pl.ds(0, split), pl.ds(split, far_limit - split))
    fetches = [
        pltpu.make_async_copy(wide.at[part], held_wide.at[part], sem_wide.at[at])
        for at, part in enumerate(parts)
    ]
    fetch_own = pltpu.make_async_copy(own.at[pl.ds(0, rows_dev)], held_own, sem_own.at[0])
    fetch_near = pltpu.make_async_copy(near, held_near, sem_near.at[0])
    for fetch in (*fetches, fetch_own, fetch_near):
        fetch.start()
    held_rows[...] = jnp.zeros(held_rows.shape, jnp.float32)
    stats[...] = jnp.zeros(stats.shape, jnp.float32)
    halves[rows_dev] = jnp.zeros(halves.shape[1:], halves.dtype)

    total = jnp.zeros((edge, samples_dev), jnp.float32)
    for k in range(far_limit):
        if k == 0:
            fetches[0].wait()
        if k == split:
            fetches[1].wait()
        rows = far[lists[2, k]]
        part = jnp.dot(
            held_wide[k],
            jnp.concatenate([rows, rows], axis=0),
            preferred_element_type=jnp.float32,
        )
        row = lists[1, k]
        total = part if k == 0 else jnp.where(row == lists[1, k - 1], total, 0.0) + part
        held_rows[row] = total

    fetch_own.wait()
    squares = jnp.zeros((8, samples_dev), jnp.float32)
    for k in range(rows_dev):
        values = held_rows[k] + held_own[k]
        held_own[k] = values
        squares = squares + jnp.sum((values * values).reshape(edge // 8, 8, samples_dev), axis=0)
        high, low = split_halves(values)
        halves[k, :edge] = high
        halves[k, edge:] = low
    store_rows = pltpu.make_async_copy(held_own, projected, sem_rows.at[0])
    store_rows.start()
    fetch_near.wait()

    def store(k):
        slot = lists[3, k]
        owner = divide(slot, SLOTS)
        rank = slot - owner * SLOTS
        return pltpu.make_async_copy(
            coded.at[k],
            payload.at[owner, pl.ds(pl.multiple_of(rank * edge, edge), edge), :],
            sem_code.at[k],
        )

    def begin(k, carry):
        store(k).start()
        return carry

    def finish(k, carry):
        store(k).wait()
        return carry

    def encode(k, rows):
        slot = lists[3, k]
        both = lax.dot_general(
            rows,
            halves[lists[1, k]],
            (((1,), (1,)), ((), ())),
            preferred_element_type=jnp.float32,
        )
        product = both[:, :edge] + both[:, edge:]
        largest = jnp.maximum(jnp.max(jnp.abs(product), axis=0, keepdims=True), 1e-30)
        code = jnp.ceil(jnp.log2(largest) * LOG_STEPS + 0.01)
        scaled = product * jnp.exp2(15.0 - HEADROOM - code * (1.0 / LOG_STEPS))
        owner = divide(slot, SLOTS)
        coded[k] = jnp.round(scaled).astype(jnp.int32).astype(jnp.int16)
        stats[owner, pl.ds(slot - owner * SLOTS, 1), :] = code

    fars = lists[0, limit + 1]
    nears = lists[0, limit + 2]
    for k in range(far_limit):
        encode(k, far[lists[2, k]])
    lax.fori_loop(0, fars, begin, 0)
    for k in range(far_limit, limit):
        encode(k, held_near[lists[2, k]])
    lax.fori_loop(far_limit, nears, begin, 0)

    term = jnp.sum(squares) * (1.0 / (2.0 * samples_dev)) - jnp.sum(logs[0:1, :])
    term = jnp.full((1, edge), term, jnp.float32)
    power = jnp.ceil(jnp.log2(jnp.maximum(jnp.abs(term), 1e-30)) + 0.01)
    scaled = term * jnp.exp2(14.0 - power)
    whole = jnp.round(scaled)
    digits = jnp.concatenate(
        [
            jnp.zeros((SLOTS, edge), jnp.float32),
            power,
            whole,
            jnp.round((scaled - whole) * FRACTION),
            jnp.zeros((STAT_ROWS - SLOTS - 3, edge), jnp.float32),
        ],
        axis=0,
    )
    tail[...] = (stats[...] + digits[None]).astype(jnp.int32).astype(jnp.int16)
    store_tail = pltpu.make_async_copy(
        tail, payload.at[:, pl.ds(SLOTS * edge, STAT_ROWS), :], sem_code.at[limit]
    )
    store_tail.start()
    lax.fori_loop(0, fars, finish, 0)
    lax.fori_loop(far_limit, nears, finish, 0)
    store_rows.wait()
    store_tail.wait()


def side_kernel(
    lists,
    x,
    omega,
    term,
    projected,
    off,
    far,
    near,
    result,
    moved,
    halves,
    *,
    rows_dev,
    devices,
    entries,
    edge,
    samples_dev,
):
    far_limit, near_limit = limits(entries, devices)
    on_diagonal = lax.broadcasted_iota(jnp.int32, (edge, edge), 0) == lax.broadcasted_iota(
        jnp.int32, (edge, edge), 1
    )

    def against(row, other):
        both = lax.dot_general(
            halves[row], other, (((1,), (1,)), ((), ())), preferred_element_type=jnp.float32
        )
        return both[:edge] + both[edge:]

    moved[...] = jnp.zeros(moved.shape, jnp.float32)
    halves[rows_dev] = jnp.zeros(halves.shape[1:], halves.dtype)
    for k in range(rows_dev):
        high, low = split_halves(projected[k])
        halves[k, :edge] = high
        halves[k, edge:] = low
        product = against(k, x[k])
        gradient = (product + product.T) * (1.0 / (2.0 * samples_dev))
        gradient = gradient + jnp.where(on_diagonal, term[k : k + 1, :], 0.0)
        value = omega[k] - STEP_SIZE * gradient
        result[k] = jnp.where(on_diagonal, value, soften(value, STEP_SIZE * PENALTY))

    def move(source, k, carry):
        e = lists[0, k]
        product = against(lists[1, k], source[lists[2, k]])
        moved[e] = off[jnp.minimum(e, entries - 1)] - product * (STEP_SIZE / (2.0 * samples_dev))
        return carry

    lax.fori_loop(0, far_limit, functools.partial(move, far), 0)
    lax.fori_loop(far_limit, far_limit + near_limit, functools.partial(move, near), 0)


def last_kernel(
    count,
    slots,
    moved,
    returned,
    result,
    objective,
    held,
    rt,
    rs,
    sem_in,
    sem_rt,
    sem_out,
    *,
    rows_dev,
    devices,
    entries,
    edge,
    samples_dev,
):
    live = live_count(count, rows_dev)

    def fetch(at, part):
        return pltpu.make_async_copy(moved.at[part], held.at[part], sem_in.at[at])

    def store(at, part):
        return pltpu.make_async_copy(rs.at[part], result.at[part], sem_out.at[at])

    width = max(k for k in range(1, 11) if entries % k == 0)
    parts = [(at, pl.ds(at * width, width)) for at in range(entries // width)]
    whole = pltpu.make_async_copy(returned, rt, sem_rt.at[0])
    whole.start()
    for at, part in parts:
        fetch(at, part).start()
    whole.wait()
    codes = rt[:, SLOTS * edge :, :].astype(jnp.int32).astype(jnp.float32)
    power = codes[:, SLOTS : SLOTS + 1]
    digits = codes[:, SLOTS + 1 : SLOTS + 2] + codes[:, SLOTS + 2 : SLOTS + 3] * (1.0 / FRACTION)
    total = jnp.sum(digits * jnp.exp2(power - 14.0), axis=0)
    objective[0] = jnp.max(total) * (1.0 / (devices * rows_dev * edge))
    for at, part in parts:
        fetch(at, part).wait()
        for e in range(at * width, (at + 1) * width):
            slot = slots[e]
            owner = divide(slot, SLOTS)
            rank = slot - owner * SLOTS
            codes = rt[owner, SLOTS * edge :, :].astype(jnp.int32).astype(jnp.float32)
            code = jnp.where(rank == 0, codes[0:1], codes[1:2])
            weight = jnp.exp2(code * (1.0 / LOG_STEPS) - (15.0 - HEADROOM)) * (
                STEP_SIZE / (2.0 * samples_dev)
            )
            weight = jnp.where(e < live, weight, 0.0)
            digits = rt[owner, pl.ds(pl.multiple_of(rank * edge, edge), edge), :]
            value = held[e] - digits.astype(jnp.int32).astype(jnp.float32) * weight
            rs[e] = soften(value, STEP_SIZE * PENALTY)
        store(at, part).start()
    for at, part in parts:
        store(at, part).wait()


def layer_of(mesh):
    spots = [getattr(d, "coords", None) for d in mesh.devices.reshape(-1, mesh.shape["rows"])[0]]
    best = 1
    for axis in range(3) if None not in spots else ():
        places = [spot[axis] for spot in spots]
        count = len(set(places))
        runs = 1 + sum(a != b for a, b in zip(places, places[1:]))
        if runs == count and count % 2 == 0:
            best = max(best, len(places) // count)
    return best


def shards(samples, omega_diag, omega_off, pattern, block_count, diag_term, *, layer):
    devices = lax.axis_size("rows")
    rows_dev, edge = omega_diag.shape[:2]
    samples_dev = samples.shape[1]
    entries = omega_off.shape[0]
    f32 = jnp.float32
    x = samples.reshape(rows_dev, edge, samples_dev)
    term = diag_term.reshape(rows_dev, edge)
    pattern = pattern.T
    smem = pl.BlockSpec(memory_space=pltpu.SMEM)
    vmem = pl.BlockSpec(memory_space=pltpu.VMEM)
    hbm = pl.BlockSpec(memory_space=pltpu.HBM)
    params = pltpu.CompilerParams(vmem_limit_bytes=VMEM_LIMIT)
    alone = pltpu.CompilerParams(vmem_limit_bytes=VMEM_ALONE)
    sizes = dict(rows_dev=rows_dev, entries=entries, edge=edge)
    every = dict(sizes, devices=devices, samples_dev=samples_dev)
    held = functools.partial(pltpu.with_memory_space_constraint, memory_space=pltpu.VMEM)
    kept = functools.partial(pltpu.with_memory_space_constraint, memory_space=pltpu.HBM)

    dma = pltpu.SemaphoreType.DMA

    half = devices // 2
    far_limit, near_limit = limits(entries, devices)
    limit = far_limit + near_limit
    across = [(o, mirror(o, devices, layer)) for o in range(devices)]
    steps = devices // layer
    outer = [(o, m) for o, m in across if 4 * abs(2 * (o // layer) + 1 - steps) > 2 * steps]
    inner = [pair for pair in across if pair not in outer]
    halves = [list(range(half)), list(range(half, devices))]

    from_outer = lax.ppermute(kept(x), "rows", outer)

    send, slots, lists, wanted = pl.pallas_call(
        functools.partial(
            pack_kernel,
            rows_dev=rows_dev,
            devices=devices,
            layer=layer,
            entries=entries,
            block_total=rows_dev * devices,
        ),
        out_shape=(
            pltpu.HBM((SLOTS * half, edge, samples_dev), samples.dtype),
            jax.ShapeDtypeStruct((entries,), jnp.int32),
            jax.ShapeDtypeStruct((4, limit + 3), jnp.int32),
            jax.ShapeDtypeStruct((SLOTS * half + 1,), jnp.int32),
        ),
        in_specs=[smem, smem, hbm],
        out_specs=(hbm, smem, smem, smem),
        scratch_shapes=[
            pltpu.SMEM((devices,), jnp.int32),
            pltpu.SMEM((entries,), jnp.int32),
            pltpu.VMEM((rows_dev, edge, samples_dev), samples.dtype),
            dma((1,)),
            dma((near_limit + 1,)),
        ],
        compiler_params=params,
        name="pack",
    )(pattern, block_count, kept(x))

    def within(blocks):
        return lax.all_to_all(
            blocks.reshape(half, SLOTS, edge, samples_dev),
            "rows",
            split_axis=0,
            concat_axis=0,
            axis_index_groups=halves,
            tiled=True,
        ).reshape(SLOTS * half, edge, samples_dev)

    wanted = lax.ppermute(wanted, "rows", across)
    near = within(send)
    from_inner = lax.ppermute(kept(x), "rows", inner)

    passed = pl.pallas_call(
        functools.partial(relay_kernel, devices=devices),
        out_shape=pltpu.HBM((SLOTS * half, edge, samples_dev), samples.dtype),
        in_specs=[smem, vmem, vmem],
        out_specs=hbm,
        scratch_shapes=[
            pltpu.VMEM((rows_dev, edge, samples_dev), samples.dtype),
            dma((SLOTS * half,)),
        ],
        compiler_params=params,
        name="relay",
    )(wanted, held(from_outer), held(from_inner))
    far = within(passed)

    own, logs, wide = pl.pallas_call(
        functools.partial(own_kernel, devices=devices, **sizes),
        out_shape=(
            pltpu.HBM((rows_dev + 1, edge, samples_dev), f32),
            jax.ShapeDtypeStruct((8, edge), f32),
            pltpu.HBM((far_limit, edge, 2 * edge), jnp.bfloat16),
        ),
        in_specs=[smem] + [vmem] * 4,
        out_specs=(vmem, vmem, vmem),
        compiler_params=params,
        cost_estimate=pl.CostEstimate(
            flops=12 * rows_dev * edge * edge * samples_dev, transcendentals=0, bytes_accessed=1 << 23
        ),
        name="own",
    )(lists, x, omega_diag, omega_off, near)

    payload, projected = pl.pallas_call(
        functools.partial(main_kernel, **every),
        out_shape=(
            pltpu.HBM((devices, SLOTS * edge + STAT_ROWS, edge), jnp.int16),
            pltpu.HBM((rows_dev, edge, samples_dev), f32),
        ),
        in_specs=[smem, vmem, vmem, hbm, hbm, hbm],
        out_specs=(hbm, hbm),
        scratch_shapes=[
            pltpu.VMEM((SLOTS * half, edge, samples_dev), samples.dtype),
            pltpu.VMEM((far_limit, edge, 2 * edge), jnp.bfloat16),
            pltpu.VMEM((rows_dev, edge, samples_dev), f32),
            pltpu.VMEM((rows_dev + 1, edge, samples_dev), f32),
            pltpu.VMEM((rows_dev + 1, 2 * edge, samples_dev), jnp.bfloat16),
            pltpu.VMEM((limit, edge, edge), jnp.int16),
            pltpu.VMEM((devices, STAT_ROWS, edge), f32),
            pltpu.VMEM((devices, STAT_ROWS, edge), jnp.int16),
            dma((1,)),
            dma((2,)),
            dma((1,)),
            dma((1,)),
            dma((limit + 1,)),
        ],
        compiler_params=params,
        name="main",
    )(lists, logs, held(far), kept(near), kept(own), kept(wide))

    returned = lax.all_to_all(kept(payload), "rows", split_axis=0, concat_axis=0, tiled=True)

    diag_next, moved = pl.pallas_call(
        functools.partial(side_kernel, **every),
        out_shape=(
            jax.ShapeDtypeStruct((rows_dev, edge, edge), f32),
            pltpu.HBM((entries + 1, edge, edge), f32),
        ),
        in_specs=[smem] + [vmem] * 7,
        out_specs=(vmem, vmem),
        scratch_shapes=[pltpu.VMEM((rows_dev + 1, 2 * edge, samples_dev), jnp.bfloat16)],
        compiler_params=params,
        cost_estimate=pl.CostEstimate(
            flops=12 * rows_dev * edge * edge * samples_dev, transcendentals=0, bytes_accessed=1 << 23
        ),
        name="side",
    )(lists, x, omega_diag, term, projected, omega_off, far, near)

    off_next, objective = pl.pallas_call(
        functools.partial(last_kernel, **every),
        out_shape=(
            jax.ShapeDtypeStruct((entries, edge, edge), f32),
            jax.ShapeDtypeStruct((1,), f32),
        ),
        in_specs=[smem, smem, hbm, hbm],
        out_specs=(hbm, smem),
        scratch_shapes=[
            pltpu.VMEM((entries, edge, edge), f32),
            pltpu.VMEM((devices, SLOTS * edge + STAT_ROWS, edge), jnp.int16),
            pltpu.VMEM((entries, edge, edge), f32),
            dma((entries,)),
            dma((1,)),
            dma((entries,)),
        ],
        compiler_params=alone,
        name="last",
    )(block_count, slots, kept(moved), kept(returned))
    return diag_next, off_next, objective


def solution(mesh):
    return jax.shard_map(
        functools.partial(shards, layer=layer_of(mesh)),
        mesh=mesh,
        in_specs=(
            P(("groups", "rows"), None),
            P(("groups", "rows"), None, None),
            P(("groups", "rows"), None, None),
            P(("groups", "rows"), None),
            P(("groups", "rows")),
            P(("groups", "rows")),
        ),
        out_specs=(
            P(("groups", "rows"), None, None),
            P(("groups", "rows"), None, None),
            P("groups"),
        ),
        check_vma=False,
    )
```

```python
import functools

import jax
import jax.numpy as jnp
from jax import lax
from jax.experimental import pallas as pl
from jax.experimental.pallas import tpu as pltpu
from jax.sharding import PartitionSpec as P


SLOTS = 2
STAT_ROWS = 8
STEP_SIZE = 0.5
PENALTY = 0.01
LOG_STEPS = 128.0
HEADROOM = 1e-4
FRACTION = 32000.0
VMEM_LIMIT = 40 * 1024 * 1024
VMEM_ALONE = 60 * 1024 * 1024


def soften(values, level):
    return values - jnp.clip(values, -level, level)


def split_halves(values):
    high = values.astype(jnp.bfloat16)
    low = (values - high.astype(jnp.float32)).astype(jnp.bfloat16)
    return high, low


def divide(value, by):
    if isinstance(value, int) or by & (by - 1):
        return value // by
    return lax.shift_right_logical(value, by.bit_length() - 1)


def mirror(o, devices, layer):
    return o + (devices - layer) - 2 * layer * divide(o, layer)


def limits(entries, devices):
    half = devices // 2
    return min(entries, SLOTS * half), min(entries, SLOTS * (half - 1))


def live_count(count, rows_dev):
    total = count[0]
    for k in range(1, rows_dev):
        total = total + count[k]
    return total


def place(pattern, keys, sums, visit, *, rows_dev, devices, entries):
    position = divide(pattern[0, 0], rows_dev)
    block_total = rows_dev * devices
    for o in range(devices):
        sums[o] = 0
    for e in range(entries):
        i = pattern[0, e]
        j = pattern[1, e]
        owner = divide(j, rows_dev)
        key = jnp.minimum(i * block_total + j, j * block_total + i)
        keys[e] = key
        sums[owner] = sums[owner] + key
    for e in range(entries):
        owner = divide(pattern[1, e], rows_dev)
        later = jnp.where(2 * keys[e] > sums[owner], 1, 0)
        visit(e, pattern[0, e] - position * rows_dev, owner, later, owner != position)


def pack_kernel(pattern, x, send, keys, sums, picks, held, sem_x, sems, *, rows_dev, devices, entries):
    half = devices // 2
    near_limit = limits(entries, devices)[1]
    fetch = pltpu.make_async_copy(x, held, sem_x.at[0])
    fetch.start()
    position = divide(pattern[0, 0], rows_dev)
    first = divide(position, half) * half
    spare = pltpu.make_async_copy(
        held.at[0], send.at[(position - first) * SLOTS], sems.at[near_limit]
    )
    total = [jnp.int32(0)]

    def visit(e, row, owner, later, alive):
        index = owner - first
        wanted = alive & (index >= 0) & (index < half)
        picks[0, total[0]] = row
        picks[1, total[0]] = index * SLOTS + later
        total[0] = total[0] + jnp.where(wanted, 1, 0)

    place(pattern, keys, sums, visit, rows_dev=rows_dev, devices=devices, entries=entries)

    def copy(k):
        return pltpu.make_async_copy(held.at[picks[0, k]], send.at[picks[1, k]], sems.at[k])

    def begin(k, carry):
        copy(k).start()
        return carry

    def finish(k, carry):
        copy(k).wait()
        return carry

    fetch.wait()
    spare.start()
    lax.fori_loop(0, total[0], begin, 0)
    spare.wait()
    lax.fori_loop(0, total[0], finish, 0)


def plan_kernel(
    pattern, other, slots, lists, wanted, keys, sums, *, rows_dev, devices, layer, entries
):
    half = devices // 2
    far_limit, near_limit = limits(entries, devices)
    limit = far_limit + near_limit
    position = divide(pattern[0, 0], rows_dev)
    first = divide(position, half) * half
    for k in range(limit):
        lists[0, k] = entries
        lists[1, k] = rows_dev
        lists[2, k] = (position - first) * SLOTS if k >= far_limit else 0
        lists[3, k] = position * SLOTS
    for q in range(SLOTS * half):
        wanted[q] = 0
    tops = [jnp.int32(0), jnp.int32(far_limit)]

    def visit(e, row, owner, later, alive):
        later = jnp.where(alive, later, 0)
        slot = owner * SLOTS + later
        slots[e] = slot
        index = owner - first
        near = (index >= 0) & (index < half)
        across = mirror(owner, devices, layer) - first
        at = jnp.where(alive, jnp.where(near, tops[1], tops[0]), limit)
        lists[0, at] = e
        lists[1, at] = row
        lists[2, at] = jnp.where(near, index, across) * SLOTS + later
        lists[3, at] = slot
        tops[0] = tops[0] + jnp.where(alive & ~near, 1, 0)
        tops[1] = tops[1] + jnp.where(alive & near, 1, 0)

    place(pattern, keys, sums, visit, rows_dev=rows_dev, devices=devices, entries=entries)
    lists[0, limit + 1] = tops[0]
    lists[0, limit + 2] = tops[1]

    def wish(e, row, owner, later, alive):
        index = owner - first
        ours = alive & (index >= 0) & (index < half)
        wanted[jnp.where(ours, index * SLOTS + later, SLOTS * half)] = row

    place(other, keys, sums, wish, rows_dev=rows_dev, devices=devices, entries=entries)


def relay_kernel(wanted, outer, inner, send, x, sems, *, devices):
    x[...] = outer[...] + inner[...]
    copies = [
        pltpu.make_async_copy(x.at[wanted[q]], send.at[q], sems.at[q])
        for q in range(SLOTS * (devices // 2))
    ]
    for copy in copies:
        copy.start()
    for copy in copies:
        copy.wait()


def own_kernel(lists, x, omega, off, near, projected, logs, wide, *, rows_dev, devices, entries, edge):
    far_limit, near_limit = limits(entries, devices)
    on_diagonal = lax.broadcasted_iota(jnp.int32, (edge, edge), 0) == lax.broadcasted_iota(
        jnp.int32, (edge, edge), 1
    )

    def apply(block, rows):
        high, low = split_halves(block)
        return jnp.dot(
            jnp.concatenate([high, low], axis=1),
            jnp.concatenate([rows, rows], axis=0),
            preferred_element_type=jnp.float32,
        )

    total = jnp.zeros((1, edge), jnp.float32)
    for k in range(rows_dev):
        projected[k] = apply(omega[k], x[k])
        total = total + jnp.log(
            jnp.sum(jnp.where(on_diagonal, omega[k], 0.0), axis=0, keepdims=True)
        )
    projected[rows_dev] = jnp.zeros(projected.shape[1:], jnp.float32)
    logs[...] = jnp.broadcast_to(total, logs.shape)

    def add(k, carry):
        row = lists[1, k]
        block = off[jnp.minimum(lists[0, k], entries - 1)]
        projected[row] = projected[row] + apply(block, near[lists[2, k]])
        return carry

    lax.fori_loop(far_limit, far_limit + near_limit, add, 0)

    def widen(k, carry):
        high, low = split_halves(off[jnp.minimum(lists[0, k], entries - 1)])
        wide[k, :, :edge] = high
        wide[k, :, edge:] = low
        return carry

    lax.fori_loop(0, far_limit, widen, 0)


def main_kernel(
    lists,
    logs,
    far,
    near,
    own,
    wide,
    payload,
    projected,
    held_near,
    held_wide,
    held_own,
    held_rows,
    halves,
    coded,
    stats,
    tail,
    sem_near,
    sem_wide,
    sem_own,
    sem_rows,
    sem_code,
    *,
    rows_dev,
    devices,
    entries,
    edge,
    samples_dev,
):
    far_limit, near_limit = limits(entries, devices)
    limit = far_limit + near_limit
    split = far_limit // 4
    parts = (pl.ds(0, split), pl.ds(split, far_limit - split))
    fetches = [
        pltpu.make_async_copy(wide.at[part], held_wide.at[part], sem_wide.at[at])
        for at, part in enumerate(parts)
    ]
    fetch_own = pltpu.make_async_copy(own.at[pl.ds(0, rows_dev)], held_own, sem_own.at[0])
    fetch_near = pltpu.make_async_copy(near, held_near, sem_near.at[0])
    for fetch in (*fetches, fetch_own, fetch_near):
        fetch.start()
    held_rows[...] = jnp.zeros(held_rows.shape, jnp.float32)
    stats[...] = jnp.zeros(stats.shape, jnp.float32)
    halves[rows_dev] = jnp.zeros(halves.shape[1:], halves.dtype)

    total = jnp.zeros((edge, samples_dev), jnp.float32)
    for k in range(far_limit):
        if k == 0:
            fetches[0].wait()
        if k == split:
            fetches[1].wait()
        rows = far[lists[2, k]]
        part = jnp.dot(
            held_wide[k],
            jnp.concatenate([rows, rows], axis=0),
            preferred_element_type=jnp.float32,
        )
        row = lists[1, k]
        total = part if k == 0 else jnp.where(row == lists[1, k - 1], total, 0.0) + part
        held_rows[row] = total

    fetch_own.wait()
    squares = jnp.zeros((8, samples_dev), jnp.float32)
    for k in range(rows_dev):
        values = held_rows[k] + held_own[k]
        held_own[k] = values
        squares = squares + jnp.sum((values * values).reshape(edge // 8, 8, samples_dev), axis=0)
        high, low = split_halves(values)
        halves[k, :edge] = high
        halves[k, edge:] = low
    store_rows = pltpu.make_async_copy(held_own, projected, sem_rows.at[0])
    store_rows.start()
    fetch_near.wait()

    def store(k):
        slot = lists[3, k]
        owner = divide(slot, SLOTS)
        rank = slot - owner * SLOTS
        return pltpu.make_async_copy(
            coded.at[k],
            payload.at[owner, pl.ds(pl.multiple_of(rank * edge, edge), edge), :],
            sem_code.at[k],
        )

    def begin(k, carry):
        store(k).start()
        return carry

    def finish(k, carry):
        store(k).wait()
        return carry

    def encode(k, rows):
        slot = lists[3, k]
        both = lax.dot_general(
            rows,
            halves[lists[1, k]],
            (((1,), (1,)), ((), ())),
            preferred_element_type=jnp.float32,
        )
        product = both[:, :edge] + both[:, edge:]
        largest = jnp.maximum(jnp.max(jnp.abs(product), axis=0, keepdims=True), 1e-30)
        code = jnp.ceil(jnp.log2(largest) * LOG_STEPS + 0.01)
        scaled = product * jnp.exp2(15.0 - HEADROOM - code * (1.0 / LOG_STEPS))
        owner = divide(slot, SLOTS)
        coded[k] = jnp.round(scaled).astype(jnp.int32).astype(jnp.int16)
        stats[owner, pl.ds(slot - owner * SLOTS, 1), :] = code

    fars = lists[0, limit + 1]
    nears = lists[0, limit + 2]
    for k in range(far_limit):
        encode(k, far[lists[2, k]])
    lax.fori_loop(0, fars, begin, 0)
    for k in range(far_limit, limit):
        encode(k, held_near[lists[2, k]])
    lax.fori_loop(far_limit, nears, begin, 0)

    term = jnp.sum(squares) * (1.0 / (2.0 * samples_dev)) - jnp.sum(logs[0:1, :])
    term = jnp.full((1, edge), term, jnp.float32)
    power = jnp.ceil(jnp.log2(jnp.maximum(jnp.abs(term), 1e-30)) + 0.01)
    scaled = term * jnp.exp2(14.0 - power)
    whole = jnp.round(scaled)
    digits = jnp.concatenate(
        [
            jnp.zeros((SLOTS, edge), jnp.float32),
            power,
            whole,
            jnp.round((scaled - whole) * FRACTION),
            jnp.zeros((STAT_ROWS - SLOTS - 3, edge), jnp.float32),
        ],
        axis=0,
    )
    tail[...] = (stats[...] + digits[None]).astype(jnp.int32).astype(jnp.int16)
    store_tail = pltpu.make_async_copy(
        tail, payload.at[:, pl.ds(SLOTS * edge, STAT_ROWS), :], sem_code.at[limit]
    )
    store_tail.start()
    lax.fori_loop(0, fars, finish, 0)
    lax.fori_loop(far_limit, nears, finish, 0)
    store_rows.wait()
    store_tail.wait()


def side_kernel(
    lists,
    x,
    omega,
    term,
    projected,
    off,
    far,
    near,
    result,
    moved,
    halves,
    *,
    rows_dev,
    devices,
    entries,
    edge,
    samples_dev,
):
    far_limit, near_limit = limits(entries, devices)
    on_diagonal = lax.broadcasted_iota(jnp.int32, (edge, edge), 0) == lax.broadcasted_iota(
        jnp.int32, (edge, edge), 1
    )

    def against(row, other):
        both = lax.dot_general(
            halves[row], other, (((1,), (1,)), ((), ())), preferred_element_type=jnp.float32
        )
        return both[:edge] + both[edge:]

    moved[...] = jnp.zeros(moved.shape, jnp.float32)
    halves[rows_dev] = jnp.zeros(halves.shape[1:], halves.dtype)
    for k in range(rows_dev):
        high, low = split_halves(projected[k])
        halves[k, :edge] = high
        halves[k, edge:] = low
        product = against(k, x[k])
        gradient = (product + product.T) * (1.0 / (2.0 * samples_dev))
        gradient = gradient + jnp.where(on_diagonal, term[k : k + 1, :], 0.0)
        value = omega[k] - STEP_SIZE * gradient
        result[k] = jnp.where(on_diagonal, value, soften(value, STEP_SIZE * PENALTY))

    def move(source, k, carry):
        e = lists[0, k]
        product = against(lists[1, k], source[lists[2, k]])
        moved[e] = off[jnp.minimum(e, entries - 1)] - product * (STEP_SIZE / (2.0 * samples_dev))
        return carry

    lax.fori_loop(0, far_limit, functools.partial(move, far), 0)
    lax.fori_loop(far_limit, far_limit + near_limit, functools.partial(move, near), 0)


def last_kernel(
    count,
    slots,
    moved,
    returned,
    result,
    objective,
    held,
    rt,
    rs,
    sem_in,
    sem_rt,
    sem_out,
    *,
    rows_dev,
    devices,
    entries,
    edge,
    samples_dev,
):
    live = live_count(count, rows_dev)

    def fetch(at, part):
        return pltpu.make_async_copy(moved.at[part], held.at[part], sem_in.at[at])

    def store(at, part):
        return pltpu.make_async_copy(rs.at[part], result.at[part], sem_out.at[at])

    width = max(k for k in range(1, 11) if entries % k == 0)
    parts = [(at, pl.ds(at * width, width)) for at in range(entries // width)]
    whole = pltpu.make_async_copy(returned, rt, sem_rt.at[0])
    whole.start()
    for at, part in parts:
        fetch(at, part).start()
    whole.wait()
    codes = rt[:, SLOTS * edge :, :].astype(jnp.int32).astype(jnp.float32)
    power = codes[:, SLOTS : SLOTS + 1]
    digits = codes[:, SLOTS + 1 : SLOTS + 2] + codes[:, SLOTS + 2 : SLOTS + 3] * (1.0 / FRACTION)
    total = jnp.sum(digits * jnp.exp2(power - 14.0), axis=0)
    objective[0] = jnp.max(total) * (1.0 / (devices * rows_dev * edge))
    for at, part in parts:
        fetch(at, part).wait()
        for e in range(at * width, (at + 1) * width):
            slot = slots[e]
            owner = divide(slot, SLOTS)
            rank = slot - owner * SLOTS
            codes = rt[owner, SLOTS * edge :, :].astype(jnp.int32).astype(jnp.float32)
            code = jnp.where(rank == 0, codes[0:1], codes[1:2])
            weight = jnp.exp2(code * (1.0 / LOG_STEPS) - (15.0 - HEADROOM)) * (
                STEP_SIZE / (2.0 * samples_dev)
            )
            weight = jnp.where(e < live, weight, 0.0)
            digits = rt[owner, pl.ds(pl.multiple_of(rank * edge, edge), edge), :]
            value = held[e] - digits.astype(jnp.int32).astype(jnp.float32) * weight
            rs[e] = soften(value, STEP_SIZE * PENALTY)
        store(at, part).start()
    for at, part in parts:
        store(at, part).wait()


def layer_of(mesh):
    spots = [getattr(d, "coords", None) for d in mesh.devices.reshape(-1, mesh.shape["rows"])[0]]
    best = 1
    for axis in range(3) if None not in spots else ():
        places = [spot[axis] for spot in spots]
        count = len(set(places))
        runs = 1 + sum(a != b for a, b in zip(places, places[1:]))
        if runs == count and count % 2 == 0:
            best = max(best, len(places) // count)
    return best


def shards(samples, omega_diag, omega_off, pattern, block_count, diag_term, *, layer):
    devices = lax.axis_size("rows")
    rows_dev, edge = omega_diag.shape[:2]
    samples_dev = samples.shape[1]
    entries = omega_off.shape[0]
    f32 = jnp.float32
    x = samples.reshape(rows_dev, edge, samples_dev)
    term = diag_term.reshape(rows_dev, edge)
    pattern = pattern.T
    smem = pl.BlockSpec(memory_space=pltpu.SMEM)
    vmem = pl.BlockSpec(memory_space=pltpu.VMEM)
    hbm = pl.BlockSpec(memory_space=pltpu.HBM)
    params = pltpu.CompilerParams(vmem_limit_bytes=VMEM_LIMIT)
    alone = pltpu.CompilerParams(vmem_limit_bytes=VMEM_ALONE)
    sizes = dict(rows_dev=rows_dev, entries=entries, edge=edge)
    every = dict(sizes, devices=devices, samples_dev=samples_dev)
    held = functools.partial(pltpu.with_memory_space_constraint, memory_space=pltpu.VMEM)
    kept = functools.partial(pltpu.with_memory_space_constraint, memory_space=pltpu.HBM)

    dma = pltpu.SemaphoreType.DMA

    half = devices // 2
    far_limit, near_limit = limits(entries, devices)
    limit = far_limit + near_limit
    across = [(o, mirror(o, devices, layer)) for o in range(devices)]
    steps = devices // layer
    outer = [(o, m) for o, m in across if 4 * abs(2 * (o // layer) + 1 - steps) > 2 * steps]
    inner = [pair for pair in across if pair not in outer]
    halves = [list(range(half)), list(range(half, devices))]

    other_pattern = lax.ppermute(kept(pattern), "rows", across)
    from_outer = lax.ppermute(kept(x), "rows", outer)

    ints = [pltpu.SMEM((entries,), jnp.int32), pltpu.SMEM((devices,), jnp.int32)]
    places = dict(rows_dev=rows_dev, devices=devices, entries=entries)
    send = pl.pallas_call(
        functools.partial(pack_kernel, **places),
        out_shape=pltpu.HBM((SLOTS * half, edge, samples_dev), samples.dtype),
        in_specs=[smem, hbm],
        out_specs=hbm,
        scratch_shapes=[
            *ints,
            pltpu.SMEM((2, entries + 1), jnp.int32),
            pltpu.VMEM((rows_dev, edge, samples_dev), samples.dtype),
            dma((1,)),
            dma((near_limit + 1,)),
        ],
        compiler_params=alone,
        name="pack",
    )(pattern, kept(x))

    slots, lists, wanted = pl.pallas_call(
        functools.partial(plan_kernel, layer=layer, **places),
        out_shape=(
            jax.ShapeDtypeStruct((entries,), jnp.int32),
            jax.ShapeDtypeStruct((4, limit + 3), jnp.int32),
            jax.ShapeDtypeStruct((SLOTS * half + 1,), jnp.int32),
        ),
        in_specs=[smem, smem],
        out_specs=(smem, smem, smem),
        scratch_shapes=ints,
        compiler_params=params,
        name="plan",
    )(pattern, other_pattern)

    def within(blocks):
        return lax.all_to_all(
            blocks.reshape(half, SLOTS, edge, samples_dev),
            "rows",
            split_axis=0,
            concat_axis=0,
            axis_index_groups=halves,
            tiled=True,
        ).reshape(SLOTS * half, edge, samples_dev)

    near = within(send)
    from_inner = lax.ppermute(kept(x), "rows", inner)

    passed = pl.pallas_call(
        functools.partial(relay_kernel, devices=devices),
        out_shape=pltpu.HBM((SLOTS * half, edge, samples_dev), samples.dtype),
        in_specs=[smem, vmem, vmem],
        out_specs=hbm,
        scratch_shapes=[
            pltpu.VMEM((rows_dev, edge, samples_dev), samples.dtype),
            dma((SLOTS * half,)),
        ],
        compiler_params=params,
        name="relay",
    )(wanted, held(from_outer), held(from_inner))
    far = within(passed)

    own, logs, wide = pl.pallas_call(
        functools.partial(own_kernel, devices=devices, **sizes),
        out_shape=(
            pltpu.HBM((rows_dev + 1, edge, samples_dev), f32),
            jax.ShapeDtypeStruct((8, edge), f32),
            pltpu.HBM((far_limit, edge, 2 * edge), jnp.bfloat16),
        ),
        in_specs=[smem] + [vmem] * 4,
        out_specs=(vmem, vmem, vmem),
        compiler_params=params,
        cost_estimate=pl.CostEstimate(
            flops=12 * rows_dev * edge * edge * samples_dev, transcendentals=0, bytes_accessed=1 << 23
        ),
        name="own",
    )(lists, x, omega_diag, omega_off, near)

    payload, projected = pl.pallas_call(
        functools.partial(main_kernel, **every),
        out_shape=(
            pltpu.HBM((devices, SLOTS * edge + STAT_ROWS, edge), jnp.int16),
            pltpu.HBM((rows_dev, edge, samples_dev), f32),
        ),
        in_specs=[smem, vmem, vmem, hbm, hbm, hbm],
        out_specs=(hbm, hbm),
        scratch_shapes=[
            pltpu.VMEM((SLOTS * half, edge, samples_dev), samples.dtype),
            pltpu.VMEM((far_limit, edge, 2 * edge), jnp.bfloat16),
            pltpu.VMEM((rows_dev, edge, samples_dev), f32),
            pltpu.VMEM((rows_dev + 1, edge, samples_dev), f32),
            pltpu.VMEM((rows_dev + 1, 2 * edge, samples_dev), jnp.bfloat16),
            pltpu.VMEM((limit, edge, edge), jnp.int16),
            pltpu.VMEM((devices, STAT_ROWS, edge), f32),
            pltpu.VMEM((devices, STAT_ROWS, edge), jnp.int16),
            dma((1,)),
            dma((2,)),
            dma((1,)),
            dma((1,)),
            dma((limit + 1,)),
        ],
        compiler_params=params,
        name="main",
    )(lists, logs, held(far), kept(near), kept(own), kept(wide))

    returned = lax.all_to_all(kept(payload), "rows", split_axis=0, concat_axis=0, tiled=True)

    diag_next, moved = pl.pallas_call(
        functools.partial(side_kernel, **every),
        out_shape=(
            jax.ShapeDtypeStruct((rows_dev, edge, edge), f32),
            pltpu.HBM((entries + 1, edge, edge), f32),
        ),
        in_specs=[smem] + [vmem] * 7,
        out_specs=(vmem, vmem),
        scratch_shapes=[pltpu.VMEM((rows_dev + 1, 2 * edge, samples_dev), jnp.bfloat16)],
        compiler_params=params,
        cost_estimate=pl.CostEstimate(
            flops=12 * rows_dev * edge * edge * samples_dev, transcendentals=0, bytes_accessed=1 << 23
        ),
        name="side",
    )(lists, x, omega_diag, term, projected, omega_off, far, near)

    off_next, objective = pl.pallas_call(
        functools.partial(last_kernel, **every),
        out_shape=(
            jax.ShapeDtypeStruct((entries, edge, edge), f32),
            jax.ShapeDtypeStruct((1,), f32),
        ),
        in_specs=[smem, smem, hbm, hbm],
        out_specs=(hbm, smem),
        scratch_shapes=[
            pltpu.VMEM((entries, edge, edge), f32),
            pltpu.VMEM((devices, SLOTS * edge + STAT_ROWS, edge), jnp.int16),
            pltpu.VMEM((entries, edge, edge), f32),
            dma((entries,)),
            dma((1,)),
            dma((entries,)),
        ],
        compiler_params=alone,
        name="last",
    )(block_count, slots, kept(moved), kept(returned))
    return diag_next, off_next, objective


def solution(mesh):
    return jax.shard_map(
        functools.partial(shards, layer=layer_of(mesh)),
        mesh=mesh,
        in_specs=(
            P(("groups", "rows"), None),
            P(("groups", "rows"), None, None),
            P(("groups", "rows"), None, None),
            P(("groups", "rows"), None),
            P(("groups", "rows")),
            P(("groups", "rows")),
        ),
        out_specs=(
            P(("groups", "rows"), None, None),
            P(("groups", "rows"), None, None),
            P("groups"),
        ),
        check_vma=False,
    )
```

```python
import functools

import jax
import jax.numpy as jnp
from jax import lax
from jax.experimental import pallas as pl
from jax.experimental.pallas import tpu as pltpu
from jax.sharding import PartitionSpec as P


SLOTS = 2
STAT_ROWS = 8
STEP_SIZE = 0.5
PENALTY = 0.01
LOG_STEPS = 128.0
HEADROOM = 1e-4
FRACTION = 32000.0
VMEM_LIMIT = 40 * 1024 * 1024
VMEM_ALONE = 60 * 1024 * 1024


def soften(values, level):
    return values - jnp.clip(values, -level, level)


def split_halves(values):
    high = values.astype(jnp.bfloat16)
    low = (values - high.astype(jnp.float32)).astype(jnp.bfloat16)
    return high, low


def divide(value, by):
    if isinstance(value, int) or by & (by - 1):
        return value // by
    return lax.shift_right_logical(value, by.bit_length() - 1)


def mirror(o, devices, layer):
    return o + (devices - layer) - 2 * layer * divide(o, layer)


def limits(entries, devices):
    half = devices // 2
    return min(entries, SLOTS * half), min(entries, SLOTS * (half - 1))


def live_count(count, rows_dev):
    total = count[0]
    for k in range(1, rows_dev):
        total = total + count[k]
    return total


def place(pattern, keys, sums, visit, *, rows_dev, devices, entries):
    position = divide(pattern[0, 0], rows_dev)
    block_total = rows_dev * devices
    for o in range(devices):
        sums[o] = 0
    for e in range(entries):
        i = pattern[0, e]
        j = pattern[1, e]
        owner = divide(j, rows_dev)
        key = jnp.minimum(i * block_total + j, j * block_total + i)
        keys[e] = key
        sums[owner] = sums[owner] + key
    for e in range(entries):
        owner = divide(pattern[1, e], rows_dev)
        later = jnp.where(2 * keys[e] > sums[owner], 1, 0)
        visit(e, pattern[0, e] - position * rows_dev, owner, later, owner != position)


def pack_kernel(
    pattern,
    x,
    send,
    keys,
    sums,
    picks,
    asked,
    held,
    tiles,
    sem_x,
    sems,
    *,
    rows_dev,
    devices,
    layer,
    entries,
    edge,
):
    half = devices // 2
    near_limit = limits(entries, devices)[1]
    fetch = pltpu.make_async_copy(x, held, sem_x.at[0])
    fetch.start()
    position = divide(pattern[0, 0], rows_dev)
    first = divide(position, half) * half
    spare = pltpu.make_async_copy(
        held.at[0], send.at[position - first, pl.ds(0, edge)], sems.at[near_limit]
    )
    total = [jnp.int32(0)]
    for q in range(SLOTS * half):
        asked[q] = 0

    def visit(e, row, owner, later, alive):
        index = owner - first
        near = (index >= 0) & (index < half)
        picks[0, total[0]] = row
        picks[1, total[0]] = index
        picks[2, total[0]] = later
        total[0] = total[0] + jnp.where(alive & near, 1, 0)
        relay = (mirror(owner, devices, layer) - first) * SLOTS + later
        asked[jnp.where(near, SLOTS * half, relay)] = pattern[1, e] - owner * rows_dev

    place(pattern, keys, sums, visit, rows_dev=rows_dev, devices=devices, entries=entries)
    at = lax.broadcasted_iota(jnp.int32, tiles.shape[1:], 0)
    for q in range(half):
        tile = jnp.zeros(at.shape, jnp.int32)
        for rank in range(SLOTS):
            tile = jnp.where(at == rank, asked[q * SLOTS + rank], tile)
        tiles[q] = tile.astype(jnp.float32).astype(jnp.bfloat16)
    tell = pltpu.make_async_copy(
        tiles, send.at[:, pl.ds(SLOTS * edge, STAT_ROWS), :], sems.at[near_limit + 1]
    )
    tell.start()

    def copy(k):
        rank = pl.multiple_of(picks[2, k] * edge, edge)
        return pltpu.make_async_copy(
            held.at[picks[0, k]], send.at[picks[1, k], pl.ds(rank, edge)], sems.at[k]
        )

    def begin(k, carry):
        copy(k).start()
        return carry

    def finish(k, carry):
        copy(k).wait()
        return carry

    fetch.wait()
    spare.start()
    lax.fori_loop(0, total[0], begin, 0)
    spare.wait()
    tell.wait()
    lax.fori_loop(0, total[0], finish, 0)


def near_block(near, at, edge):
    peer = divide(at, SLOTS)
    return near[peer, pl.ds(pl.multiple_of((at - peer * SLOTS) * edge, edge), edge), :]


def plan_kernel(pattern, slots, lists, keys, sums, *, rows_dev, devices, layer, entries):
    half = devices // 2
    far_limit, near_limit = limits(entries, devices)
    limit = far_limit + near_limit
    position = divide(pattern[0, 0], rows_dev)
    first = divide(position, half) * half
    for k in range(limit):
        lists[0, k] = entries
        lists[1, k] = rows_dev
        lists[2, k] = (position - first) * SLOTS if k >= far_limit else 0
        lists[3, k] = position * SLOTS
    tops = [jnp.int32(0), jnp.int32(far_limit)]

    def visit(e, row, owner, later, alive):
        later = jnp.where(alive, later, 0)
        slot = owner * SLOTS + later
        slots[e] = slot
        index = owner - first
        near = (index >= 0) & (index < half)
        across = mirror(owner, devices, layer) - first
        at = jnp.where(alive, jnp.where(near, tops[1], tops[0]), limit)
        lists[0, at] = e
        lists[1, at] = row
        lists[2, at] = jnp.where(near, index, across) * SLOTS + later
        lists[3, at] = slot
        tops[0] = tops[0] + jnp.where(alive & ~near, 1, 0)
        tops[1] = tops[1] + jnp.where(alive & near, 1, 0)

    place(pattern, keys, sums, visit, rows_dev=rows_dev, devices=devices, entries=entries)
    lists[0, limit + 1] = tops[0]
    lists[0, limit + 2] = tops[1]


def relay_kernel(near, outer, inner, send, x, sems, *, devices, edge):
    x[...] = outer[...] + inner[...]
    copies = []
    for q in range(devices // 2):
        tile = near[q, SLOTS * edge :, :].astype(jnp.float32)
        for rank in range(SLOTS):
            row = jnp.max(tile[rank : rank + 1, :128]).astype(jnp.int32)
            row = jnp.clip(row, 0, x.shape[0] - 1)
            at = q * SLOTS + rank
            copies.append(pltpu.make_async_copy(x.at[row], send.at[at], sems.at[at]))
            copies[-1].start()
    for copy in copies:
        copy.wait()


def own_kernel(lists, x, omega, off, near, projected, logs, wide, *, rows_dev, devices, entries, edge):
    far_limit, near_limit = limits(entries, devices)
    on_diagonal = lax.broadcasted_iota(jnp.int32, (edge, edge), 0) == lax.broadcasted_iota(
        jnp.int32, (edge, edge), 1
    )

    def apply(block, rows):
        high, low = split_halves(block)
        return jnp.dot(
            jnp.concatenate([high, low], axis=1),
            jnp.concatenate([rows, rows], axis=0),
            preferred_element_type=jnp.float32,
        )

    total = jnp.zeros((1, edge), jnp.float32)
    for k in range(rows_dev):
        projected[k] = apply(omega[k], x[k])
        total = total + jnp.log(
            jnp.sum(jnp.where(on_diagonal, omega[k], 0.0), axis=0, keepdims=True)
        )
    projected[rows_dev] = jnp.zeros(projected.shape[1:], jnp.float32)
    logs[...] = jnp.broadcast_to(total, logs.shape)

    def add(k, carry):
        row = lists[1, k]
        block = off[jnp.minimum(lists[0, k], entries - 1)]
        projected[row] = projected[row] + apply(block, near_block(near, lists[2, k], edge))
        return carry

    lax.fori_loop(far_limit, far_limit + near_limit, add, 0)

    def widen(k, carry):
        high, low = split_halves(off[jnp.minimum(lists[0, k], entries - 1)])
        wide[k, :, :edge] = high
        wide[k, :, edge:] = low
        return carry

    lax.fori_loop(0, far_limit, widen, 0)


def main_kernel(
    lists,
    logs,
    far,
    near,
    own,
    wide,
    payload,
    projected,
    held_near,
    held_wide,
    held_own,
    held_rows,
    halves,
    coded,
    stats,
    tail,
    sem_near,
    sem_wide,
    sem_own,
    sem_rows,
    sem_code,
    *,
    rows_dev,
    devices,
    entries,
    edge,
    samples_dev,
):
    far_limit, near_limit = limits(entries, devices)
    limit = far_limit + near_limit
    split = far_limit // 4
    parts = (pl.ds(0, split), pl.ds(split, far_limit - split))
    fetches = [
        pltpu.make_async_copy(wide.at[part], held_wide.at[part], sem_wide.at[at])
        for at, part in enumerate(parts)
    ]
    fetch_own = pltpu.make_async_copy(own.at[pl.ds(0, rows_dev)], held_own, sem_own.at[0])
    fetch_near = pltpu.make_async_copy(near, held_near, sem_near.at[0])
    for fetch in (*fetches, fetch_own, fetch_near):
        fetch.start()
    held_rows[...] = jnp.zeros(held_rows.shape, jnp.float32)
    stats[...] = jnp.zeros(stats.shape, jnp.float32)
    halves[rows_dev] = jnp.zeros(halves.shape[1:], halves.dtype)

    total = jnp.zeros((edge, samples_dev), jnp.float32)
    for k in range(far_limit):
        if k == 0:
            fetches[0].wait()
        if k == split:
            fetches[1].wait()
        rows = far[lists[2, k]]
        part = jnp.dot(
            held_wide[k],
            jnp.concatenate([rows, rows], axis=0),
            preferred_element_type=jnp.float32,
        )
        row = lists[1, k]
        total = part if k == 0 else jnp.where(row == lists[1, k - 1], total, 0.0) + part
        held_rows[row] = total

    fetch_own.wait()
    squares = jnp.zeros((8, samples_dev), jnp.float32)
    for k in range(rows_dev):
        values = held_rows[k] + held_own[k]
        held_own[k] = values
        squares = squares + jnp.sum((values * values).reshape(edge // 8, 8, samples_dev), axis=0)
        high, low = split_halves(values)
        halves[k, :edge] = high
        halves[k, edge:] = low
    store_rows = pltpu.make_async_copy(held_own, projected, sem_rows.at[0])
    store_rows.start()
    fetch_near.wait()

    def store(k):
        slot = lists[3, k]
        owner = divide(slot, SLOTS)
        rank = slot - owner * SLOTS
        return pltpu.make_async_copy(
            coded.at[k],
            payload.at[owner, pl.ds(pl.multiple_of(rank * edge, edge), edge), :],
            sem_code.at[k],
        )

    def begin(k, carry):
        store(k).start()
        return carry

    def finish(k, carry):
        store(k).wait()
        return carry

    def encode(k, rows):
        slot = lists[3, k]
        both = lax.dot_general(
            rows,
            halves[lists[1, k]],
            (((1,), (1,)), ((), ())),
            preferred_element_type=jnp.float32,
        )
        product = both[:, :edge] + both[:, edge:]
        largest = jnp.maximum(jnp.max(jnp.abs(product), axis=0, keepdims=True), 1e-30)
        code = jnp.ceil(jnp.log2(largest) * LOG_STEPS + 0.01)
        scaled = product * jnp.exp2(15.0 - HEADROOM - code * (1.0 / LOG_STEPS))
        owner = divide(slot, SLOTS)
        coded[k] = jnp.round(scaled).astype(jnp.int32).astype(jnp.int16)
        stats[owner, pl.ds(slot - owner * SLOTS, 1), :] = code

    fars = lists[0, limit + 1]
    nears = lists[0, limit + 2]
    for k in range(far_limit):
        encode(k, far[lists[2, k]])
    lax.fori_loop(0, fars, begin, 0)
    for k in range(far_limit, limit):
        encode(k, near_block(held_near, lists[2, k], edge))
    lax.fori_loop(far_limit, nears, begin, 0)

    term = jnp.sum(squares) * (1.0 / (2.0 * samples_dev)) - jnp.sum(logs[0:1, :])
    term = jnp.full((1, edge), term, jnp.float32)
    power = jnp.ceil(jnp.log2(jnp.maximum(jnp.abs(term), 1e-30)) + 0.01)
    scaled = term * jnp.exp2(14.0 - power)
    whole = jnp.round(scaled)
    digits = jnp.concatenate(
        [
            jnp.zeros((SLOTS, edge), jnp.float32),
            power,
            whole,
            jnp.round((scaled - whole) * FRACTION),
            jnp.zeros((STAT_ROWS - SLOTS - 3, edge), jnp.float32),
        ],
        axis=0,
    )
    tail[...] = (stats[...] + digits[None]).astype(jnp.int32).astype(jnp.int16)
    store_tail = pltpu.make_async_copy(
        tail, payload.at[:, pl.ds(SLOTS * edge, STAT_ROWS), :], sem_code.at[limit]
    )
    store_tail.start()
    lax.fori_loop(0, fars, finish, 0)
    lax.fori_loop(far_limit, nears, finish, 0)
    store_rows.wait()
    store_tail.wait()


def side_kernel(
    lists,
    x,
    omega,
    term,
    projected,
    off,
    far,
    near,
    result,
    moved,
    halves,
    *,
    rows_dev,
    devices,
    entries,
    edge,
    samples_dev,
):
    far_limit, near_limit = limits(entries, devices)
    on_diagonal = lax.broadcasted_iota(jnp.int32, (edge, edge), 0) == lax.broadcasted_iota(
        jnp.int32, (edge, edge), 1
    )

    def against(row, other):
        both = lax.dot_general(
            halves[row], other, (((1,), (1,)), ((), ())), preferred_element_type=jnp.float32
        )
        return both[:edge] + both[edge:]

    moved[...] = jnp.zeros(moved.shape, jnp.float32)
    halves[rows_dev] = jnp.zeros(halves.shape[1:], halves.dtype)
    for k in range(rows_dev):
        high, low = split_halves(projected[k])
        halves[k, :edge] = high
        halves[k, edge:] = low
        product = against(k, x[k])
        gradient = (product + product.T) * (1.0 / (2.0 * samples_dev))
        gradient = gradient + jnp.where(on_diagonal, term[k : k + 1, :], 0.0)
        value = omega[k] - STEP_SIZE * gradient
        result[k] = jnp.where(on_diagonal, value, soften(value, STEP_SIZE * PENALTY))

    def move(block, k, carry):
        e = lists[0, k]
        product = against(lists[1, k], block(lists[2, k]))
        moved[e] = off[jnp.minimum(e, entries - 1)] - product * (STEP_SIZE / (2.0 * samples_dev))
        return carry

    lax.fori_loop(0, far_limit, functools.partial(move, lambda at: far[at]), 0)
    lax.fori_loop(
        far_limit,
        far_limit + near_limit,
        functools.partial(move, lambda at: near_block(near, at, edge)),
        0,
    )


def last_kernel(
    count,
    slots,
    moved,
    returned,
    result,
    objective,
    held,
    rt,
    rs,
    sem_in,
    sem_rt,
    sem_out,
    *,
    rows_dev,
    devices,
    entries,
    edge,
    samples_dev,
):
    live = live_count(count, rows_dev)

    def fetch(at, part):
        return pltpu.make_async_copy(moved.at[part], held.at[part], sem_in.at[at])

    def store(at, part):
        return pltpu.make_async_copy(rs.at[part], result.at[part], sem_out.at[at])

    width = max(k for k in range(1, 11) if entries % k == 0)
    parts = [(at, pl.ds(at * width, width)) for at in range(entries // width)]
    whole = pltpu.make_async_copy(returned, rt, sem_rt.at[0])
    whole.start()
    for at, part in parts:
        fetch(at, part).start()
    whole.wait()
    codes = rt[:, SLOTS * edge :, :].astype(jnp.int32).astype(jnp.float32)
    power = codes[:, SLOTS : SLOTS + 1]
    digits = codes[:, SLOTS + 1 : SLOTS + 2] + codes[:, SLOTS + 2 : SLOTS + 3] * (1.0 / FRACTION)
    total = jnp.sum(digits * jnp.exp2(power - 14.0), axis=0)
    objective[0] = jnp.max(total) * (1.0 / (devices * rows_dev * edge))
    for at, part in parts:
        fetch(at, part).wait()
        for e in range(at * width, (at + 1) * width):
            slot = slots[e]
            owner = divide(slot, SLOTS)
            rank = slot - owner * SLOTS
            codes = rt[owner, SLOTS * edge :, :].astype(jnp.int32).astype(jnp.float32)
            code = jnp.where(rank == 0, codes[0:1], codes[1:2])
            weight = jnp.exp2(code * (1.0 / LOG_STEPS) - (15.0 - HEADROOM)) * (
                STEP_SIZE / (2.0 * samples_dev)
            )
            weight = jnp.where(e < live, weight, 0.0)
            digits = rt[owner, pl.ds(pl.multiple_of(rank * edge, edge), edge), :]
            value = held[e] - digits.astype(jnp.int32).astype(jnp.float32) * weight
            rs[e] = soften(value, STEP_SIZE * PENALTY)
        store(at, part).start()
    for at, part in parts:
        store(at, part).wait()


def layer_of(mesh):
    spots = [getattr(d, "coords", None) for d in mesh.devices.reshape(-1, mesh.shape["rows"])[0]]
    best = 1
    for axis in range(3) if None not in spots else ():
        places = [spot[axis] for spot in spots]
        count = len(set(places))
        runs = 1 + sum(a != b for a, b in zip(places, places[1:]))
        if runs == count and count % 2 == 0:
            best = max(best, len(places) // count)
    return best


def shards(samples, omega_diag, omega_off, pattern, block_count, diag_term, *, layer):
    devices = lax.axis_size("rows")
    rows_dev, edge = omega_diag.shape[:2]
    samples_dev = samples.shape[1]
    entries = omega_off.shape[0]
    f32 = jnp.float32
    x = samples.reshape(rows_dev, edge, samples_dev)
    term = diag_term.reshape(rows_dev, edge)
    pattern = pattern.T
    smem = pl.BlockSpec(memory_space=pltpu.SMEM)
    vmem = pl.BlockSpec(memory_space=pltpu.VMEM)
    hbm = pl.BlockSpec(memory_space=pltpu.HBM)
    params = pltpu.CompilerParams(vmem_limit_bytes=VMEM_LIMIT)
    alone = pltpu.CompilerParams(vmem_limit_bytes=VMEM_ALONE)
    sizes = dict(rows_dev=rows_dev, entries=entries, edge=edge)
    every = dict(sizes, devices=devices, samples_dev=samples_dev)
    held = functools.partial(pltpu.with_memory_space_constraint, memory_space=pltpu.VMEM)
    kept = functools.partial(pltpu.with_memory_space_constraint, memory_space=pltpu.HBM)

    dma = pltpu.SemaphoreType.DMA

    half = devices // 2
    far_limit, near_limit = limits(entries, devices)
    limit = far_limit + near_limit
    across = [(o, mirror(o, devices, layer)) for o in range(devices)]
    steps = devices // layer
    outer = [(o, m) for o, m in across if 4 * abs(2 * (o // layer) + 1 - steps) > 2 * steps]
    inner = [pair for pair in across if pair not in outer]
    halves = [list(range(half)), list(range(half, devices))]

    from_outer = lax.ppermute(kept(x), "rows", outer)

    ints = [pltpu.SMEM((entries,), jnp.int32), pltpu.SMEM((devices,), jnp.int32)]
    places = dict(rows_dev=rows_dev, devices=devices, entries=entries)
    near_rows = SLOTS * edge + STAT_ROWS
    send = pl.pallas_call(
        functools.partial(pack_kernel, layer=layer, edge=edge, **places),
        out_shape=pltpu.HBM((half, near_rows, samples_dev), samples.dtype),
        in_specs=[smem, hbm],
        out_specs=hbm,
        scratch_shapes=[
            *ints,
            pltpu.SMEM((3, entries + 1), jnp.int32),
            pltpu.SMEM((SLOTS * half + 1,), jnp.int32),
            pltpu.VMEM((rows_dev, edge, samples_dev), samples.dtype),
            pltpu.VMEM((half, STAT_ROWS, samples_dev), samples.dtype),
            dma((1,)),
            dma((near_limit + 2,)),
        ],
        compiler_params=alone,
        name="pack",
    )(pattern, kept(x))

    slots, lists = pl.pallas_call(
        functools.partial(plan_kernel, layer=layer, **places),
        out_shape=(
            jax.ShapeDtypeStruct((entries,), jnp.int32),
            jax.ShapeDtypeStruct((4, limit + 3), jnp.int32),
        ),
        in_specs=[smem],
        out_specs=(smem, smem),
        scratch_shapes=ints,
        compiler_params=params,
        name="plan",
    )(pattern)

    def within(blocks):
        return lax.all_to_all(
            blocks, "rows", split_axis=0, concat_axis=0, axis_index_groups=halves, tiled=True
        )

    near = within(send)
    from_inner = lax.ppermute(kept(x), "rows", inner)

    passed = pl.pallas_call(
        functools.partial(relay_kernel, devices=devices, edge=edge),
        out_shape=pltpu.HBM((SLOTS * half, edge, samples_dev), samples.dtype),
        in_specs=[vmem, vmem, vmem],
        out_specs=hbm,
        scratch_shapes=[
            pltpu.VMEM((rows_dev, edge, samples_dev), samples.dtype),
            dma((SLOTS * half,)),
        ],
        compiler_params=params,
        name="relay",
    )(held(near), held(from_outer), held(from_inner))
    far = within(passed.reshape(half, SLOTS, edge, samples_dev))
    far = far.reshape(SLOTS * half, edge, samples_dev)

    own, logs, wide = pl.pallas_call(
        functools.partial(own_kernel, devices=devices, **sizes),
        out_shape=(
            pltpu.HBM((rows_dev + 1, edge, samples_dev), f32),
            jax.ShapeDtypeStruct((8, edge), f32),
            pltpu.HBM((far_limit, edge, 2 * edge), jnp.bfloat16),
        ),
        in_specs=[smem] + [vmem] * 4,
        out_specs=(vmem, vmem, vmem),
        compiler_params=params,
        cost_estimate=pl.CostEstimate(
            flops=12 * rows_dev * edge * edge * samples_dev, transcendentals=0, bytes_accessed=1 << 23
        ),
        name="own",
    )(lists, x, omega_diag, omega_off, near)

    payload, projected = pl.pallas_call(
        functools.partial(main_kernel, **every),
        out_shape=(
            pltpu.HBM((devices, SLOTS * edge + STAT_ROWS, edge), jnp.int16),
            pltpu.HBM((rows_dev, edge, samples_dev), f32),
        ),
        in_specs=[smem, vmem, vmem, hbm, hbm, hbm],
        out_specs=(hbm, hbm),
        scratch_shapes=[
            pltpu.VMEM((half, near_rows, samples_dev), samples.dtype),
            pltpu.VMEM((far_limit, edge, 2 * edge), jnp.bfloat16),
            pltpu.VMEM((rows_dev, edge, samples_dev), f32),
            pltpu.VMEM((rows_dev + 1, edge, samples_dev), f32),
            pltpu.VMEM((rows_dev + 1, 2 * edge, samples_dev), jnp.bfloat16),
            pltpu.VMEM((limit, edge, edge), jnp.int16),
            pltpu.VMEM((devices, STAT_ROWS, edge), f32),
            pltpu.VMEM((devices, STAT_ROWS, edge), jnp.int16),
            dma((1,)),
            dma((2,)),
            dma((1,)),
            dma((1,)),
            dma((limit + 1,)),
        ],
        compiler_params=params,
        name="main",
    )(lists, logs, held(far), kept(near), kept(own), kept(wide))

    returned = lax.all_to_all(kept(payload), "rows", split_axis=0, concat_axis=0, tiled=True)

    diag_next, moved = pl.pallas_call(
        functools.partial(side_kernel, **every),
        out_shape=(
            jax.ShapeDtypeStruct((rows_dev, edge, edge), f32),
            pltpu.HBM((entries + 1, edge, edge), f32),
        ),
        in_specs=[smem] + [vmem] * 7,
        out_specs=(vmem, vmem),
        scratch_shapes=[pltpu.VMEM((rows_dev + 1, 2 * edge, samples_dev), jnp.bfloat16)],
        compiler_params=params,
        cost_estimate=pl.CostEstimate(
            flops=12 * rows_dev * edge * edge * samples_dev, transcendentals=0, bytes_accessed=1 << 23
        ),
        name="side",
    )(lists, x, omega_diag, term, projected, omega_off, far, near)

    off_next, objective = pl.pallas_call(
        functools.partial(last_kernel, **every),
        out_shape=(
            jax.ShapeDtypeStruct((entries, edge, edge), f32),
            jax.ShapeDtypeStruct((1,), f32),
        ),
        in_specs=[smem, smem, hbm, hbm],
        out_specs=(hbm, smem),
        scratch_shapes=[
            pltpu.VMEM((entries, edge, edge), f32),
            pltpu.VMEM((devices, SLOTS * edge + STAT_ROWS, edge), jnp.int16),
            pltpu.VMEM((entries, edge, edge), f32),
            dma((entries,)),
            dma((1,)),
            dma((entries,)),
        ],
        compiler_params=alone,
        name="last",
    )(block_count, slots, kept(moved), kept(returned))
    return diag_next, off_next, objective


def solution(mesh):
    return jax.shard_map(
        functools.partial(shards, layer=layer_of(mesh)),
        mesh=mesh,
        in_specs=(
            P(("groups", "rows"), None),
            P(("groups", "rows"), None, None),
            P(("groups", "rows"), None, None),
            P(("groups", "rows"), None),
            P(("groups", "rows")),
            P(("groups", "rows")),
        ),
        out_specs=(
            P(("groups", "rows"), None, None),
            P(("groups", "rows"), None, None),
            P("groups"),
        ),
        check_vma=False,
    )
```

```python
import functools

import jax
import jax.numpy as jnp
from jax import lax
from jax.experimental import pallas as pl
from jax.experimental.pallas import tpu as pltpu
from jax.sharding import PartitionSpec as P


SLOTS = 2
STAT_ROWS = 8
STEP_SIZE = 0.5
PENALTY = 0.01
LOG_STEPS = 128.0
HEADROOM = 1e-4
FRACTION = 32000.0
VMEM_LIMIT = 40 * 1024 * 1024
VMEM_ALONE = 60 * 1024 * 1024


def soften(values, level):
    return values - jnp.clip(values, -level, level)


def split_halves(values):
    high = values.astype(jnp.bfloat16)
    low = (values - high.astype(jnp.float32)).astype(jnp.bfloat16)
    return high, low


def divide(value, by):
    if isinstance(value, int) or by & (by - 1):
        return value // by
    return lax.shift_right_logical(value, by.bit_length() - 1)


def mirror(o, devices, layer):
    return o + (devices - layer) - 2 * layer * divide(o, layer)


def limits(entries, devices):
    half = devices // 2
    return min(entries, SLOTS * half), min(entries, SLOTS * (half - 1))


def place(pattern, keys, sums, visit, *, rows_dev, devices, entries):
    position = divide(pattern[0, 0], rows_dev)
    block_total = rows_dev * devices
    for o in range(devices):
        sums[o] = 0
    for e in range(entries):
        i = pattern[0, e]
        j = pattern[1, e]
        owner = divide(j, rows_dev)
        key = jnp.minimum(i * block_total + j, j * block_total + i)
        keys[e] = key
        sums[owner] = sums[owner] + key
    for e in range(entries):
        owner = divide(pattern[1, e], rows_dev)
        later = jnp.where(2 * keys[e] > sums[owner], 1, 0)
        visit(e, pattern[0, e] - position * rows_dev, owner, later, owner != position)


def pack_kernel(
    pattern,
    x,
    send,
    keys,
    sums,
    picks,
    asked,
    held,
    tiles,
    sem_x,
    sems,
    *,
    rows_dev,
    devices,
    layer,
    entries,
    edge,
):
    half = devices // 2
    near_limit = limits(entries, devices)[1]
    fetch = pltpu.make_async_copy(x, held, sem_x.at[0])
    fetch.start()
    position = divide(pattern[0, 0], rows_dev)
    first = divide(position, half) * half
    spare = pltpu.make_async_copy(
        held.at[0], send.at[position - first, pl.ds(0, edge)], sems.at[near_limit]
    )
    total = [jnp.int32(0)]
    for q in range(SLOTS * half):
        asked[q] = 0

    def visit(e, row, owner, later, alive):
        index = owner - first
        near = (index >= 0) & (index < half)
        picks[0, total[0]] = row
        picks[1, total[0]] = index
        picks[2, total[0]] = later
        total[0] = total[0] + jnp.where(alive & near, 1, 0)
        relay = (mirror(owner, devices, layer) - first) * SLOTS + later
        asked[jnp.where(near, SLOTS * half, relay)] = pattern[1, e] - owner * rows_dev

    place(pattern, keys, sums, visit, rows_dev=rows_dev, devices=devices, entries=entries)
    at = lax.broadcasted_iota(jnp.int32, tiles.shape[1:], 0)
    for q in range(half):
        tile = jnp.zeros(at.shape, jnp.int32)
        for rank in range(SLOTS):
            tile = jnp.where(at == rank, asked[q * SLOTS + rank], tile)
        tiles[q] = tile.astype(jnp.float32).astype(jnp.bfloat16)
    tell = pltpu.make_async_copy(
        tiles, send.at[:, pl.ds(SLOTS * edge, STAT_ROWS), :], sems.at[near_limit + 1]
    )
    tell.start()

    def copy(k):
        rank = pl.multiple_of(picks[2, k] * edge, edge)
        return pltpu.make_async_copy(
            held.at[picks[0, k]], send.at[picks[1, k], pl.ds(rank, edge)], sems.at[k]
        )

    def begin(k, carry):
        copy(k).start()
        return carry

    def finish(k, carry):
        copy(k).wait()
        return carry

    fetch.wait()
    spare.start()
    lax.fori_loop(0, total[0], begin, 0)
    spare.wait()
    tell.wait()
    lax.fori_loop(0, total[0], finish, 0)


def near_block(near, at, edge):
    peer = divide(at, SLOTS)
    return near[peer, pl.ds(pl.multiple_of((at - peer * SLOTS) * edge, edge), edge), :]


def plan_kernel(pattern, slots, lists, keys, sums, *, rows_dev, devices, layer, entries):
    half = devices // 2
    far_limit, near_limit = limits(entries, devices)
    limit = far_limit + near_limit
    position = divide(pattern[0, 0], rows_dev)
    first = divide(position, half) * half
    for k in range(limit):
        lists[0, k] = entries
        lists[1, k] = rows_dev
        lists[2, k] = (position - first) * SLOTS if k >= far_limit else 0
        lists[3, k] = position * SLOTS
    tops = [jnp.int32(0), jnp.int32(far_limit)]

    def visit(e, row, owner, later, alive):
        later = jnp.where(alive, later, 0)
        slot = owner * SLOTS + later
        slots[e] = jnp.where(alive, slot, -1)
        index = owner - first
        near = (index >= 0) & (index < half)
        across = mirror(owner, devices, layer) - first
        at = jnp.where(alive, jnp.where(near, tops[1], tops[0]), limit)
        lists[0, at] = e
        lists[1, at] = row
        lists[2, at] = jnp.where(near, index, across) * SLOTS + later
        lists[3, at] = slot
        tops[0] = tops[0] + jnp.where(alive & ~near, 1, 0)
        tops[1] = tops[1] + jnp.where(alive & near, 1, 0)

    place(pattern, keys, sums, visit, rows_dev=rows_dev, devices=devices, entries=entries)
    lists[0, limit + 1] = tops[0]
    lists[0, limit + 2] = tops[1]


def relay_kernel(near, outer, inner, send, x, sems, *, devices, edge):
    x[...] = outer[...] + inner[...]
    copies = []
    for q in range(devices // 2):
        tile = near[q, SLOTS * edge :, :].astype(jnp.float32)
        for rank in range(SLOTS):
            row = jnp.max(tile[rank : rank + 1, :128]).astype(jnp.int32)
            row = jnp.clip(row, 0, x.shape[0] - 1)
            at = q * SLOTS + rank
            copies.append(pltpu.make_async_copy(x.at[row], send.at[at], sems.at[at]))
            copies[-1].start()
    for copy in copies:
        copy.wait()


def own_kernel(lists, x, omega, off, near, projected, logs, wide, *, rows_dev, devices, entries, edge):
    far_limit, near_limit = limits(entries, devices)
    on_diagonal = lax.broadcasted_iota(jnp.int32, (edge, edge), 0) == lax.broadcasted_iota(
        jnp.int32, (edge, edge), 1
    )

    def apply(block, rows):
        high, low = split_halves(block)
        return jnp.dot(
            jnp.concatenate([high, low], axis=1),
            jnp.concatenate([rows, rows], axis=0),
            preferred_element_type=jnp.float32,
        )

    total = jnp.zeros((1, edge), jnp.float32)
    for k in range(rows_dev):
        projected[k] = apply(omega[k], x[k])
        total = total + jnp.log(
            jnp.sum(jnp.where(on_diagonal, omega[k], 0.0), axis=0, keepdims=True)
        )
    projected[rows_dev] = jnp.zeros(projected.shape[1:], jnp.float32)
    logs[...] = jnp.broadcast_to(total, logs.shape)

    def add(k, carry):
        row = lists[1, k]
        block = off[jnp.minimum(lists[0, k], entries - 1)]
        projected[row] = projected[row] + apply(block, near_block(near, lists[2, k], edge))
        return carry

    lax.fori_loop(far_limit, far_limit + near_limit, add, 0)

    def widen(k, carry):
        high, low = split_halves(off[jnp.minimum(lists[0, k], entries - 1)])
        wide[k, :, :edge] = high
        wide[k, :, edge:] = low
        return carry

    lax.fori_loop(0, far_limit, widen, 0)


def main_kernel(
    lists,
    logs,
    far,
    near,
    own,
    wide,
    payload,
    projected,
    held_near,
    held_wide,
    held_own,
    held_rows,
    halves,
    coded,
    stats,
    tail,
    sem_near,
    sem_wide,
    sem_own,
    sem_rows,
    sem_code,
    *,
    rows_dev,
    devices,
    entries,
    edge,
    samples_dev,
):
    far_limit, near_limit = limits(entries, devices)
    limit = far_limit + near_limit
    split = far_limit // 4
    parts = (pl.ds(0, split), pl.ds(split, far_limit - split))
    fetches = [
        pltpu.make_async_copy(wide.at[part], held_wide.at[part], sem_wide.at[at])
        for at, part in enumerate(parts)
    ]
    fetch_own = pltpu.make_async_copy(own.at[pl.ds(0, rows_dev)], held_own, sem_own.at[0])
    fetch_near = pltpu.make_async_copy(near, held_near, sem_near.at[0])
    for fetch in (*fetches, fetch_own, fetch_near):
        fetch.start()
    held_rows[...] = jnp.zeros(held_rows.shape, jnp.float32)
    stats[...] = jnp.zeros(stats.shape, jnp.float32)
    halves[rows_dev] = jnp.zeros(halves.shape[1:], halves.dtype)

    total = jnp.zeros((edge, samples_dev), jnp.float32)
    for k in range(far_limit):
        if k == 0:
            fetches[0].wait()
        if k == split:
            fetches[1].wait()
        rows = far[lists[2, k]]
        part = jnp.dot(
            held_wide[k],
            jnp.concatenate([rows, rows], axis=0),
            preferred_element_type=jnp.float32,
        )
        row = lists[1, k]
        total = part if k == 0 else jnp.where(row == lists[1, k - 1], total, 0.0) + part
        held_rows[row] = total

    fetch_own.wait()
    squares = jnp.zeros((8, samples_dev), jnp.float32)
    for k in range(rows_dev):
        values = held_rows[k] + held_own[k]
        held_own[k] = values
        squares = squares + jnp.sum((values * values).reshape(edge // 8, 8, samples_dev), axis=0)
        high, low = split_halves(values)
        halves[k, :edge] = high
        halves[k, edge:] = low
    store_rows = pltpu.make_async_copy(held_own, projected, sem_rows.at[0])
    store_rows.start()
    fetch_near.wait()

    def store(k):
        slot = lists[3, k]
        owner = divide(slot, SLOTS)
        rank = slot - owner * SLOTS
        return pltpu.make_async_copy(
            coded.at[k],
            payload.at[owner, pl.ds(pl.multiple_of(rank * edge, edge), edge), :],
            sem_code.at[k],
        )

    def begin(k, carry):
        store(k).start()
        return carry

    def finish(k, carry):
        store(k).wait()
        return carry

    def encode(k, rows):
        slot = lists[3, k]
        both = lax.dot_general(
            rows,
            halves[lists[1, k]],
            (((1,), (1,)), ((), ())),
            preferred_element_type=jnp.float32,
        )
        product = both[:, :edge] + both[:, edge:]
        largest = jnp.maximum(jnp.max(jnp.abs(product), axis=0, keepdims=True), 1e-30)
        code = jnp.ceil(jnp.log2(largest) * LOG_STEPS + 0.01)
        scaled = product * jnp.exp2(15.0 - HEADROOM - code * (1.0 / LOG_STEPS))
        owner = divide(slot, SLOTS)
        coded[k] = jnp.round(scaled).astype(jnp.int32).astype(jnp.int16)
        stats[owner, pl.ds(slot - owner * SLOTS, 1), :] = code

    fars = lists[0, limit + 1]
    nears = lists[0, limit + 2]
    for k in range(far_limit):
        encode(k, far[lists[2, k]])
    lax.fori_loop(0, fars, begin, 0)
    for k in range(far_limit, limit):
        encode(k, near_block(held_near, lists[2, k], edge))
    lax.fori_loop(far_limit, nears, begin, 0)

    term = jnp.sum(squares) * (1.0 / (2.0 * samples_dev)) - jnp.sum(logs[0:1, :])
    term = jnp.full((1, edge), term, jnp.float32)
    power = jnp.ceil(jnp.log2(jnp.maximum(jnp.abs(term), 1e-30)) + 0.01)
    scaled = term * jnp.exp2(14.0 - power)
    whole = jnp.round(scaled)
    digits = jnp.concatenate(
        [
            jnp.zeros((SLOTS, edge), jnp.float32),
            power,
            whole,
            jnp.round((scaled - whole) * FRACTION),
            jnp.zeros((STAT_ROWS - SLOTS - 3, edge), jnp.float32),
        ],
        axis=0,
    )
    tail[...] = (stats[...] + digits[None]).astype(jnp.int32).astype(jnp.int16)
    store_tail = pltpu.make_async_copy(
        tail, payload.at[:, pl.ds(SLOTS * edge, STAT_ROWS), :], sem_code.at[limit]
    )
    store_tail.start()
    lax.fori_loop(0, fars, finish, 0)
    lax.fori_loop(far_limit, nears, finish, 0)
    store_rows.wait()
    store_tail.wait()


def side_kernel(
    lists,
    x,
    omega,
    term,
    projected,
    off,
    far,
    near,
    result,
    moved,
    halves,
    *,
    rows_dev,
    devices,
    entries,
    edge,
    samples_dev,
):
    far_limit, near_limit = limits(entries, devices)
    on_diagonal = lax.broadcasted_iota(jnp.int32, (edge, edge), 0) == lax.broadcasted_iota(
        jnp.int32, (edge, edge), 1
    )

    def against(row, other):
        both = lax.dot_general(
            halves[row], other, (((1,), (1,)), ((), ())), preferred_element_type=jnp.float32
        )
        return both[:edge] + both[edge:]

    moved[...] = jnp.zeros(moved.shape, jnp.float32)
    halves[rows_dev] = jnp.zeros(halves.shape[1:], halves.dtype)
    for k in range(rows_dev):
        high, low = split_halves(projected[k])
        halves[k, :edge] = high
        halves[k, edge:] = low
        product = against(k, x[k])
        gradient = (product + product.T) * (1.0 / (2.0 * samples_dev))
        gradient = gradient + jnp.where(on_diagonal, term[k : k + 1, :], 0.0)
        value = omega[k] - STEP_SIZE * gradient
        result[k] = jnp.where(on_diagonal, value, soften(value, STEP_SIZE * PENALTY))

    def move(block, k, carry):
        e = lists[0, k]
        product = against(lists[1, k], block(lists[2, k]))
        moved[e] = off[jnp.minimum(e, entries - 1)] - product * (STEP_SIZE / (2.0 * samples_dev))
        return carry

    lax.fori_loop(0, far_limit, functools.partial(move, lambda at: far[at]), 0)
    lax.fori_loop(
        far_limit,
        far_limit + near_limit,
        functools.partial(move, lambda at: near_block(near, at, edge)),
        0,
    )


def last_kernel(
    slots,
    moved,
    returned,
    result,
    objective,
    held,
    rt,
    rs,
    sem_in,
    sem_rt,
    sem_out,
    *,
    rows_dev,
    devices,
    entries,
    edge,
    samples_dev,
):
    def fetch(at, part):
        return pltpu.make_async_copy(moved.at[part], held.at[part], sem_in.at[at])

    def store(at, part):
        return pltpu.make_async_copy(rs.at[part], result.at[part], sem_out.at[at])

    width = max(k for k in range(1, 7) if entries % k == 0)
    parts = [(at, pl.ds(at * width, width)) for at in range(entries // width)]
    pieces = [
        pltpu.make_async_copy(returned.at[piece], rt.at[piece], sem_rt.at[at])
        for at, piece in enumerate(pl.ds(q, devices // 4) for q in range(0, devices, devices // 4))
    ]
    for piece in pieces:
        piece.start()
    for at, part in parts:
        fetch(at, part).start()
    for piece in pieces:
        piece.wait()
    codes = rt[:, SLOTS * edge :, :].astype(jnp.int32).astype(jnp.float32)
    power = codes[:, SLOTS : SLOTS + 1]
    digits = codes[:, SLOTS + 1 : SLOTS + 2] + codes[:, SLOTS + 2 : SLOTS + 3] * (1.0 / FRACTION)
    total = jnp.sum(digits * jnp.exp2(power - 14.0), axis=0)
    objective[0] = jnp.max(total) * (1.0 / (devices * rows_dev * edge))
    for at, part in parts:
        fetch(at, part).wait()
        for e in range(at * width, (at + 1) * width):
            slot = jnp.maximum(slots[e], 0)
            owner = divide(slot, SLOTS)
            rank = slot - owner * SLOTS
            codes = rt[owner, SLOTS * edge :, :].astype(jnp.int32).astype(jnp.float32)
            code = jnp.where(rank == 0, codes[0:1], codes[1:2])
            weight = jnp.exp2(code * (1.0 / LOG_STEPS) - (15.0 - HEADROOM)) * (
                STEP_SIZE / (2.0 * samples_dev)
            )
            weight = jnp.where(slots[e] >= 0, weight, 0.0)
            digits = rt[owner, pl.ds(pl.multiple_of(rank * edge, edge), edge), :]
            value = held[e] - digits.astype(jnp.int32).astype(jnp.float32) * weight
            rs[e] = soften(value, STEP_SIZE * PENALTY)
        store(at, part).start()
    for at, part in parts:
        store(at, part).wait()


def layer_of(mesh):
    spots = [getattr(d, "coords", None) for d in mesh.devices.reshape(-1, mesh.shape["rows"])[0]]
    best = 1
    for axis in range(3) if None not in spots else ():
        places = [spot[axis] for spot in spots]
        count = len(set(places))
        runs = 1 + sum(a != b for a, b in zip(places, places[1:]))
        if runs == count and count % 2 == 0:
            best = max(best, len(places) // count)
    return best


def shards(samples, omega_diag, omega_off, pattern, block_count, diag_term, *, layer):
    devices = lax.axis_size("rows")
    rows_dev, edge = omega_diag.shape[:2]
    samples_dev = samples.shape[1]
    entries = omega_off.shape[0]
    f32 = jnp.float32
    x = samples.reshape(rows_dev, edge, samples_dev)
    term = diag_term.reshape(rows_dev, edge)
    pattern = pattern.T
    smem = pl.BlockSpec(memory_space=pltpu.SMEM)
    vmem = pl.BlockSpec(memory_space=pltpu.VMEM)
    hbm = pl.BlockSpec(memory_space=pltpu.HBM)
    params = pltpu.CompilerParams(vmem_limit_bytes=VMEM_LIMIT)
    alone = pltpu.CompilerParams(vmem_limit_bytes=VMEM_ALONE)
    sizes = dict(rows_dev=rows_dev, entries=entries, edge=edge)
    every = dict(sizes, devices=devices, samples_dev=samples_dev)
    held = functools.partial(pltpu.with_memory_space_constraint, memory_space=pltpu.VMEM)
    kept = functools.partial(pltpu.with_memory_space_constraint, memory_space=pltpu.HBM)

    dma = pltpu.SemaphoreType.DMA

    half = devices // 2
    far_limit, near_limit = limits(entries, devices)
    limit = far_limit + near_limit
    across = [(o, mirror(o, devices, layer)) for o in range(devices)]
    steps = devices // layer
    outer = [(o, m) for o, m in across if 4 * abs(2 * (o // layer) + 1 - steps) > 2 * steps]
    inner = [pair for pair in across if pair not in outer]
    halves = [list(range(half)), list(range(half, devices))]

    from_outer = lax.ppermute(kept(x), "rows", outer)

    ints = [pltpu.SMEM((entries,), jnp.int32), pltpu.SMEM((devices,), jnp.int32)]
    places = dict(rows_dev=rows_dev, devices=devices, entries=entries)
    near_rows = SLOTS * edge + STAT_ROWS
    send = pl.pallas_call(
        functools.partial(pack_kernel, layer=layer, edge=edge, **places),
        out_shape=pltpu.HBM((half, near_rows, samples_dev), samples.dtype),
        in_specs=[smem, hbm],
        out_specs=hbm,
        scratch_shapes=[
            *ints,
            pltpu.SMEM((3, entries + 1), jnp.int32),
            pltpu.SMEM((SLOTS * half + 1,), jnp.int32),
            pltpu.VMEM((rows_dev, edge, samples_dev), samples.dtype),
            pltpu.VMEM((half, STAT_ROWS, samples_dev), samples.dtype),
            dma((1,)),
            dma((near_limit + 2,)),
        ],
        compiler_params=alone,
        name="pack",
    )(pattern, kept(x))

    slots, lists = pl.pallas_call(
        functools.partial(plan_kernel, layer=layer, **places),
        out_shape=(
            jax.ShapeDtypeStruct((entries,), jnp.int32),
            jax.ShapeDtypeStruct((4, limit + 3), jnp.int32),
        ),
        in_specs=[smem],
        out_specs=(smem, smem),
        scratch_shapes=ints,
        compiler_params=params,
        name="plan",
    )(pattern)

    def within(blocks):
        return lax.all_to_all(
            blocks, "rows", split_axis=0, concat_axis=0, axis_index_groups=halves, tiled=True
        )

    near = within(send)
    from_inner = lax.ppermute(kept(x), "rows", inner)

    passed = pl.pallas_call(
        functools.partial(relay_kernel, devices=devices, edge=edge),
        out_shape=pltpu.HBM((SLOTS * half, edge, samples_dev), samples.dtype),
        in_specs=[vmem, vmem, vmem],
        out_specs=hbm,
        scratch_shapes=[
            pltpu.VMEM((rows_dev, edge, samples_dev), samples.dtype),
            dma((SLOTS * half,)),
        ],
        compiler_params=params,
        name="relay",
    )(held(near), held(from_outer), held(from_inner))
    far = within(passed.reshape(half, SLOTS, edge, samples_dev))
    far = far.reshape(SLOTS * half, edge, samples_dev)

    own, logs, wide = pl.pallas_call(
        functools.partial(own_kernel, devices=devices, **sizes),
        out_shape=(
            pltpu.HBM((rows_dev + 1, edge, samples_dev), f32),
            jax.ShapeDtypeStruct((8, edge), f32),
            pltpu.HBM((far_limit, edge, 2 * edge), jnp.bfloat16),
        ),
        in_specs=[smem] + [vmem] * 4,
        out_specs=(vmem, vmem, vmem),
        compiler_params=params,
        cost_estimate=pl.CostEstimate(
            flops=12 * rows_dev * edge * edge * samples_dev, transcendentals=0, bytes_accessed=1 << 23
        ),
        name="own",
    )(lists, x, omega_diag, omega_off, near)

    payload, projected = pl.pallas_call(
        functools.partial(main_kernel, **every),
        out_shape=(
            pltpu.HBM((devices, SLOTS * edge + STAT_ROWS, edge), jnp.int16),
            pltpu.HBM((rows_dev, edge, samples_dev), f32),
        ),
        in_specs=[smem, vmem, vmem, hbm, hbm, hbm],
        out_specs=(hbm, hbm),
        scratch_shapes=[
            pltpu.VMEM((half, near_rows, samples_dev), samples.dtype),
            pltpu.VMEM((far_limit, edge, 2 * edge), jnp.bfloat16),
            pltpu.VMEM((rows_dev, edge, samples_dev), f32),
            pltpu.VMEM((rows_dev + 1, edge, samples_dev), f32),
            pltpu.VMEM((rows_dev + 1, 2 * edge, samples_dev), jnp.bfloat16),
            pltpu.VMEM((limit, edge, edge), jnp.int16),
            pltpu.VMEM((devices, STAT_ROWS, edge), f32),
            pltpu.VMEM((devices, STAT_ROWS, edge), jnp.int16),
            dma((1,)),
            dma((2,)),
            dma((1,)),
            dma((1,)),
            dma((limit + 1,)),
        ],
        compiler_params=params,
        name="main",
    )(lists, logs, held(far), kept(near), kept(own), kept(wide))

    returned = lax.all_to_all(kept(payload), "rows", split_axis=0, concat_axis=0, tiled=True)

    diag_next, moved = pl.pallas_call(
        functools.partial(side_kernel, **every),
        out_shape=(
            jax.ShapeDtypeStruct((rows_dev, edge, edge), f32),
            pltpu.HBM((entries + 1, edge, edge), f32),
        ),
        in_specs=[smem] + [vmem] * 7,
        out_specs=(vmem, vmem),
        scratch_shapes=[pltpu.VMEM((rows_dev + 1, 2 * edge, samples_dev), jnp.bfloat16)],
        compiler_params=params,
        cost_estimate=pl.CostEstimate(
            flops=12 * rows_dev * edge * edge * samples_dev, transcendentals=0, bytes_accessed=1 << 23
        ),
        name="side",
    )(lists, x, omega_diag, term, projected, omega_off, far, near)

    off_next, objective = pl.pallas_call(
        functools.partial(last_kernel, **every),
        out_shape=(
            jax.ShapeDtypeStruct((entries, edge, edge), f32),
            jax.ShapeDtypeStruct((1,), f32),
        ),
        in_specs=[smem, hbm, hbm],
        out_specs=(hbm, smem),
        scratch_shapes=[
            pltpu.VMEM((entries, edge, edge), f32),
            pltpu.VMEM((devices, SLOTS * edge + STAT_ROWS, edge), jnp.int16),
            pltpu.VMEM((entries, edge, edge), f32),
            dma((entries,)),
            dma((4,)),
            dma((entries,)),
        ],
        compiler_params=alone,
        name="last",
    )(slots, kept(moved), kept(returned))
    return diag_next, off_next, objective


def solution(mesh):
    return jax.shard_map(
        functools.partial(shards, layer=layer_of(mesh)),
        mesh=mesh,
        in_specs=(
            P(("groups", "rows"), None),
            P(("groups", "rows"), None, None),
            P(("groups", "rows"), None, None),
            P(("groups", "rows"), None),
            P(("groups", "rows")),
            P(("groups", "rows")),
        ),
        out_specs=(
            P(("groups", "rows"), None, None),
            P(("groups", "rows"), None, None),
            P("groups"),
        ),
        check_vma=False,
    )
```

```python
import functools

import jax
import jax.numpy as jnp
from jax import lax
from jax.experimental import pallas as pl
from jax.experimental.pallas import tpu as pltpu
from jax.sharding import PartitionSpec as P


SLOTS = 2
STAT_ROWS = 8
STEP_SIZE = 0.5
PENALTY = 0.01
LOG_STEPS = 128.0
HEADROOM = 1e-4
FRACTION = 32000.0
VMEM_LIMIT = 40 * 1024 * 1024
VMEM_ALONE = 60 * 1024 * 1024


def soften(values, level):
    return values - jnp.clip(values, -level, level)


def split_halves(values):
    high = values.astype(jnp.bfloat16)
    low = (values - high.astype(jnp.float32)).astype(jnp.bfloat16)
    return high, low


def divide(value, by):
    if isinstance(value, int) or by & (by - 1):
        return value // by
    return lax.shift_right_logical(value, by.bit_length() - 1)


def mirror(o, devices, layer):
    return o + (devices - layer) - 2 * layer * divide(o, layer)


def limits(entries, devices):
    half = devices // 2
    return min(entries, SLOTS * half), min(entries, SLOTS * (half - 1))


def place(pattern, keys, sums, visit, *, rows_dev, devices, entries):
    position = divide(pattern[0, 0], rows_dev)
    block_total = rows_dev * devices
    for o in range(devices):
        sums[o] = 0
    for e in range(entries):
        i = pattern[0, e]
        j = pattern[1, e]
        owner = divide(j, rows_dev)
        key = jnp.minimum(i * block_total + j, j * block_total + i)
        keys[e] = key
        sums[owner] = sums[owner] + key
    for e in range(entries):
        owner = divide(pattern[1, e], rows_dev)
        later = jnp.where(2 * keys[e] > sums[owner], 1, 0)
        visit(e, pattern[0, e] - position * rows_dev, owner, later, owner != position)


def pack_kernel(
    pattern,
    x,
    send,
    keys,
    sums,
    picks,
    asked,
    held,
    tiles,
    sem_x,
    sems,
    *,
    rows_dev,
    devices,
    layer,
    entries,
    edge,
):
    half = devices // 2
    near_limit = limits(entries, devices)[1]
    fetch = pltpu.make_async_copy(x, held, sem_x.at[0])
    fetch.start()
    position = divide(pattern[0, 0], rows_dev)
    first = divide(position, half) * half
    spare = pltpu.make_async_copy(
        held.at[0], send.at[position - first, pl.ds(0, edge)], sems.at[near_limit]
    )
    total = [jnp.int32(0)]
    for q in range(SLOTS * half):
        asked[q] = 0

    def visit(e, row, owner, later, alive):
        index = owner - first
        near = (index >= 0) & (index < half)
        picks[0, total[0]] = row
        picks[1, total[0]] = index
        picks[2, total[0]] = later
        total[0] = total[0] + jnp.where(alive & near, 1, 0)
        relay = (mirror(owner, devices, layer) - first) * SLOTS + later
        asked[jnp.where(near, SLOTS * half, relay)] = pattern[1, e] - owner * rows_dev

    place(pattern, keys, sums, visit, rows_dev=rows_dev, devices=devices, entries=entries)
    at = lax.broadcasted_iota(jnp.int32, tiles.shape[1:], 0)
    for q in range(half):
        tile = jnp.zeros(at.shape, jnp.int32)
        for rank in range(SLOTS):
            tile = jnp.where(at == rank, asked[q * SLOTS + rank], tile)
        tiles[q] = tile.astype(jnp.float32).astype(jnp.bfloat16)
    tell = pltpu.make_async_copy(
        tiles, send.at[:, pl.ds(SLOTS * edge, STAT_ROWS), :], sems.at[near_limit + 1]
    )
    tell.start()

    def copy(k):
        rank = pl.multiple_of(picks[2, k] * edge, edge)
        return pltpu.make_async_copy(
            held.at[picks[0, k]], send.at[picks[1, k], pl.ds(rank, edge)], sems.at[k]
        )

    def begin(k, carry):
        copy(k).start()
        return carry

    def finish(k, carry):
        copy(k).wait()
        return carry

    fetch.wait()
    spare.start()
    lax.fori_loop(0, total[0], begin, 0)
    spare.wait()
    tell.wait()
    lax.fori_loop(0, total[0], finish, 0)


def near_block(near, at, edge):
    peer = divide(at, SLOTS)
    return near[peer, pl.ds(pl.multiple_of((at - peer * SLOTS) * edge, edge), edge), :]


def plan_kernel(pattern, owners, lists, keys, sums, *, rows_dev, devices, layer, entries):
    half = devices // 2
    far_limit, near_limit = limits(entries, devices)
    limit = far_limit + near_limit
    position = divide(pattern[0, 0], rows_dev)
    first = divide(position, half) * half
    for k in range(limit):
        lists[0, k] = entries
        lists[1, k] = rows_dev
        lists[2, k] = (position - first) * SLOTS if k >= far_limit else 0
        lists[3, k] = position * SLOTS
    for q in range(SLOTS * devices):
        owners[q] = -1
    tops = [jnp.int32(0), jnp.int32(far_limit)]

    def visit(e, row, owner, later, alive):
        later = jnp.where(alive, later, 0)
        slot = owner * SLOTS + later
        owners[jnp.where(alive, slot, SLOTS * devices + 1)] = e
        index = owner - first
        near = (index >= 0) & (index < half)
        across = mirror(owner, devices, layer) - first
        at = jnp.where(alive, jnp.where(near, tops[1], tops[0]), limit)
        lists[0, at] = e
        lists[1, at] = row
        lists[2, at] = jnp.where(near, index, across) * SLOTS + later
        lists[3, at] = slot
        tops[0] = tops[0] + jnp.where(alive & ~near, 1, 0)
        tops[1] = tops[1] + jnp.where(alive & near, 1, 0)

    place(pattern, keys, sums, visit, rows_dev=rows_dev, devices=devices, entries=entries)
    owners[SLOTS * devices] = tops[0] + tops[1] - far_limit
    lists[0, limit + 1] = tops[0]
    lists[0, limit + 2] = tops[1]


def relay_kernel(near, outer, inner, send, x, sems, *, devices, edge):
    x[...] = outer[...] + inner[...]
    copies = []
    for q in range(devices // 2):
        tile = near[q, SLOTS * edge :, :].astype(jnp.float32)
        for rank in range(SLOTS):
            row = jnp.max(tile[rank : rank + 1, :128]).astype(jnp.int32)
            row = jnp.clip(row, 0, x.shape[0] - 1)
            at = q * SLOTS + rank
            copies.append(pltpu.make_async_copy(x.at[row], send.at[at], sems.at[at]))
            copies[-1].start()
    for copy in copies:
        copy.wait()


def own_kernel(lists, x, omega, off, near, projected, logs, wide, *, rows_dev, devices, entries, edge):
    far_limit, near_limit = limits(entries, devices)
    on_diagonal = lax.broadcasted_iota(jnp.int32, (edge, edge), 0) == lax.broadcasted_iota(
        jnp.int32, (edge, edge), 1
    )

    def apply(block, rows):
        high, low = split_halves(block)
        return jnp.dot(
            jnp.concatenate([high, low], axis=1),
            jnp.concatenate([rows, rows], axis=0),
            preferred_element_type=jnp.float32,
        )

    total = jnp.zeros((1, edge), jnp.float32)
    for k in range(rows_dev):
        projected[k] = apply(omega[k], x[k])
        total = total + jnp.log(
            jnp.sum(jnp.where(on_diagonal, omega[k], 0.0), axis=0, keepdims=True)
        )
    projected[rows_dev] = jnp.zeros(projected.shape[1:], jnp.float32)
    logs[...] = jnp.broadcast_to(total, logs.shape)

    def add(k, carry):
        row = lists[1, k]
        block = off[jnp.minimum(lists[0, k], entries - 1)]
        projected[row] = projected[row] + apply(block, near_block(near, lists[2, k], edge))
        return carry

    lax.fori_loop(far_limit, far_limit + near_limit, add, 0)

    def widen(k, carry):
        high, low = split_halves(off[jnp.minimum(lists[0, k], entries - 1)])
        wide[k, :, :edge] = high
        wide[k, :, edge:] = low
        return carry

    lax.fori_loop(0, far_limit, widen, 0)


def main_kernel(
    lists,
    logs,
    far,
    near,
    own,
    wide,
    payload,
    projected,
    held_near,
    held_wide,
    held_own,
    held_rows,
    halves,
    coded,
    stats,
    tail,
    sem_near,
    sem_wide,
    sem_own,
    sem_rows,
    sem_code,
    *,
    rows_dev,
    devices,
    entries,
    edge,
    samples_dev,
):
    far_limit, near_limit = limits(entries, devices)
    limit = far_limit + near_limit
    split = max(1, far_limit // 8)
    parts = (pl.ds(0, split), pl.ds(split, far_limit - split))
    fetches = [
        pltpu.make_async_copy(wide.at[part], held_wide.at[part], sem_wide.at[at])
        for at, part in enumerate(parts)
    ]
    fetch_own = pltpu.make_async_copy(own.at[pl.ds(0, rows_dev)], held_own, sem_own.at[0])
    fetch_near = pltpu.make_async_copy(near, held_near, sem_near.at[0])
    for fetch in (*fetches, fetch_own, fetch_near):
        fetch.start()
    held_rows[...] = jnp.zeros(held_rows.shape, jnp.float32)
    stats[...] = jnp.zeros(stats.shape, jnp.float32)
    halves[rows_dev] = jnp.zeros(halves.shape[1:], halves.dtype)

    total = jnp.zeros((edge, samples_dev), jnp.float32)
    for k in range(far_limit):
        if k == 0:
            fetches[0].wait()
        if k == split:
            fetches[1].wait()
        rows = far[lists[2, k]]
        part = jnp.dot(
            held_wide[k],
            jnp.concatenate([rows, rows], axis=0),
            preferred_element_type=jnp.float32,
        )
        row = lists[1, k]
        total = part if k == 0 else jnp.where(row == lists[1, k - 1], total, 0.0) + part
        held_rows[row] = total

    fetch_own.wait()
    squares = jnp.zeros((8, samples_dev), jnp.float32)
    for k in range(rows_dev):
        values = held_rows[k] + held_own[k]
        held_own[k] = values
        squares = squares + jnp.sum((values * values).reshape(edge // 8, 8, samples_dev), axis=0)
        high, low = split_halves(values)
        halves[k, :edge] = high
        halves[k, edge:] = low
    store_rows = pltpu.make_async_copy(held_own, projected, sem_rows.at[0])
    store_rows.start()
    fetch_near.wait()

    def store(k):
        slot = lists[3, k]
        owner = divide(slot, SLOTS)
        rank = slot - owner * SLOTS
        return pltpu.make_async_copy(
            coded.at[k],
            payload.at[owner, pl.ds(pl.multiple_of(rank * edge, edge), edge), :],
            sem_code.at[k],
        )

    def begin(k, carry):
        store(k).start()
        return carry

    def finish(k, carry):
        store(k).wait()
        return carry

    def encode(k, rows):
        slot = lists[3, k]
        both = lax.dot_general(
            rows,
            halves[lists[1, k]],
            (((1,), (1,)), ((), ())),
            preferred_element_type=jnp.float32,
        )
        product = both[:, :edge] + both[:, edge:]
        largest = jnp.maximum(jnp.max(jnp.abs(product), axis=0, keepdims=True), 1e-30)
        code = jnp.ceil(jnp.log2(largest) * LOG_STEPS + 0.01)
        scaled = product * jnp.exp2(15.0 - HEADROOM - code * (1.0 / LOG_STEPS))
        owner = divide(slot, SLOTS)
        coded[k] = jnp.round(scaled).astype(jnp.int32).astype(jnp.int16)
        stats[owner, pl.ds(slot - owner * SLOTS, 1), :] = code

    fars = lists[0, limit + 1]
    nears = lists[0, limit + 2]
    for k in range(far_limit):
        encode(k, far[lists[2, k]])
    lax.fori_loop(0, fars, begin, 0)
    for k in range(far_limit, limit):
        encode(k, near_block(held_near, lists[2, k], edge))
    lax.fori_loop(far_limit, nears, begin, 0)

    term = jnp.sum(squares) * (1.0 / (2.0 * samples_dev)) - jnp.sum(logs[0:1, :])
    term = jnp.full((1, edge), term, jnp.float32)
    power = jnp.ceil(jnp.log2(jnp.maximum(jnp.abs(term), 1e-30)) + 0.01)
    scaled = term * jnp.exp2(14.0 - power)
    whole = jnp.round(scaled)
    digits = jnp.concatenate(
        [
            jnp.zeros((SLOTS, edge), jnp.float32),
            power,
            whole,
            jnp.round((scaled - whole) * FRACTION),
            jnp.zeros((STAT_ROWS - SLOTS - 3, edge), jnp.float32),
        ],
        axis=0,
    )
    tail[...] = (stats[...] + digits[None]).astype(jnp.int32).astype(jnp.int16)
    store_tail = pltpu.make_async_copy(
        tail, payload.at[:, pl.ds(SLOTS * edge, STAT_ROWS), :], sem_code.at[limit]
    )
    store_tail.start()
    lax.fori_loop(0, fars, finish, 0)
    lax.fori_loop(far_limit, nears, finish, 0)
    store_rows.wait()
    store_tail.wait()


def side_kernel(
    lists,
    x,
    omega,
    term,
    projected,
    off,
    far,
    near,
    result,
    moved,
    halves,
    *,
    rows_dev,
    devices,
    entries,
    edge,
    samples_dev,
):
    far_limit, near_limit = limits(entries, devices)
    on_diagonal = lax.broadcasted_iota(jnp.int32, (edge, edge), 0) == lax.broadcasted_iota(
        jnp.int32, (edge, edge), 1
    )

    def against(row, other):
        both = lax.dot_general(
            halves[row], other, (((1,), (1,)), ((), ())), preferred_element_type=jnp.float32
        )
        return both[:edge] + both[edge:]

    halves[rows_dev] = jnp.zeros(halves.shape[1:], halves.dtype)
    for k in range(rows_dev):
        high, low = split_halves(projected[k])
        halves[k, :edge] = high
        halves[k, edge:] = low
        product = against(k, x[k])
        gradient = (product + product.T) * (1.0 / (2.0 * samples_dev))
        gradient = gradient + jnp.where(on_diagonal, term[k : k + 1, :], 0.0)
        value = omega[k] - STEP_SIZE * gradient
        result[k] = jnp.where(on_diagonal, value, soften(value, STEP_SIZE * PENALTY))

    def move(block, k, carry):
        product = against(lists[1, k], block(lists[2, k]))
        moved[lists[3, k]] = off[jnp.minimum(lists[0, k], entries - 1)] - product * (
            STEP_SIZE / (2.0 * samples_dev)
        )
        return carry

    lax.fori_loop(0, far_limit, functools.partial(move, lambda at: far[at]), 0)
    lax.fori_loop(
        far_limit,
        far_limit + near_limit,
        functools.partial(move, lambda at: near_block(near, at, edge)),
        0,
    )


def last_kernel(
    owners,
    moved,
    returned,
    result,
    objective,
    held,
    rt,
    rs,
    zeros,
    sem_in,
    sem_rt,
    sem_out,
    *,
    rows_dev,
    devices,
    entries,
    edge,
    samples_dev,
):
    width = max(k for k in (2, 1) if devices % k == 0)
    live = owners[SLOTS * devices]
    fetches = []
    for at in range(devices // width):
        peers = pl.ds(at * width, width)
        blocks = pl.ds(at * width * SLOTS, width * SLOTS)
        fetches.append(
            (
                pltpu.make_async_copy(returned.at[peers], rt.at[peers], sem_rt.at[at]),
                pltpu.make_async_copy(moved.at[blocks], held.at[blocks], sem_in.at[at]),
            )
        )
        for fetch in fetches[-1]:
            fetch.start()
    zeros[...] = jnp.zeros(zeros.shape, jnp.float32)

    def store(q):
        e = owners[q]
        return pltpu.make_async_copy(rs.at[q], result.at[e], sem_out.at[e])

    def clear(e):
        return pltpu.make_async_copy(zeros, result.at[e], sem_out.at[e])

    def begin_clear(e, carry):
        clear(e).start()
        return carry

    def finish_clear(e, carry):
        clear(e).wait()
        return carry

    def begin(q, carry):
        @pl.when(owners[q] >= 0)
        def _():
            store(q).start()

        return carry

    def finish(q, carry):
        @pl.when(owners[q] >= 0)
        def _():
            store(q).wait()

        return carry

    lax.fori_loop(live, entries, begin_clear, 0)
    for at in range(devices // width):
        for fetch in fetches[at]:
            fetch.wait()
        for peer in range(at * width, (at + 1) * width):
            codes = rt[peer, SLOTS * edge :, :].astype(jnp.int32).astype(jnp.float32)
            weights = jnp.exp2(codes[:SLOTS] * (1.0 / LOG_STEPS) - (15.0 - HEADROOM)) * (
                STEP_SIZE / (2.0 * samples_dev)
            )
            for rank in range(SLOTS):
                q = peer * SLOTS + rank
                digits = rt[peer, rank * edge : (rank + 1) * edge, :]
                value = held[q] - digits.astype(jnp.int32).astype(jnp.float32) * weights[
                    rank : rank + 1
                ]
                rs[q] = soften(value, STEP_SIZE * PENALTY)
        lax.fori_loop(at * width * SLOTS, (at + 1) * width * SLOTS, begin, 0)
    codes = rt[:, SLOTS * edge :, :].astype(jnp.int32).astype(jnp.float32)
    power = codes[:, SLOTS : SLOTS + 1]
    digits = codes[:, SLOTS + 1 : SLOTS + 2] + codes[:, SLOTS + 2 : SLOTS + 3] * (1.0 / FRACTION)
    total = jnp.sum(digits * jnp.exp2(power - 14.0), axis=0)
    objective[0] = jnp.max(total) * (1.0 / (devices * rows_dev * edge))
    lax.fori_loop(0, SLOTS * devices, finish, 0)
    lax.fori_loop(live, entries, finish_clear, 0)


def layer_of(mesh):
    spots = [getattr(d, "coords", None) for d in mesh.devices.reshape(-1, mesh.shape["rows"])[0]]
    best = 1
    for axis in range(3) if None not in spots else ():
        places = [spot[axis] for spot in spots]
        count = len(set(places))
        runs = 1 + sum(a != b for a, b in zip(places, places[1:]))
        if runs == count and count % 2 == 0:
            best = max(best, len(places) // count)
    return best


def shards(samples, omega_diag, omega_off, pattern, block_count, diag_term, *, layer):
    devices = lax.axis_size("rows")
    rows_dev, edge = omega_diag.shape[:2]
    samples_dev = samples.shape[1]
    entries = omega_off.shape[0]
    f32 = jnp.float32
    x = samples.reshape(rows_dev, edge, samples_dev)
    term = diag_term.reshape(rows_dev, edge)
    pattern = pattern.T
    smem = pl.BlockSpec(memory_space=pltpu.SMEM)
    vmem = pl.BlockSpec(memory_space=pltpu.VMEM)
    hbm = pl.BlockSpec(memory_space=pltpu.HBM)
    params = pltpu.CompilerParams(vmem_limit_bytes=VMEM_LIMIT)
    alone = pltpu.CompilerParams(vmem_limit_bytes=VMEM_ALONE)
    sizes = dict(rows_dev=rows_dev, entries=entries, edge=edge)
    every = dict(sizes, devices=devices, samples_dev=samples_dev)
    held = functools.partial(pltpu.with_memory_space_constraint, memory_space=pltpu.VMEM)
    kept = functools.partial(pltpu.with_memory_space_constraint, memory_space=pltpu.HBM)

    dma = pltpu.SemaphoreType.DMA

    half = devices // 2
    far_limit, near_limit = limits(entries, devices)
    limit = far_limit + near_limit
    across = [(o, mirror(o, devices, layer)) for o in range(devices)]
    steps = devices // layer
    outer = [(o, m) for o, m in across if 4 * abs(2 * (o // layer) + 1 - steps) > 2 * steps]
    inner = [pair for pair in across if pair not in outer]
    halves = [list(range(half)), list(range(half, devices))]

    from_outer = lax.ppermute(kept(x), "rows", outer)

    ints = [pltpu.SMEM((entries,), jnp.int32), pltpu.SMEM((devices,), jnp.int32)]
    places = dict(rows_dev=rows_dev, devices=devices, entries=entries)
    near_rows = SLOTS * edge + STAT_ROWS
    send = pl.pallas_call(
        functools.partial(pack_kernel, layer=layer, edge=edge, **places),
        out_shape=pltpu.HBM((half, near_rows, samples_dev), samples.dtype),
        in_specs=[smem, hbm],
        out_specs=hbm,
        scratch_shapes=[
            *ints,
            pltpu.SMEM((3, entries + 1), jnp.int32),
            pltpu.SMEM((SLOTS * half + 1,), jnp.int32),
            pltpu.VMEM((rows_dev, edge, samples_dev), samples.dtype),
            pltpu.VMEM((half, STAT_ROWS, samples_dev), samples.dtype),
            dma((1,)),
            dma((near_limit + 2,)),
        ],
        compiler_params=alone,
        name="pack",
    )(pattern, kept(x))

    owners, lists = pl.pallas_call(
        functools.partial(plan_kernel, layer=layer, **places),
        out_shape=(
            jax.ShapeDtypeStruct((SLOTS * devices + 2,), jnp.int32),
            jax.ShapeDtypeStruct((4, limit + 3), jnp.int32),
        ),
        in_specs=[smem],
        out_specs=(smem, smem),
        scratch_shapes=ints,
        compiler_params=params,
        name="plan",
    )(pattern)

    def within(blocks):
        return lax.all_to_all(
            blocks, "rows", split_axis=0, concat_axis=0, axis_index_groups=halves, tiled=True
        )

    near = within(send)
    from_inner = lax.ppermute(kept(x), "rows", inner)

    passed = pl.pallas_call(
        functools.partial(relay_kernel, devices=devices, edge=edge),
        out_shape=pltpu.HBM((SLOTS * half, edge, samples_dev), samples.dtype),
        in_specs=[vmem, vmem, vmem],
        out_specs=hbm,
        scratch_shapes=[
            pltpu.VMEM((rows_dev, edge, samples_dev), samples.dtype),
            dma((SLOTS * half,)),
        ],
        compiler_params=params,
        name="relay",
    )(held(near), held(from_outer), held(from_inner))
    far = within(passed.reshape(half, SLOTS, edge, samples_dev))
    far = far.reshape(SLOTS * half, edge, samples_dev)

    own, logs, wide = pl.pallas_call(
        functools.partial(own_kernel, devices=devices, **sizes),
        out_shape=(
            pltpu.HBM((rows_dev + 1, edge, samples_dev), f32),
            jax.ShapeDtypeStruct((8, edge), f32),
            pltpu.HBM((far_limit, edge, 2 * edge), jnp.bfloat16),
        ),
        in_specs=[smem] + [vmem] * 4,
        out_specs=(vmem, vmem, vmem),
        compiler_params=params,
        cost_estimate=pl.CostEstimate(
            flops=12 * rows_dev * edge * edge * samples_dev, transcendentals=0, bytes_accessed=1 << 23
        ),
        name="own",
    )(lists, x, omega_diag, omega_off, near)

    payload, projected = pl.pallas_call(
        functools.partial(main_kernel, **every),
        out_shape=(
            pltpu.HBM((devices, SLOTS * edge + STAT_ROWS, edge), jnp.int16),
            pltpu.HBM((rows_dev, edge, samples_dev), f32),
        ),
        in_specs=[smem, vmem, vmem, hbm, hbm, hbm],
        out_specs=(hbm, hbm),
        scratch_shapes=[
            pltpu.VMEM((half, near_rows, samples_dev), samples.dtype),
            pltpu.VMEM((far_limit, edge, 2 * edge), jnp.bfloat16),
            pltpu.VMEM((rows_dev, edge, samples_dev), f32),
            pltpu.VMEM((rows_dev + 1, edge, samples_dev), f32),
            pltpu.VMEM((rows_dev + 1, 2 * edge, samples_dev), jnp.bfloat16),
            pltpu.VMEM((limit, edge, edge), jnp.int16),
            pltpu.VMEM((devices, STAT_ROWS, edge), f32),
            pltpu.VMEM((devices, STAT_ROWS, edge), jnp.int16),
            dma((1,)),
            dma((2,)),
            dma((1,)),
            dma((1,)),
            dma((limit + 1,)),
        ],
        compiler_params=params,
        name="main",
    )(lists, logs, held(far), kept(near), kept(own), kept(wide))

    returned = lax.all_to_all(kept(payload), "rows", split_axis=0, concat_axis=0, tiled=True)

    diag_next, moved = pl.pallas_call(
        functools.partial(side_kernel, **every),
        out_shape=(
            jax.ShapeDtypeStruct((rows_dev, edge, edge), f32),
            pltpu.HBM((SLOTS * devices, edge, edge), f32),
        ),
        in_specs=[smem] + [vmem] * 7,
        out_specs=(vmem, vmem),
        scratch_shapes=[pltpu.VMEM((rows_dev + 1, 2 * edge, samples_dev), jnp.bfloat16)],
        compiler_params=params,
        cost_estimate=pl.CostEstimate(
            flops=12 * rows_dev * edge * edge * samples_dev, transcendentals=0, bytes_accessed=1 << 23
        ),
        name="side",
    )(lists, x, omega_diag, term, projected, omega_off, far, near)

    off_next, objective = pl.pallas_call(
        functools.partial(last_kernel, **every),
        out_shape=(
            jax.ShapeDtypeStruct((entries, edge, edge), f32),
            jax.ShapeDtypeStruct((1,), f32),
        ),
        in_specs=[smem, hbm, hbm],
        out_specs=(hbm, smem),
        scratch_shapes=[
            pltpu.VMEM((SLOTS * devices, edge, edge), f32),
            pltpu.VMEM((devices, SLOTS * edge + STAT_ROWS, edge), jnp.int16),
            pltpu.VMEM((SLOTS * devices, edge, edge), f32),
            pltpu.VMEM((edge, edge), f32),
            dma((devices,)),
            dma((devices,)),
            dma((entries,)),
        ],
        compiler_params=alone,
        name="last",
    )(owners, kept(moved), kept(returned))
    return diag_next, off_next, objective


def solution(mesh):
    return jax.shard_map(
        functools.partial(shards, layer=layer_of(mesh)),
        mesh=mesh,
        in_specs=(
            P(("groups", "rows"), None),
            P(("groups", "rows"), None, None),
            P(("groups", "rows"), None, None),
            P(("groups", "rows"), None),
            P(("groups", "rows")),
            P(("groups", "rows")),
        ),
        out_specs=(
            P(("groups", "rows"), None, None),
            P(("groups", "rows"), None, None),
            P("groups"),
        ),
        check_vma=False,
    )
```
